128 devices in a mesh: gx: 16 (over y_hi, x, core), gy: 8 (over y_lo, z).
Axes of the slice: x: 4, y: 4 (y_hi: 2, y_lo: 2; y = y_hi * 2 + y_lo), z: 4, core: 2. Of those that a mesh axis runs over, the one named last changes fastest.
Arguments:
- res_charge: float32 [262144], P(('gx', 'gy')), may hold values from -6 to 6
- res_frac: float32 [3, 262144], P(None, ('gx', 'gy')), may hold values from 0 to 1
- res_cell: int32 [262144], P(('gx', 'gy')), may hold values from 0 to 65535
- res_count: int32 [128], P(('gx', 'gy')), may hold values from 1024 to 2048, as said below
- mov_charge: float32 [65536], P(('gx', 'gy')), may hold values from -6 to 6
- mov_frac: float32 [3, 65536], P(None, ('gx', 'gy')), may hold values from 0 to 1
- mov_cell: int32 [65536], P(('gx', 'gy')), may hold values from 0 to 65535
- mov_dest: int32 [65536, 1], P(('gx', 'gy')), may hold values from 0 to 127; in each aligned block of 512 rows (0 to 511, 512 to 1023, ...) at most 8 rows name the same one
- fine_taps: float32 [3, 13], replicated, may hold values from -3 to 3
- coarse_taps: float32 [3, 13], replicated, may hold values from -3 to 3
Outputs:
- res_potential: float32 [262144], P(('gx', 'gy'))
- arrived_potential: float32 [128, 1024], P(('gx', 'gy'))
- grid_potential: float32 [512, 128, 128], P('gx', 'gy')
The draws below stay inside these ranges and needn't reach their ends.
Inputs may be any that keep to these rules, and one draw needn't show every extreme that they name: `res_count`: a multiple of 128; some box has exactly 2048 live atoms. `mov_dest`: among the rows of one source box, at most 8 name the same destination, a bound that some block reaches of them.
All inputs are finite; a program needn't handle non-finite values.
Results may differ from the reference program's by a relative error of at most 0.0048.
Values sent between devices are 32-bit elements; how exact they have to be, the bound alone decides.
A program may use at most 64 MiB of HBM per device.

```python
import math
import jax
import jax.numpy as jnp
import numpy as np
from jax import lax

CX = 32
CY = 16
NZ = 128
RES_DEV = 2048
MOVE_DEV = 512
TAPS = 13
NX = 512
NY = 128
CAP = 8
N_GY = 8
DEVICES = 128


def draw_res_count(key, part):
    first_key, second_key = jax.random.split(jax.random.fold_in(key, 17))
    blocks = jax.random.randint(first_key, (DEVICES,), max(1, RES_DEV // 256), RES_DEV // 128 + 1)
    fullest = jax.random.randint(second_key, (), 0, DEVICES)
    blocks = jnp.where(jnp.arange(DEVICES) == fullest, RES_DEV // 128, blocks)
    return (blocks * 128).astype(jnp.int32)


def plant(entries, rng, low, high):
    longest = entries.shape.index(max(entries.shape))
    spots = []
    for shift in (0, 1):
        where = [jax.random.randint(jax.random.fold_in(rng, axis), (), 0, length) for axis, length in enumerate(entries.shape)]
        where[longest] = (where[longest] + shift) % entries.shape[longest]
        spots.append(tuple(where))
    return entries.at[spots[0]].set(low).at[spots[1]].set(high)


def block_levels(stream_key, shape, pieces, low, high):
    def one(axis_at, shards_of):
        heights = jax.random.uniform(jax.random.fold_in(jax.random.fold_in(stream_key, 6), axis_at), (shards_of,), jnp.float32, low / len(pieces), high / len(pieces))
        return jnp.repeat(jnp.exp(heights), shape[axis_at] // shards_of).reshape((-1,) + (1,) * (len(shape) - axis_at - 1))

    loudness = one(*pieces[0])
    for cut in pieces[1:]:
        loudness = loudness * one(*cut)
    return loudness


def routed_block(own_key, own, number, rows, count, top, limit, lean):
    sequence = jax.random.permutation(own_key, count)
    crowded, ordinary = shares(count, rows * top, limit, lean, True), shares(count, rows * top, limit, lean, False)
    places = jnp.arange(count)

    def named(sizes, offset_by):
        used = int((sizes > 0).sum())
        fixed = max(1, used // 4)
        shifted = fixed + (places - fixed + offset_by * (used - fixed)) % max(1, count - fixed)
        return jnp.zeros((count,), jnp.int32).at[sequence[jnp.where(places < fixed, places, shifted)]].set(jnp.asarray(sizes, jnp.int32))

    sizes = jnp.where(number % 4 == 0, named(crowded, number // 4), named(ordinary, number - number // 4 - 1))
    mixed = jax.random.permutation(jax.random.fold_in(own, 3), count)
    source_of, receiver = mixed[0:count // 2 * 2:2], mixed[1:count // 2 * 2:2]
    margin = jnp.minimum(sizes[source_of] - 1, limit - sizes[receiver]) // 2
    margin = jnp.where((source_of == sequence[0]) | (receiver == sequence[0]) | (sizes[receiver] == 0), 0, jnp.maximum(margin, 0))
    shifted = jax.random.randint(jax.random.fold_in(own, 4), (count // 2,), 0, 1 << 20) % (margin + 1)
    sizes = sizes.at[source_of].add(-shifted).at[receiver].add(shifted)
    labels = jnp.searchsorted(jnp.cumsum(sizes), jnp.arange(rows * top), side="right").astype(jnp.int32)
    table = labels.reshape(top, rows).T
    table = table[jax.random.permutation(jax.random.fold_in(own, 1), rows)]
    offset_by = jax.random.randint(jax.random.fold_in(own, 2), (rows, 1), 0, top)
    return jnp.take_along_axis(table, (jnp.arange(top)[None, :] + offset_by) % top, axis=1)


def shares(count, total, reach, skew, full):
    loads = [(1 << 20) // math.isqrt(grade ** skew) + 1 for grade in range(1, count + 1)]
    largest = reach if full else min(reach, max(-(-total // count), total * loads[0] // sum(loads)))
    least = 1 if total - largest >= count - 1 else 0
    holding, spare = [largest] + [least] * (count - 1), total - largest - least * (count - 1)
    while spare > 0:
        candidates = [i for i in range(1, count) if holding[i] < largest] or [i for i in range(1, count) if holding[i] < reach]
        mass, remaining = sum([loads[i] for i in candidates]), spare
        for i in candidates:
            more = min(reach - holding[i], max(1, remaining * loads[i] // mass), spare)
            holding[i] = holding[i] + more
            spare = spare - more
    return np.array(holding)


def noise(own_key, shape, width, bound, shards=(), kind=jnp.bfloat16):
    level = block_levels(own_key, shape, shards, -0.22, 0.18) if shards else 1.0
    result = jax.random.normal(own_key, shape, jnp.float32) * width * level
    return jnp.minimum(jnp.maximum(result, -bound), bound).astype(kind)


def setup_inputs(seed: int = 0) -> dict:
    key_of = jax.random.split(jax.random.key(seed), 11)
    res_charge = noise(key_of[0], (DEVICES * RES_DEV,), 1.0, 6.0, ((0, 128),), jnp.float32)
    res_frac = jnp.clip(1.0 * jax.random.uniform(key_of[1], (3, DEVICES * RES_DEV), jnp.float32) ** block_levels(key_of[1], (3, DEVICES * RES_DEV), ((1, 128),), -0.2, 0.2), 0.0, 1.0)
    res_cell = plant(jax.random.randint(key_of[2], (DEVICES * RES_DEV,), 0, CX * CY * NZ), jax.random.fold_in(key_of[2], 1), 0, (CX * CY * NZ) - 1).astype(jnp.int32)
    res_count = draw_res_count(jax.random.fold_in(key_of[10], 71), 0)
    mov_charge = noise(key_of[4], (DEVICES * MOVE_DEV,), 1.0, 6.0, ((0, 128),), jnp.float32)
    mov_frac = jnp.clip(1.0 * jax.random.uniform(key_of[5], (3, DEVICES * MOVE_DEV), jnp.float32) ** block_levels(key_of[5], (3, DEVICES * MOVE_DEV), ((1, 128),), -0.2, 0.2), 0.0, 1.0)
    mov_cell = plant(jax.random.randint(key_of[6], (DEVICES * MOVE_DEV,), 0, CX * CY * NZ), jax.random.fold_in(key_of[6], 1), 0, (CX * CY * NZ) - 1).astype(jnp.int32)
    mov_dest_keys = jax.random.split(jax.random.fold_in(key_of[7], 1), (DEVICES * MOVE_DEV) // MOVE_DEV)
    mov_dest_turns = jax.random.permutation(jax.random.fold_in(key_of[7], 3), (DEVICES * MOVE_DEV) // MOVE_DEV)
    mov_dest = jax.vmap(lambda own, number: routed_block(jax.random.fold_in(key_of[7], 2), own, number, MOVE_DEV, DEVICES, 1, 2 * MOVE_DEV // DEVICES, 2))(mov_dest_keys, mov_dest_turns).reshape((DEVICES * MOVE_DEV, 1))
    fine_taps = noise(key_of[8], (3, TAPS), 0.7, 3.0, (), jnp.float32)
    coarse_taps = noise(key_of[9], (3, TAPS), 0.5, 3.0, (), jnp.float32)
    return {"res_charge": res_charge, "res_frac": res_frac, "res_cell": res_cell, "res_count": res_count, "mov_charge": mov_charge, "mov_frac": mov_frac, "mov_cell": mov_cell, "mov_dest": mov_dest, "fine_taps": fine_taps, "coarse_taps": coarse_taps}


def spline_weights(fracs):
    rest = 1.0 - fracs
    cube = fracs * fracs * fracs
    square = fracs * fracs
    return jnp.stack([rest * rest * rest / 6.0, (3.0 * cube - 6.0 * square + 4.0) / 6.0, (-3.0 * cube + 3.0 * square + 3.0 * fracs + 1.0) / 6.0, cube / 6.0])


def rounded(values):
    return lax.optimization_barrier(values.astype(jnp.bfloat16)).astype(jnp.float32)


def periodic_pass(field, filter_taps, along_dim):
    summed = jnp.zeros_like(field)
    half_width = filter_taps.shape[0] // 2
    for tap_index in range(filter_taps.shape[0]):
        summed = summed + filter_taps[tap_index] * jnp.roll(field, half_width - tap_index, axis=along_dim)
    return summed


def convolve(field, filter_taps):
    field = periodic_pass(field, filter_taps[0], 0)
    field = periodic_pass(field, filter_taps[1], 1)
    return periodic_pass(field, filter_taps[2], 2)


def home(device, cells):
    first = (device // N_GY) * CX + cells // (CY * NZ)
    second = (device % N_GY) * CY + (cells // NZ) % CY
    return first, second, cells % NZ


def reference(res_charge, res_frac, res_cell, res_count, mov_charge, mov_frac, mov_cell, mov_dest, fine_taps, coarse_taps):
    res_rows = jnp.arange(DEVICES * RES_DEV, dtype=jnp.int32)
    res_owner = res_rows // RES_DEV
    live = (res_rows % RES_DEV) < res_count[res_owner]
    mov_rows = jnp.arange(DEVICES * MOVE_DEV, dtype=jnp.int32)
    targets = mov_dest[:, 0]
    sources = mov_rows // MOVE_DEV
    charges = jnp.concatenate([jnp.where(live, res_charge, 0.0), mov_charge])
    fracs = jnp.concatenate([res_frac, mov_frac], 1)
    res_x, res_y, res_z = home(res_owner, res_cell)
    mov_x, mov_y, mov_z = home(targets, mov_cell)
    base_x = jnp.concatenate([res_x, mov_x])
    base_y = jnp.concatenate([res_y, mov_y])
    base_z = jnp.concatenate([res_z, mov_z])
    weight_x = spline_weights(fracs[0])
    weight_y = spline_weights(fracs[1])
    weight_z = spline_weights(fracs[2])
    x_charge = rounded(weight_x * charges[None, :])
    yz_weights = rounded(weight_y[:, None, :] * weight_z[None, :, :])
    x_plain = rounded(weight_x)
    indices = []
    charge_flat = jnp.zeros((NX * NY * NZ,), jnp.float32)
    for step_x in range(4):
        for step_y in range(4):
            for step_z in range(4):
                linear = (((base_x + step_x) % NX) * NY + (base_y + step_y) % NY) * NZ + (base_z + step_z) % NZ
                indices.append((step_x, step_y, step_z, linear))
                charge_flat = charge_flat.at[linear].add(x_charge[step_x] * yz_weights[step_y, step_z])
    charge_grid = charge_flat.reshape(NX, NY, NZ)
    fine_field = convolve(charge_grid, fine_taps)
    coarse_charge = charge_grid.reshape(NX // 2, 2, NY // 2, 2, NZ // 2, 2).sum(axis=(1, 3, 5))
    coarse_field = convolve(coarse_charge, coarse_taps)
    spread_coarse = jnp.repeat(jnp.repeat(jnp.repeat(coarse_field, 2, 0), 2, 1), 2, 2)
    grid_potential = fine_field + spread_coarse
    half_flat = rounded(grid_potential).reshape(-1)
    potential = jnp.zeros(charges.shape, jnp.float32)
    for step_x, step_y, step_z, linear in indices:
        potential = potential + x_plain[step_x] * yz_weights[step_y, step_z] * half_flat[linear]
    res_potential = jnp.where(live, potential[:DEVICES * RES_DEV], 0.0)
    moved = potential[DEVICES * RES_DEV:]
    hits = (targets.reshape(DEVICES, MOVE_DEV)[:, :, None] == jnp.arange(DEVICES, dtype=jnp.int32)[None, None, :]).astype(jnp.int32)
    ranks = jnp.cumsum(hits, axis=1)
    slot = jnp.sum(hits * ranks, axis=2).reshape(-1) - 1
    arrived_potential = jnp.zeros((DEVICES, DEVICES * CAP), jnp.float32).at[targets, sources * CAP + slot].set(moved)
    return res_potential, arrived_potential, grid_potential
```

```python
import functools

import jax
import jax.numpy as jnp
from jax import lax
from jax.experimental import pallas as pl
from jax.experimental.pallas import tpu as pltpu
from jax.sharding import PartitionSpec as P

F32 = jnp.float32
BF16 = jnp.bfloat16
MESH = pl.DeviceIdType.MESH
CX = 32
CY = 16
NZ = 128
TAPS = 13
XP = 40
YR = 19
YP = 20
CP = 24
ROWS = YP * XP
RES = 2048
ARR = 1024
ATOMS = RES + ARR
MOV = 512
FH = 9
CH = 4


def iota(shape, dim):
    return lax.broadcasted_iota(jnp.int32, shape, dim)


def split2(v):
    hi = v.astype(BF16)
    return hi, (v - hi.astype(F32)).astype(BF16)


def split3(v):
    hi = v.astype(BF16)
    rest = v - hi.astype(F32)
    mid = rest.astype(BF16)
    return hi, mid, (rest - mid.astype(F32)).astype(BF16)


def dot_nt(a, b):
    return lax.dot_general(a, b, (((1,), (1,)), ((), ())), preferred_element_type=F32)


def dot_nn(a, b):
    return lax.dot_general(a, b, (((1,), (0,)), ((), ())), preferred_element_type=F32)


def spline(u):
    r = 1.0 - u
    s = u * u
    c = s * u
    return (
        r * r * r * (1.0 / 6.0),
        (3.0 * c - 6.0 * s + 4.0) * (1.0 / 6.0),
        (-3.0 * c + 3.0 * s + 3.0 * u + 1.0) * (1.0 / 6.0),
        c * (1.0 / 6.0),
    )


def pick(d, w, row):
    out = jnp.zeros(d.shape, F32)
    for k in range(4):
        out = jnp.where(d == k, w[k][row : row + 1], out)
    return out


def build_group(lane0, charge, weights, row, cell, a_ref, wx_ref, wy_ref, wz_ref):
    lanes = pl.ds(pl.multiple_of(lane0, 128), 128)
    cx = lax.shift_right_logical(cell, 11)
    cy = lax.shift_right_logical(cell, 7) & 15
    cz = cell & 127
    wx = pick(iota((XP, 128), 0) - cx, weights, row)
    wy = pick(iota((CP, 128), 0) - cy, weights, row + 1)
    wz = pick((iota((NZ, 128), 0) - cz) & 127, weights, row + 2)
    wx_ref[:, lanes] = wx
    wy_ref[:, lanes] = wy
    hi, lo = split2(wz)
    wz_ref[0:NZ, lanes] = hi
    wz_ref[NZ : 2 * NZ, lanes] = lo
    wxq = wx * charge
    for p in range(YP // 2):
        blk = jnp.concatenate(
            [wy[2 * p : 2 * p + 1] * wxq, wy[2 * p + 1 : 2 * p + 2] * wxq], axis=0
        )
        a_ref[p * 2 * XP : (p + 1) * 2 * XP, lanes] = blk.astype(BF16)


def spread_chunk(lane0, size, acc_ref, a_ref, wz_ref):
    lanes = pl.ds(pl.multiple_of(lane0, 256), size)
    acc_ref[...] += dot_nt(a_ref[:, lanes], wz_ref[:, lanes])


def tap_sum(t, taps_ref, dim):
    out = jnp.zeros(t.shape, F32)
    for k in range(TAPS):
        out = jnp.where(t == k, taps_ref[dim, k], out)
    return out


def kernel(
    nx,
    ny,
    rq_ref,
    rf_ref,
    rc_ref,
    count_ref,
    mq_ref,
    mf_ref,
    mc_ref,
    md_ref,
    ft_ref,
    ct_ref,
    res_ref,
    arr_ref,
    grid_ref,
    pay_ref,
    snd_ref,
    b1_ref,
    t2_ref,
    r2_ref,
    rt_ref,
    a_ref,
    wx_ref,
    wy_ref,
    wz_ref,
    acc_ref,
    gf_ref,
    xs_ref,
    xl_ref,
    xr_ref,
    xh_ref,
    bx_ref,
    zf_ref,
    zc_ref,
    f_ref,
    c3_ref,
    fl_ref,
    fr_ref,
    cl_ref,
    cr_ref,
    fin_ref,
    cin_ref,
    fo_ref,
    up_ref,
    hb_ref,
    ao_ref,
    s1_sem,
    r1_sem,
    s2_sem,
    r2_sem,
    sx_sem,
    rx_sem,
    sy_sem,
    ry_sem,
):
    gx = lax.axis_index("gx")
    gy = lax.axis_index("gy")

    barrier = pltpu.get_barrier_semaphore()
    for k in range(1, ny):
        pl.semaphore_signal(
            barrier, inc=1, device_id=(gx, lax.rem(gy + k, ny)), device_id_type=MESH
        )
    for k in range(1, nx):
        pl.semaphore_signal(
            barrier, inc=1, device_id=(lax.rem(gx + k, nx), gy), device_id_type=MESH
        )

    with jax.named_scope("pack"):
        dest = md_ref[...]
        row_of = (dest & (ny - 1)) * nx + lax.div(dest, ny)
        hot = jnp.where(iota((nx * ny, MOV), 0) == row_of, 1.0, 0.0)
        hot16 = hot.astype(BF16)
        earlier = jnp.where(iota((MOV, MOV), 0) < iota((MOV, MOV), 1), 1.0, 0.0)
        counts = dot_nn(hot16, earlier.astype(BF16))
        slot = jnp.sum(hot * counts, axis=0, keepdims=True)
        pay_ref[0:1, :] = mq_ref[...]
        pay_ref[1:4, :] = mf_ref[...]
        pay_ref[4:5, :] = mc_ref[...].astype(F32) + 1.0
        pay_ref[5:8, :] = jnp.zeros((3, MOV), F32)
        pay = pay_ref[...]
        spots = jnp.concatenate([jnp.where(slot == float(s), pay, 0.0) for s in range(8)], axis=0)
        hi, mid, lo = split3(spots)
        packed = dot_nt(hot16, hi) + dot_nt(hot16, mid) + dot_nt(hot16, lo)
        snd_ref[:, 0:64] = packed
        snd_ref[:, 64:128] = jnp.zeros((nx * ny, 64), F32)

    pl.semaphore_wait(barrier, nx + ny - 2)

    def hop1(k):
        to = lax.rem(gy + k, ny)
        return pltpu.make_async_remote_copy(
            src_ref=snd_ref.at[pl.ds(pl.multiple_of(to * nx, nx), nx), :],
            dst_ref=b1_ref.at[pl.ds(pl.multiple_of(gy * nx, nx), nx), :],
            send_sem=s1_sem.at[k],
            recv_sem=r1_sem.at[k],
            device_id=(gx, to),
            device_id_type=MESH,
        )

    for k in range(1, ny):
        hop1(k).start()
    mine = pl.ds(pl.multiple_of(gy * nx, nx), nx)
    b1_ref[mine, :] = snd_ref[mine, :]

    def build_res(g, carry):
        live = iota((1, 128), 1) + g * 128 < count_ref[0]
        charge = jnp.where(live, rq_ref[pl.ds(g, 1), :], 0.0)
        frac = rf_ref[:, pl.ds(pl.multiple_of(g * 128, 128), 128)]
        build_group(
            g * 128, charge, spline(frac), 0, rc_ref[pl.ds(g, 1), :], a_ref, wx_ref, wy_ref, wz_ref
        )
        return carry

    def spread_at(c, carry):
        spread_chunk(c * 512, 512, acc_ref, a_ref, wz_ref)
        return carry

    acc_ref[...] = jnp.zeros_like(acc_ref)
    lax.fori_loop(0, 8, build_res, 0)
    lax.fori_loop(0, 2, spread_at, 0)

    for k in range(1, ny):
        hop1(k).wait()
    for g in range(nx):
        t2_ref[g] = b1_ref[pl.ds(g, ny, stride=nx), :]

    def hop2(k):
        to = lax.rem(gx + k, nx)
        return pltpu.make_async_remote_copy(
            src_ref=t2_ref.at[to],
            dst_ref=r2_ref.at[pl.ds(pl.multiple_of(gx * ny, ny), ny), :],
            send_sem=s2_sem.at[k],
            recv_sem=r2_sem.at[k],
            device_id=(to, gy),
            device_id_type=MESH,
        )

    for k in range(1, nx):
        hop2(k).start()
    r2_ref[pl.ds(pl.multiple_of(gx * ny, ny), ny), :] = t2_ref[gx]

    lax.fori_loop(8, 16, build_res, 0)
    lax.fori_loop(2, 4, spread_at, 0)

    with jax.named_scope("matrices"):
        col = iota((64, 256), 1)
        part = jnp.where(col >= 160, 2, jnp.where(col >= 80, 1, 0))
        base = col - part * 80
        pos = jnp.where(base < 48, base, jnp.where(base < 64, base - 60, base - 32))
        out_x = iota((64, 256), 0)
        fine_t = pos - out_x + 6
        coarse_t = lax.shift_right_arithmetic(pos, 1) - (out_x - XP) + 6
        bx = jnp.where(out_x < XP, tap_sum(fine_t, ft_ref, 0), tap_sum(coarse_t, ct_ref, 0))
        bx_hi = bx.astype(BF16).astype(F32)
        bx = jnp.where(part == 2, bx - bx_hi, bx_hi)
        bx_ref[...] = jnp.where(col < 240, bx, 0.0).astype(BF16)
        t = (iota((NZ, NZ), 0) - iota((NZ, NZ), 1) + 6) & 127
        hi, lo = split2(tap_sum(t, ft_ref, 2))
        zf_ref[0:NZ, 0:NZ] = hi
        zf_ref[NZ : 2 * NZ, 0:NZ] = hi
        zf_ref[0:NZ, NZ : 2 * NZ] = lo
        zf_ref[NZ : 2 * NZ, NZ : 2 * NZ] = jnp.zeros((NZ, NZ), BF16)
        r, c = iota((NZ, 2 * NZ), 0), iota((NZ, 2 * NZ), 1)
        t = ((r & 63) - lax.shift_right_logical(c & 127, 1) + 6) & 63
        zc = tap_sum(t, ct_ref, 2)
        same = lax.shift_right_logical(r, 6) == lax.shift_right_logical(c, 7)
        hi, lo = split2(jnp.where(same, zc, 0.0))
        zc_ref[0:NZ, :] = hi
        zc_ref[NZ : 2 * NZ, :] = hi
        zc_ref[2 * NZ : 3 * NZ, :] = lo

    for k in range(1, nx):
        hop2(k).wait()

    rt_ref[...] = r2_ref[...].T

    def build_arr(s, carry):
        block = rt_ref[pl.ds(pl.multiple_of(s * 8, 8), 8), :]
        cell = jnp.maximum(block[4:5] - 1.0, 0.0).astype(jnp.int32)
        build_group(
            RES + s * 128, block[0:1], spline(block), 1, cell, a_ref, wx_ref, wy_ref, wz_ref
        )
        return carry

    lax.fori_loop(0, 8, build_arr, 0)
    lax.fori_loop(4, 6, spread_at, 0)

    for y in range(YR):
        rows = slice(y * XP, (y + 1) * XP)
        gf_ref[:, y * NZ : (y + 1) * NZ] = acc_ref[rows, 0:NZ] + acc_ref[rows, NZ : 2 * NZ]
    xs_ref[...] = gf_ref[20:36, :]

    up_x = lax.rem(gx + 1, nx)
    down_x = lax.rem(gx + nx - 1, nx)
    up_y = lax.rem(gy + 1, ny)
    down_y = lax.rem(gy + ny - 1, ny)
    x_copies = [
        pltpu.make_async_remote_copy(
            src_ref=xs_ref,
            dst_ref=xl_ref,
            send_sem=sx_sem.at[0],
            recv_sem=rx_sem.at[0],
            device_id=(up_x, gy),
            device_id_type=MESH,
        ),
        pltpu.make_async_remote_copy(
            src_ref=gf_ref.at[pl.ds(0, 16), :],
            dst_ref=xr_ref,
            send_sem=sx_sem.at[1],
            recv_sem=rx_sem.at[1],
            device_id=(down_x, gy),
            device_id_type=MESH,
        ),
    ]
    for copy in x_copies:
        copy.start()
    hi, lo = split2(gf_ref[...])
    zero8 = jnp.zeros((8, YR * NZ), BF16)
    own_hi = jnp.concatenate([hi, zero8], axis=0)
    xh_ref[0:48, :] = own_hi
    xh_ref[160:208, :] = own_hi
    xh_ref[80:128, :] = jnp.concatenate([lo, zero8], axis=0)
    xh_ref[240:256, :] = jnp.zeros((16, YR * NZ), BF16)
    for copy in x_copies:
        copy.wait()
    for at, ref in ((48, xl_ref), (64, xr_ref)):
        hi, lo = split2(ref[...])
        xh_ref[at : at + 16, :] = hi
        xh_ref[at + 160 : at + 176, :] = hi
        xh_ref[at + 80 : at + 96, :] = lo

    conv = dot_nn(bx_ref[...], xh_ref[...])
    f_ref[...] = conv[0:XP]

    r, c = iota((2 * NZ, NZ), 0), iota((2 * NZ, NZ), 1)
    pair = jnp.where(lax.shift_right_logical(r, 1) == c, 1.0, 0.0).astype(BF16)
    coarse = conv[XP : XP + CP]
    tiles = []
    for m in range(5):
        both = []
        for j in (2 * m, 2 * m + 1):
            row = coarse[:, 2 * j * NZ : (2 * j + 1) * NZ]
            if 2 * j + 1 < YR:
                row = row + coarse[:, (2 * j + 1) * NZ : (2 * j + 2) * NZ]
            both.append(row)
        tiles.append(jnp.concatenate(both, axis=1))
    packed = jnp.concatenate(tiles, axis=0)
    hi, lo = split2(packed)
    packed = dot_nn(hi, pair) + dot_nn(lo, pair)
    for m in range(5):
        c3_ref[m] = packed[m * CP : (m + 1) * CP]

    def y_copy(n, src, dst, to):
        return pltpu.make_async_remote_copy(
            src_ref=src,
            dst_ref=dst,
            send_sem=sy_sem.at[n],
            recv_sem=ry_sem.at[n],
            device_id=(gx, to),
            device_id_type=MESH,
        )

    y_copies = [
        y_copy(0, f_ref.at[:, pl.ds(10 * NZ, FH * NZ)], fl_ref, up_y),
        y_copy(1, f_ref.at[:, pl.ds(0, FH * NZ)], fr_ref, down_y),
        y_copy(2, c3_ref.at[pl.ds(1, CH)], cl_ref, up_y),
        y_copy(3, c3_ref.at[pl.ds(0, CH)], cr_ref, down_y),
    ]
    for copy in y_copies:
        copy.start()

    def fine_z(block):
        hi, lo = split2(block)
        both = dot_nn(jnp.concatenate([hi, lo], axis=1), zf_ref[...])
        return both[:, 0:NZ] + both[:, NZ : 2 * NZ]

    def coarse_z(block):
        hi, lo = split2(block)
        return dot_nn(jnp.concatenate([hi, lo], axis=1), zc_ref[0 : 2 * NZ, :]) + dot_nn(
            hi, zc_ref[2 * NZ : 3 * NZ, :]
        )

    def stacked(ref, count):
        return jnp.concatenate([ref[:, y * NZ : (y + 1) * NZ] for y in range(count)], axis=0)

    own = fine_z(stacked(f_ref, YR))
    for y in range(YR):
        fin_ref[:, (y + 6) * NZ : (y + 7) * NZ] = own[y * XP : (y + 1) * XP]
    zero = jnp.zeros((XP, 6 * NZ), F32)
    fin_ref[:, 0 : 6 * NZ] = zero
    fin_ref[:, 25 * NZ : 31 * NZ] = zero
    own = coarse_z(jnp.concatenate([c3_ref[m] for m in range(5)], axis=0))
    zero = jnp.zeros((CP, 6 * NZ), F32)
    cin_ref[:, 0 : 6 * NZ] = zero
    cin_ref[:, 16 * NZ : 22 * NZ] = zero
    for m in range(5):
        cin_ref[:, (2 * m + 6) * NZ : (2 * m + 8) * NZ] = own[m * CP : (m + 1) * CP]

    for copy in y_copies:
        copy.wait()
    for ref, at in ((fl_ref, 0), (fr_ref, 22)):
        halo = fine_z(stacked(ref, FH))
        for y in range(FH):
            fin_ref[:, (y + at) * NZ : (y + at + 1) * NZ] += halo[y * XP : (y + 1) * XP]
    for ref, at in ((cl_ref, 0), (cr_ref, 14)):
        halo = coarse_z(jnp.concatenate([ref[m] for m in range(CH)], axis=0))
        for m in range(CH):
            cin_ref[:, (2 * m + at) * NZ : (2 * m + at + 2) * NZ] += halo[m * CP : (m + 1) * CP]

    def fine_y(i, carry):
        rows = pl.ds(pl.multiple_of(i * 8, 8), 8)
        out = jnp.zeros((8, YR * NZ), F32)
        for k in range(TAPS):
            out = out + ft_ref[1, k] * fin_ref[rows, k * NZ : (k + YR) * NZ]
        fo_ref[rows, 0 : YR * NZ] = out
        fo_ref[rows, YR * NZ : YP * NZ] = jnp.zeros((8, NZ), F32)
        return carry

    lax.fori_loop(0, XP // 8, fine_y, 0)

    def coarse_y(i, carry):
        rows = pl.ds(pl.multiple_of(i * 8, 8), 8)
        out = jnp.zeros((8, 10 * NZ), F32)
        for k in range(TAPS):
            out = out + ct_ref[1, k] * cin_ref[rows, k * NZ : (k + 10) * NZ]
        for j in range(10):
            one = out[:, j * NZ : (j + 1) * NZ]
            up_ref[j, pl.ds(i * 16, 8, stride=2), :] = one
            up_ref[j, pl.ds(i * 16 + 1, 8, stride=2), :] = one
        return carry

    lax.fori_loop(0, CP // 8, coarse_y, 0)

    for p in range(YP // 2):
        add = up_ref[p, 0:XP, :]
        rows = []
        for y in (2 * p, 2 * p + 1):
            total = fo_ref[:, y * NZ : (y + 1) * NZ] + add
            if y < CY:
                for i in range(CX // 8):
                    grid_ref[pl.ds(y + i * 8 * CY, 8, stride=CY), :] = total[i * 8 : i * 8 + 8]
            rows.append(total)
        half = jnp.concatenate(rows, axis=0).astype(BF16)
        hb_ref[p * 2 * XP : (p + 1) * 2 * XP, 0:NZ] = half
        hb_ref[p * 2 * XP : (p + 1) * 2 * XP, NZ : 2 * NZ] = half

    def sample_at(c):
        lanes = pl.ds(pl.multiple_of(c * 256, 256), 256)
        values = dot_nn(hb_ref[...], wz_ref[:, lanes])
        wy = wy_ref[:, lanes]
        part = jnp.zeros((XP, 256), F32)
        for y in range(YR):
            part = part + wy[y : y + 1] * values[y * XP : (y + 1) * XP]
        return jnp.sum(part * wx_ref[:, lanes], axis=0, keepdims=True)

    def sample_res(c, carry):
        value = sample_at(c)
        live = iota((1, 256), 1) + c * 256 < count_ref[0]
        value = jnp.where(live, value, 0.0)
        res_ref[pl.ds(2 * c, 1), :] = value[:, 0:128]
        res_ref[pl.ds(2 * c + 1, 1), :] = value[:, 128:256]
        return carry

    def sample_arr(c, carry):
        value = sample_at(c + RES // 256)
        ao_ref[pl.ds(2 * c, 1), :] = value[:, 0:128]
        ao_ref[pl.ds(2 * c + 1, 1), :] = value[:, 128:256]
        return carry

    lax.fori_loop(0, RES // 256, sample_res, 0)
    lax.fori_loop(0, ARR // 256, sample_arr, 0)

    occupied = jnp.concatenate([rt_ref[s * 8 + 4 : s * 8 + 5, :] for s in range(8)], axis=0)
    value = jnp.where(occupied > 0.5, ao_ref[...], 0.0)
    hi, mid, lo = split3(value)
    wide = (NZ, ARR)
    spread_to = jnp.where(lax.shift_right_logical(iota(wide, 1), 3) == iota(wide, 0), 1.0, 0.0)
    spread_to = spread_to.astype(BF16)
    flat = dot_nn(hi, spread_to) + dot_nn(mid, spread_to) + dot_nn(lo, spread_to)
    keep = (iota((8, ARR), 1) & 7) == iota((8, ARR), 0)
    arr_ref[...] = jnp.sum(jnp.where(keep, flat, 0.0), axis=0, keepdims=True)


def on_device(rq, rf, rc, count, mq, mf, mc, md, ft, ct):
    nx = lax.axis_size("gx")
    ny = lax.axis_size("gy")
    vmem = pl.BlockSpec(memory_space=pltpu.VMEM)
    smem = pl.BlockSpec(memory_space=pltpu.SMEM)
    lanes = YR * NZ
    dma = pltpu.SemaphoreType.DMA
    res, arr, grid = pl.pallas_call(
        functools.partial(kernel, nx, ny),
        out_shape=(
            jax.ShapeDtypeStruct((16, 128), F32),
            jax.ShapeDtypeStruct((1, ARR), F32),
            jax.ShapeDtypeStruct((CX * CY, NZ), F32),
        ),
        in_specs=[vmem, vmem, vmem, smem, vmem, vmem, vmem, vmem, smem, smem],
        out_specs=(vmem, vmem, vmem),
        scratch_shapes=[
            pltpu.VMEM((8, MOV), F32),
            pltpu.VMEM((128, 128), F32),
            pltpu.VMEM((128, 128), F32),
            pltpu.VMEM((nx, ny, 128), F32),
            pltpu.VMEM((128, 128), F32),
            pltpu.VMEM((128, 128), F32),
            pltpu.VMEM((ROWS, ATOMS), BF16),
            pltpu.VMEM((XP, ATOMS), F32),
            pltpu.VMEM((CP, ATOMS), F32),
            pltpu.VMEM((2 * NZ, ATOMS), BF16),
            pltpu.VMEM((ROWS, 2 * NZ), F32),
            pltpu.VMEM((XP, lanes), F32),
            pltpu.VMEM((16, lanes), F32),
            pltpu.VMEM((16, lanes), F32),
            pltpu.VMEM((16, lanes), F32),
            pltpu.VMEM((256, lanes), BF16),
            pltpu.VMEM((64, 256), BF16),
            pltpu.VMEM((2 * NZ, 2 * NZ), BF16),
            pltpu.VMEM((3 * NZ, 2 * NZ), BF16),
            pltpu.VMEM((XP, lanes), F32),
            pltpu.VMEM((5, CP, NZ), F32),
            pltpu.VMEM((XP, FH * NZ), F32),
            pltpu.VMEM((XP, FH * NZ), F32),
            pltpu.VMEM((CH, CP, NZ), F32),
            pltpu.VMEM((CH, CP, NZ), F32),
            pltpu.VMEM((XP, 31 * NZ), F32),
            pltpu.VMEM((CP, 22 * NZ), F32),
            pltpu.VMEM((XP, YP * NZ), F32),
            pltpu.VMEM((10, 2 * CP, NZ), F32),
            pltpu.VMEM((ROWS, 2 * NZ), BF16),
            pltpu.VMEM((8, 128), F32),
            dma((ny,)),
            dma((ny,)),
            dma((nx,)),
            dma((nx,)),
            dma((2,)),
            dma((2,)),
            dma((4,)),
            dma((4,)),
        ],
        compiler_params=pltpu.CompilerParams(
            collective_id=0, has_side_effects=True, vmem_limit_bytes=40 << 20
        ),
        name="multilevel",
    )(
        rq.reshape(16, 128),
        rf,
        rc.reshape(16, 128),
        count,
        mq.reshape(1, MOV),
        mf,
        mc.reshape(1, MOV),
        md.reshape(1, MOV),
        ft,
        ct,
    )
    return res.reshape(RES), arr, grid.reshape(CX, CY, NZ)


def solution(mesh):
    both = ("gx", "gy")
    return jax.shard_map(
        on_device,
        mesh=mesh,
        in_specs=(
            P(both),
            P(None, both),
            P(both),
            P(both),
            P(both),
            P(None, both),
            P(both),
            P(both, None),
            P(),
            P(),
        ),
        out_specs=(P(both), P(both, None), P("gx", "gy", None)),
        check_vma=False,
    )
```

```python
import functools

import jax
import jax.numpy as jnp
from jax import lax
from jax.experimental import pallas as pl
from jax.experimental.pallas import tpu as pltpu
from jax.sharding import PartitionSpec as P

F32 = jnp.float32
BF16 = jnp.bfloat16
MESH = pl.DeviceIdType.MESH
CX = 32
CY = 16
NZ = 128
TAPS = 13
XP = 40
YR = 19
YP = 20
CP = 24
ROWS = YP * XP
RES = 2048
ARR = 1024
ATOMS = RES + ARR
MOV = 512
FH = 9
CH = 4


def iota(shape, dim):
    return lax.broadcasted_iota(jnp.int32, shape, dim)


def split2(v):
    hi = v.astype(BF16)
    return hi, (v - hi.astype(F32)).astype(BF16)


def split3(v):
    hi = v.astype(BF16)
    rest = v - hi.astype(F32)
    mid = rest.astype(BF16)
    return hi, mid, (rest - mid.astype(F32)).astype(BF16)


def dot_nt(a, b):
    return lax.dot_general(a, b, (((1,), (1,)), ((), ())), preferred_element_type=F32)


def dot_nn(a, b):
    return lax.dot_general(a, b, (((1,), (0,)), ((), ())), preferred_element_type=F32)


def spline(u):
    r = 1.0 - u
    s = u * u
    c = s * u
    return (
        r * r * r * (1.0 / 6.0),
        (3.0 * c - 6.0 * s + 4.0) * (1.0 / 6.0),
        (-3.0 * c + 3.0 * s + 3.0 * u + 1.0) * (1.0 / 6.0),
        c * (1.0 / 6.0),
    )


def pick(d, w, row):
    out = jnp.zeros(d.shape, F32)
    for k in range(4):
        out = jnp.where(d == k, w[k][row : row + 1], out)
    return out


def build_group(block, lane0, x0, a_ref, wz_ref, own):
    lanes = pl.ds(pl.multiple_of(lane0, 128), 128)
    xrows = XP if own is not None else 16
    weights = spline(block)
    cell = jnp.maximum(block[4:5] - 1.0, 0.0).astype(jnp.int32)
    cx = lax.shift_right_logical(cell, 11) - x0
    cy = lax.shift_right_logical(cell, 7) & 15
    cz = cell & 127
    wx = pick(iota((xrows, 128), 0) - cx, weights, 1)
    wy = pick(iota((CP, 128), 0) - cy, weights, 2)
    wz = pick((iota((NZ, 128), 0) - cz) & 127, weights, 3)
    if own is not None:
        own[0][:, lanes] = wx
        own[1][:, lanes] = wy
    hi, lo = split2(wz)
    wz_ref[0:NZ, lanes] = hi
    wz_ref[NZ : 2 * NZ, lanes] = lo
    wxq = wx * block[0:1]
    for p in range(YP // 2):
        blk = jnp.concatenate(
            [wy[2 * p : 2 * p + 1] * wxq, wy[2 * p + 1 : 2 * p + 2] * wxq], axis=0
        )
        a_ref[p * 2 * xrows : (p + 1) * 2 * xrows, lanes] = blk.astype(BF16)


def spread_chunk(lane0, size, acc_ref, a_ref, wz_ref):
    lanes = pl.ds(pl.multiple_of(lane0, 256), size)
    acc_ref[...] += dot_nt(a_ref[:, lanes], wz_ref[:, lanes])


def tap_sum(t, taps_ref, dim):
    out = jnp.zeros(t.shape, F32)
    for k in range(TAPS):
        out = jnp.where(t == k, taps_ref[dim, k], out)
    return out


def kernel(
    nx,
    ny,
    rq_hbm,
    rf_hbm,
    rc_hbm,
    count_hbm,
    mq_hbm,
    mf_hbm,
    mc_hbm,
    md_hbm,
    ft_hbm,
    ct_hbm,
    res_hbm,
    arr_hbm,
    grid_hbm,
    res_ref,
    arr_ref,
    grid_ref,
    rq_ref,
    rf_ref,
    rc_ref,
    count_ref,
    mq_ref,
    mf_ref,
    mc_ref,
    md_ref,
    ft_ref,
    ct_ref,
    pay_ref,
    snd_ref,
    b1_ref,
    t2_ref,
    r2_ref,
    rt_ref,
    rb_ref,
    rl_ref,
    rr_ref,
    a_ref,
    al_ref,
    ar_ref,
    wx_ref,
    wy_ref,
    wz_ref,
    wl_ref,
    wr_ref,
    acc_ref,
    accl_ref,
    accr_ref,
    xh_ref,
    bx_ref,
    zf_ref,
    zc_ref,
    f_ref,
    c3_ref,
    fl_ref,
    fr_ref,
    cl_ref,
    cr_ref,
    fin_ref,
    cin_ref,
    fo_ref,
    up_ref,
    hb_ref,
    ao_ref,
    in_sem,
    out_sem,
    s1_sem,
    r1_sem,
    s2_sem,
    r2_sem,
    sx_sem,
    rx_sem,
    sy_sem,
    ry_sem,
):
    gx = lax.axis_index("gx")
    gy = lax.axis_index("gy")

    inputs = [
        pltpu.make_async_copy(src, dst, in_sem.at[n])
        for n, (src, dst) in enumerate(
            (
                (md_hbm, md_ref),
                (mq_hbm, mq_ref),
                (mf_hbm, mf_ref),
                (mc_hbm, mc_ref),
                (count_hbm, count_ref),
                (rq_hbm, rq_ref),
                (rf_hbm, rf_ref),
                (rc_hbm, rc_ref),
                (ft_hbm, ft_ref),
                (ct_hbm, ct_ref),
            )
        )
    ]
    for copy in inputs:
        copy.start()

    barrier = pltpu.get_barrier_semaphore()
    for k in range(1, ny):
        pl.semaphore_signal(
            barrier, inc=1, device_id=(gx, lax.rem(gy + k, ny)), device_id_type=MESH
        )
    for k in range(1, nx):
        pl.semaphore_signal(
            barrier, inc=1, device_id=(lax.rem(gx + k, nx), gy), device_id_type=MESH
        )
    for copy in inputs[:4]:
        copy.wait()

    with jax.named_scope("pack"):
        dest = md_ref[...]
        row_of = (dest & (ny - 1)) * nx + lax.div(dest, ny)
        hot = jnp.where(iota((nx * ny, MOV), 0) == row_of, 1.0, 0.0)
        hot16 = hot.astype(BF16)
        earlier = jnp.where(iota((MOV, MOV), 0) < iota((MOV, MOV), 1), 1.0, 0.0)
        counts = dot_nn(hot16, earlier.astype(BF16))
        slot = jnp.sum(hot * counts, axis=0, keepdims=True)
        pay_ref[0:1, :] = mq_ref[...]
        pay_ref[1:4, :] = mf_ref[...]
        pay_ref[4:5, :] = mc_ref[...].astype(F32) + 1.0
        pay_ref[5:8, :] = jnp.zeros((3, MOV), F32)
        pay = pay_ref[...]
        spots = jnp.concatenate([jnp.where(slot == float(s), pay, 0.0) for s in range(8)], axis=0)
        hi, mid, lo = split3(spots)
        packed = dot_nt(hot16, hi) + dot_nt(hot16, mid) + dot_nt(hot16, lo)
        snd_ref[:, 0:64] = packed
        snd_ref[:, 64:128] = jnp.zeros((nx * ny, 64), F32)

    pl.semaphore_wait(barrier, nx + ny - 2)

    def hop1(k):
        to = lax.rem(gy + k, ny)
        return pltpu.make_async_remote_copy(
            src_ref=snd_ref.at[pl.ds(pl.multiple_of(to * nx, nx), nx), :],
            dst_ref=b1_ref.at[pl.ds(pl.multiple_of(gy * nx, nx), nx), :],
            send_sem=s1_sem.at[k],
            recv_sem=r1_sem.at[k],
            device_id=(gx, to),
            device_id_type=MESH,
        )

    for k in range(1, ny):
        hop1(k).start()
    mine = pl.ds(pl.multiple_of(gy * nx, nx), nx)
    b1_ref[mine, :] = snd_ref[mine, :]

    for copy in inputs[4:]:
        copy.wait()
    for g in range(RES // 128):
        live = iota((1, 128), 1) + g * 128 < count_ref[0]
        rb_ref[g, 0:1, :] = jnp.where(live, rq_ref[g : g + 1, :], 0.0)
        rb_ref[g, 1:4, :] = rf_ref[:, g * 128 : (g + 1) * 128]
        rb_ref[g, 4:5, :] = rc_ref[g : g + 1, :].astype(F32) + 1.0
        rb_ref[g, 5:8, :] = jnp.zeros((3, 128), F32)

    def x_copy(n, dst, to):
        return pltpu.make_async_remote_copy(
            src_ref=rb_ref,
            dst_ref=dst,
            send_sem=sx_sem.at[n],
            recv_sem=rx_sem.at[n],
            device_id=(to, gy),
            device_id_type=MESH,
        )

    x_copies = [
        x_copy(0, rl_ref, lax.rem(gx + 1, nx)),
        x_copy(1, rr_ref, lax.rem(gx + nx - 1, nx)),
    ]
    for copy in x_copies:
        copy.start()

    acc_ref[...] = jnp.zeros_like(acc_ref)
    accl_ref[...] = jnp.zeros_like(accl_ref)
    accr_ref[...] = jnp.zeros_like(accr_ref)

    def own_res(c, carry):
        for n in range(4):
            g = c * 4 + n
            build_group(rb_ref[g], g * 128, 0, a_ref, wz_ref, (wx_ref, wy_ref))
        spread_chunk(c * 512, 512, acc_ref, a_ref, wz_ref)
        return carry

    lax.fori_loop(0, RES // 512, own_res, 0)

    for k in range(1, ny):
        hop1(k).wait()
    for g in range(nx):
        t2_ref[g + 1] = b1_ref[pl.ds(g, ny, stride=nx), :]
    t2_ref[0] = t2_ref[nx]
    t2_ref[nx + 1] = t2_ref[1]

    def hop2(k):
        to = lax.rem(gx + k, nx)
        return pltpu.make_async_remote_copy(
            src_ref=t2_ref.at[pl.ds(to, 3)],
            dst_ref=r2_ref.at[gx],
            send_sem=s2_sem.at[k],
            recv_sem=r2_sem.at[k],
            device_id=(to, gy),
            device_id_type=MESH,
        )

    for k in range(1, nx):
        hop2(k).start()
    r2_ref[gx] = t2_ref[pl.ds(gx, 3)]

    for copy in x_copies:
        copy.wait()

    def near_res(c, carry):
        for n in range(4):
            g = c * 4 + n
            build_group(rl_ref[g], g * 128, 20, al_ref, wl_ref, None)
            build_group(rr_ref[g], g * 128, 0, ar_ref, wr_ref, None)
        spread_chunk(c * 512, 512, accl_ref, al_ref, wl_ref)
        spread_chunk(c * 512, 512, accr_ref, ar_ref, wr_ref)
        return carry

    lax.fori_loop(0, RES // 512, near_res, 0)

    with jax.named_scope("matrices"):
        col = iota((64, 256), 1)
        part = jnp.where(col >= 160, 2, jnp.where(col >= 80, 1, 0))
        base = col - part * 80
        pos = jnp.where(base < 48, base, jnp.where(base < 64, base - 60, base - 32))
        out_x = iota((64, 256), 0)
        fine_t = pos - out_x + 6
        coarse_t = lax.shift_right_arithmetic(pos, 1) - (out_x - XP) + 6
        bx = jnp.where(out_x < XP, tap_sum(fine_t, ft_ref, 0), tap_sum(coarse_t, ct_ref, 0))
        bx_hi = bx.astype(BF16).astype(F32)
        bx = jnp.where(part == 2, bx - bx_hi, bx_hi)
        bx_ref[...] = jnp.where(col < 240, bx, 0.0).astype(BF16)
        t = (iota((NZ, NZ), 0) - iota((NZ, NZ), 1) + 6) & 127
        hi, lo = split2(tap_sum(t, ft_ref, 2))
        zf_ref[0:NZ, 0:NZ] = hi
        zf_ref[NZ : 2 * NZ, 0:NZ] = hi
        zf_ref[0:NZ, NZ : 2 * NZ] = lo
        zf_ref[NZ : 2 * NZ, NZ : 2 * NZ] = jnp.zeros((NZ, NZ), BF16)
        r, c = iota((NZ, 2 * NZ), 0), iota((NZ, 2 * NZ), 1)
        t = ((r & 63) - lax.shift_right_logical(c & 127, 1) + 6) & 63
        zc = tap_sum(t, ct_ref, 2)
        same = lax.shift_right_logical(r, 6) == lax.shift_right_logical(c, 7)
        hi, lo = split2(jnp.where(same, zc, 0.0))
        zc_ref[0:NZ, :] = hi
        zc_ref[NZ : 2 * NZ, :] = hi
        zc_ref[2 * NZ : 3 * NZ, :] = lo

    for k in range(1, nx):
        hop2(k).wait()

    for n in range(3):
        rt_ref[n] = r2_ref[:, n].reshape(nx * ny, 128).T

    def all_arr(c, carry):
        for n in range(4):
            s = c * 4 + n
            at = RES + s * 128
            rows = pl.ds(pl.multiple_of(s * 8, 8), 8)
            build_group(rt_ref[1, rows, :], at, 0, a_ref, wz_ref, (wx_ref, wy_ref))
            build_group(rt_ref[0, rows, :], at, 20, al_ref, wl_ref, None)
            build_group(rt_ref[2, rows, :], at, 0, ar_ref, wr_ref, None)
        spread_chunk(RES + c * 512, 512, acc_ref, a_ref, wz_ref)
        spread_chunk(RES + c * 512, 512, accl_ref, al_ref, wl_ref)
        spread_chunk(RES + c * 512, 512, accr_ref, ar_ref, wr_ref)
        return carry

    lax.fori_loop(0, ARR // 512, all_arr, 0)

    up_y = lax.rem(gy + 1, ny)
    down_y = lax.rem(gy + ny - 1, ny)
    for y in range(YR):
        lanes = slice(y * NZ, (y + 1) * NZ)
        rows = []
        for ref, count in ((acc_ref, XP), (accl_ref, 16), (accr_ref, 16)):
            part = ref[y * count : (y + 1) * count]
            rows.append(part[:, 0:NZ] + part[:, NZ : 2 * NZ])
            if count == XP:
                rows.append(jnp.zeros((8, NZ), F32))
        hi, lo = split2(jnp.concatenate(rows, axis=0))
        xh_ref[0:80, lanes] = hi
        xh_ref[80:160, lanes] = lo
        xh_ref[160:240, lanes] = hi
        xh_ref[240:256, lanes] = jnp.zeros((16, NZ), BF16)

    conv = dot_nn(bx_ref[...], xh_ref[...])
    f_ref[...] = conv[0:XP]

    r, c = iota((2 * NZ, NZ), 0), iota((2 * NZ, NZ), 1)
    pair = jnp.where(lax.shift_right_logical(r, 1) == c, 1.0, 0.0).astype(BF16)
    coarse = conv[XP : XP + CP]
    tiles = []
    for m in range(5):
        both = []
        for j in (2 * m, 2 * m + 1):
            row = coarse[:, 2 * j * NZ : (2 * j + 1) * NZ]
            if 2 * j + 1 < YR:
                row = row + coarse[:, (2 * j + 1) * NZ : (2 * j + 2) * NZ]
            both.append(row)
        tiles.append(jnp.concatenate(both, axis=1))
    packed = jnp.concatenate(tiles, axis=0)
    hi, lo = split2(packed)
    packed = dot_nn(hi, pair) + dot_nn(lo, pair)
    for m in range(5):
        c3_ref[m] = packed[m * CP : (m + 1) * CP]

    def y_copy(n, src, dst, to):
        return pltpu.make_async_remote_copy(
            src_ref=src,
            dst_ref=dst,
            send_sem=sy_sem.at[n],
            recv_sem=ry_sem.at[n],
            device_id=(gx, to),
            device_id_type=MESH,
        )

    y_copies = [
        y_copy(0, f_ref.at[:, pl.ds(10 * NZ, FH * NZ)], fl_ref, up_y),
        y_copy(1, f_ref.at[:, pl.ds(0, FH * NZ)], fr_ref, down_y),
        y_copy(2, c3_ref.at[pl.ds(1, CH)], cl_ref, up_y),
        y_copy(3, c3_ref.at[pl.ds(0, CH)], cr_ref, down_y),
    ]
    for copy in y_copies:
        copy.start()

    def fine_z(block):
        hi, lo = split2(block)
        both = dot_nn(jnp.concatenate([hi, lo], axis=1), zf_ref[...])
        return both[:, 0:NZ] + both[:, NZ : 2 * NZ]

    def coarse_z(block):
        hi, lo = split2(block)
        return dot_nn(jnp.concatenate([hi, lo], axis=1), zc_ref[0 : 2 * NZ, :]) + dot_nn(
            hi, zc_ref[2 * NZ : 3 * NZ, :]
        )

    def stacked(ref, count):
        return jnp.concatenate([ref[:, y * NZ : (y + 1) * NZ] for y in range(count)], axis=0)

    own = fine_z(stacked(f_ref, YR))
    for y in range(YR):
        fin_ref[:, (y + 6) * NZ : (y + 7) * NZ] = own[y * XP : (y + 1) * XP]
    zero = jnp.zeros((XP, 6 * NZ), F32)
    fin_ref[:, 0 : 6 * NZ] = zero
    fin_ref[:, 25 * NZ : 31 * NZ] = zero
    own = coarse_z(jnp.concatenate([c3_ref[m] for m in range(5)], axis=0))
    zero = jnp.zeros((CP, 6 * NZ), F32)
    cin_ref[:, 0 : 6 * NZ] = zero
    cin_ref[:, 16 * NZ : 22 * NZ] = zero
    for m in range(5):
        cin_ref[:, (2 * m + 6) * NZ : (2 * m + 8) * NZ] = own[m * CP : (m + 1) * CP]

    for copy in y_copies:
        copy.wait()
    for ref, at in ((fl_ref, 0), (fr_ref, 22)):
        halo = fine_z(stacked(ref, FH))
        for y in range(FH):
            fin_ref[:, (y + at) * NZ : (y + at + 1) * NZ] += halo[y * XP : (y + 1) * XP]
    for ref, at in ((cl_ref, 0), (cr_ref, 14)):
        halo = coarse_z(jnp.concatenate([ref[m] for m in range(CH)], axis=0))
        for m in range(CH):
            cin_ref[:, (2 * m + at) * NZ : (2 * m + at + 2) * NZ] += halo[m * CP : (m + 1) * CP]

    def fine_y(i, carry):
        rows = pl.ds(pl.multiple_of(i * 8, 8), 8)
        out = jnp.zeros((8, YR * NZ), F32)
        for k in range(TAPS):
            out = out + ft_ref[1, k] * fin_ref[rows, k * NZ : (k + YR) * NZ]
        fo_ref[rows, 0 : YR * NZ] = out
        fo_ref[rows, YR * NZ : YP * NZ] = jnp.zeros((8, NZ), F32)
        return carry

    lax.fori_loop(0, XP // 8, fine_y, 0)

    def coarse_y(i, carry):
        rows = pl.ds(pl.multiple_of(i * 8, 8), 8)
        out = jnp.zeros((8, 10 * NZ), F32)
        for k in range(TAPS):
            out = out + ct_ref[1, k] * cin_ref[rows, k * NZ : (k + 10) * NZ]
        for j in range(10):
            one = out[:, j * NZ : (j + 1) * NZ]
            up_ref[j, pl.ds(i * 16, 8, stride=2), :] = one
            up_ref[j, pl.ds(i * 16 + 1, 8, stride=2), :] = one
        return carry

    lax.fori_loop(0, CP // 8, coarse_y, 0)

    for p in range(YP // 2):
        add = up_ref[p, 0:XP, :]
        rows = []
        for y in (2 * p, 2 * p + 1):
            total = fo_ref[:, y * NZ : (y + 1) * NZ] + add
            if y < CY:
                for i in range(CX // 8):
                    grid_ref[pl.ds(y + i * 8 * CY, 8, stride=CY), :] = total[i * 8 : i * 8 + 8]
            rows.append(total)
        half = jnp.concatenate(rows, axis=0).astype(BF16)
        hb_ref[p * 2 * XP : (p + 1) * 2 * XP, 0:NZ] = half
        hb_ref[p * 2 * XP : (p + 1) * 2 * XP, NZ : 2 * NZ] = half

    outputs = [
        pltpu.make_async_copy(grid_ref, grid_hbm, out_sem.at[0]),
        pltpu.make_async_copy(res_ref, res_hbm, out_sem.at[1]),
        pltpu.make_async_copy(arr_ref, arr_hbm, out_sem.at[2]),
    ]
    outputs[0].start()

    def sample_at(c):
        lanes = pl.ds(pl.multiple_of(c * 256, 256), 256)
        values = dot_nn(hb_ref[...], wz_ref[:, lanes])
        wy = wy_ref[:, lanes]
        part = jnp.zeros((XP, 256), F32)
        for y in range(YR):
            part = part + wy[y : y + 1] * values[y * XP : (y + 1) * XP]
        return jnp.sum(part * wx_ref[:, lanes], axis=0, keepdims=True)

    def sample_res(c, carry):
        value = sample_at(c)
        live = iota((1, 256), 1) + c * 256 < count_ref[0]
        value = jnp.where(live, value, 0.0)
        res_ref[pl.ds(2 * c, 1), :] = value[:, 0:128]
        res_ref[pl.ds(2 * c + 1, 1), :] = value[:, 128:256]
        return carry

    def sample_arr(c, carry):
        value = sample_at(c + RES // 256)
        ao_ref[pl.ds(2 * c, 1), :] = value[:, 0:128]
        ao_ref[pl.ds(2 * c + 1, 1), :] = value[:, 128:256]
        return carry

    lax.fori_loop(0, RES // 256, sample_res, 0)
    outputs[1].start()
    lax.fori_loop(0, ARR // 256, sample_arr, 0)

    occupied = jnp.concatenate([rt_ref[1, s * 8 + 4 : s * 8 + 5, :] for s in range(8)], axis=0)
    value = jnp.where(occupied > 0.5, ao_ref[...], 0.0)
    hi, mid, lo = split3(value)
    wide = (NZ, ARR)
    spread_to = jnp.where(lax.shift_right_logical(iota(wide, 1), 3) == iota(wide, 0), 1.0, 0.0)
    spread_to = spread_to.astype(BF16)
    flat = dot_nn(hi, spread_to) + dot_nn(mid, spread_to) + dot_nn(lo, spread_to)
    keep = (iota((8, ARR), 1) & 7) == iota((8, ARR), 0)
    arr_ref[...] = jnp.sum(jnp.where(keep, flat, 0.0), axis=0, keepdims=True)
    outputs[2].start()
    for copy in outputs:
        copy.wait()


def hand_out(*refs):
    given, out, held, sems = refs[0:3], refs[3:6], refs[6:9], refs[9]
    reads = [pltpu.make_async_copy(given[n], held[n], sems.at[n]) for n in range(3)]
    writes = [pltpu.make_async_copy(held[n], out[n], sems.at[n + 3]) for n in range(3)]
    for copy in reads:
        copy.start()
    for read, write in zip(reads, writes):
        read.wait()
        write.start()
    for copy in writes:
        copy.wait()


def on_device(rq, rf, rc, count, mq, mf, mc, md, ft, ct):
    nx = lax.axis_size("gx")
    ny = lax.axis_size("gy")
    hbm = pl.BlockSpec(memory_space=pltpu.HBM)
    lanes = YR * NZ
    near = YP * 16
    dma = pltpu.SemaphoreType.DMA
    res, arr, grid = pl.pallas_call(
        functools.partial(kernel, nx, ny),
        out_shape=(
            jax.ShapeDtypeStruct((16, 128), F32),
            jax.ShapeDtypeStruct((1, ARR), F32),
            jax.ShapeDtypeStruct((CX * CY, NZ), F32),
        ),
        in_specs=[hbm] * 10,
        out_specs=(hbm, hbm, hbm),
        scratch_shapes=[
            pltpu.VMEM((16, 128), F32),
            pltpu.VMEM((1, ARR), F32),
            pltpu.VMEM((CX * CY, NZ), F32),
            pltpu.VMEM((16, 128), F32),
            pltpu.VMEM((3, RES), F32),
            pltpu.VMEM((16, 128), jnp.int32),
            pltpu.SMEM((1,), jnp.int32),
            pltpu.VMEM((1, MOV), F32),
            pltpu.VMEM((3, MOV), F32),
            pltpu.VMEM((1, MOV), jnp.int32),
            pltpu.VMEM((1, MOV), jnp.int32),
            pltpu.SMEM((3, TAPS), F32),
            pltpu.SMEM((3, TAPS), F32),
            pltpu.VMEM((8, MOV), F32),
            pltpu.VMEM((128, 128), F32),
            pltpu.VMEM((128, 128), F32),
            pltpu.VMEM((nx + 2, ny, 128), F32),
            pltpu.VMEM((nx, 3, ny, 128), F32),
            pltpu.VMEM((3, 128, 128), F32),
            pltpu.VMEM((16, 8, 128), F32),
            pltpu.VMEM((16, 8, 128), F32),
            pltpu.VMEM((16, 8, 128), F32),
            pltpu.VMEM((ROWS, ATOMS), BF16),
            pltpu.VMEM((near, ATOMS), BF16),
            pltpu.VMEM((near, ATOMS), BF16),
            pltpu.VMEM((XP, ATOMS), F32),
            pltpu.VMEM((CP, ATOMS), F32),
            pltpu.VMEM((2 * NZ, ATOMS), BF16),
            pltpu.VMEM((2 * NZ, ATOMS), BF16),
            pltpu.VMEM((2 * NZ, ATOMS), BF16),
            pltpu.VMEM((ROWS, 2 * NZ), F32),
            pltpu.VMEM((near, 2 * NZ), F32),
            pltpu.VMEM((near, 2 * NZ), F32),
            pltpu.VMEM((256, lanes), BF16),
            pltpu.VMEM((64, 256), BF16),
            pltpu.VMEM((2 * NZ, 2 * NZ), BF16),
            pltpu.VMEM((3 * NZ, 2 * NZ), BF16),
            pltpu.VMEM((XP, lanes), F32),
            pltpu.VMEM((5, CP, NZ), F32),
            pltpu.VMEM((XP, FH * NZ), F32),
            pltpu.VMEM((XP, FH * NZ), F32),
            pltpu.VMEM((CH, CP, NZ), F32),
            pltpu.VMEM((CH, CP, NZ), F32),
            pltpu.VMEM((XP, 31 * NZ), F32),
            pltpu.VMEM((CP, 22 * NZ), F32),
            pltpu.VMEM((XP, YP * NZ), F32),
            pltpu.VMEM((10, 2 * CP, NZ), F32),
            pltpu.VMEM((ROWS, 2 * NZ), BF16),
            pltpu.VMEM((8, 128), F32),
            dma((10,)),
            dma((3,)),
            dma((ny,)),
            dma((ny,)),
            dma((nx,)),
            dma((nx,)),
            dma((2,)),
            dma((2,)),
            dma((4,)),
            dma((4,)),
        ],
        compiler_params=pltpu.CompilerParams(
            collective_id=0, has_side_effects=True, vmem_limit_bytes=64 << 20
        ),
        name="multilevel",
    )(
        rq.reshape(16, 128),
        rf,
        rc.reshape(16, 128),
        count,
        mq.reshape(1, MOV),
        mf,
        mc.reshape(1, MOV),
        md.reshape(1, MOV),
        ft,
        ct,
    )
    res, arr, grid = pl.pallas_call(
        hand_out,
        out_shape=(
            jax.ShapeDtypeStruct((16, 128), F32),
            jax.ShapeDtypeStruct((1, ARR), F32),
            jax.ShapeDtypeStruct((CX * CY, NZ), F32),
        ),
        in_specs=[hbm] * 3,
        out_specs=(hbm, hbm, hbm),
        scratch_shapes=[
            pltpu.VMEM((16, 128), F32),
            pltpu.VMEM((1, ARR), F32),
            pltpu.VMEM((CX * CY, NZ), F32),
            dma((6,)),
        ],
        name="hand_out",
    )(res, arr, grid)
    return res.reshape(RES), arr, grid.reshape(CX, CY, NZ)


def solution(mesh):
    both = ("gx", "gy")
    return jax.shard_map(
        on_device,
        mesh=mesh,
        in_specs=(
            P(both),
            P(None, both),
            P(both),
            P(both),
            P(both),
            P(None, both),
            P(both),
            P(both, None),
            P(),
            P(),
        ),
        out_specs=(P(both), P(both, None), P("gx", "gy", None)),
        check_vma=False,
    )
```

```python
import functools

import jax
import jax.numpy as jnp
from jax import lax
from jax.experimental import pallas as pl
from jax.experimental.pallas import tpu as pltpu
from jax.sharding import PartitionSpec as P

F32 = jnp.float32
BF16 = jnp.bfloat16
MESH = pl.DeviceIdType.MESH
CX = 32
CY = 16
NZ = 128
TAPS = 13
XP = 40
YR = 19
YP = 20
CP = 24
ROWS = YP * XP
RES = 2048
ARR = 1024
ATOMS = RES + ARR
MOV = 512
FH = 9
CH = 4


def iota(shape, dim):
    return lax.broadcasted_iota(jnp.int32, shape, dim)


def split2(v):
    hi = v.astype(BF16)
    return hi, (v - hi.astype(F32)).astype(BF16)


def split3(v):
    hi = v.astype(BF16)
    rest = v - hi.astype(F32)
    mid = rest.astype(BF16)
    return hi, mid, (rest - mid.astype(F32)).astype(BF16)


def dot_nt(a, b):
    return lax.dot_general(a, b, (((1,), (1,)), ((), ())), preferred_element_type=F32)


def dot_nn(a, b):
    return lax.dot_general(a, b, (((1,), (0,)), ((), ())), preferred_element_type=F32)


def spline(u):
    r = 1.0 - u
    s = u * u
    c = s * u
    return (
        r * r * r * (1.0 / 6.0),
        (3.0 * c - 6.0 * s + 4.0) * (1.0 / 6.0),
        (-3.0 * c + 3.0 * s + 3.0 * u + 1.0) * (1.0 / 6.0),
        c * (1.0 / 6.0),
    )


def pick(rows, at, values):
    out = jnp.zeros(rows.shape, rows.dtype)
    for k in range(4):
        out = jnp.where(rows == at[k], values[k], out)
    return out


def prepare(charge, fracs, cells, x0):
    cell = jnp.maximum(cells - 1.0, 0.0).astype(jnp.int32)
    cx = lax.shift_right_logical(cell, 11) - x0
    cy = lax.shift_right_logical(cell, 7) & 15
    cz = cell & 127
    steps = range(4)
    at_x = [cx + k for k in steps]
    at_y = [cy + k for k in steps]
    at_z = [((cz + k) & 127).astype(F32) for k in steps]
    w_x, w_y, w_z = (spline(frac) for frac in fracs)
    hi = [w.astype(BF16).astype(F32) for w in w_z]
    lo = [w - h for w, h in zip(w_z, hi)]
    return charge, at_x, w_x, at_y, w_y, at_z, hi, lo


def build_group(rows, s, lane0, a_ref, wz_ref, own):
    charge, *lists = rows
    charge = charge[s : s + 1]
    at_x, w_x, at_y, w_y, at_z, hi, lo = ([v[s : s + 1] for v in each] for each in lists)
    lanes = lane_window(lane0, 128)
    xrows = XP if own is not None else 16
    wx = pick(iota((xrows, 128), 0), at_x, w_x)
    wy = pick(iota((CP, 128), 0), at_y, w_y)
    if own is not None:
        own[0][:, lanes] = wx
        own[1][:, lanes] = wy
    z = iota((NZ, 128), 0).astype(BF16)
    at_z, hi, lo = ([v.astype(BF16) for v in each] for each in (at_z, hi, lo))
    wz_ref[0:NZ, lanes] = pick(z, at_z, hi)
    wz_ref[NZ : 2 * NZ, lanes] = pick(z, at_z, lo)
    wxq = wx * charge
    for p in range(YP // 2):
        blk = jnp.concatenate(
            [wy[2 * p : 2 * p + 1] * wxq, wy[2 * p + 1 : 2 * p + 2] * wxq], axis=0
        )
        a_ref[p * 2 * xrows : (p + 1) * 2 * xrows, lanes] = blk.astype(BF16)


def lane_window(start, size):
    if isinstance(start, int):
        return slice(start, start + size)
    return pl.ds(pl.multiple_of(start, 128), size)


def spread_chunk(lane0, size, acc_ref, a_ref, wz_ref):
    lanes = lane_window(lane0, size)
    acc_ref[...] += dot_nt(a_ref[:, lanes], wz_ref[:, lanes])


def tap_sum(t, taps_ref, dim):
    out = jnp.zeros(t.shape, F32)
    for k in range(TAPS):
        out = jnp.where(t == k, taps_ref[dim, k], out)
    return out


def kernel(
    nx,
    ny,
    rq_hbm,
    rf_hbm,
    rc_hbm,
    count_hbm,
    mq_hbm,
    mf_hbm,
    mc_hbm,
    md_hbm,
    ft_hbm,
    ct_hbm,
    res_hbm,
    arr_hbm,
    grid_hbm,
    res_ref,
    arr_ref,
    grid_ref,
    rq_ref,
    rf_ref,
    rc_ref,
    count_ref,
    mq_ref,
    mf_ref,
    mc_ref,
    md_ref,
    ft_ref,
    ct_ref,
    pay_ref,
    snd_ref,
    b1_ref,
    t2_ref,
    r2_ref,
    rt_ref,
    rb_ref,
    rl_ref,
    rr_ref,
    a_ref,
    al_ref,
    ar_ref,
    wx_ref,
    wy_ref,
    wz_ref,
    wl_ref,
    wr_ref,
    acc_ref,
    accl_ref,
    accr_ref,
    xh_ref,
    bx_ref,
    zf_ref,
    zc_ref,
    f_ref,
    c3_ref,
    fl_ref,
    fr_ref,
    cl_ref,
    cr_ref,
    fin_ref,
    cin_ref,
    fo_ref,
    up_ref,
    hb_ref,
    ao_ref,
    in_sem,
    out_sem,
    s1_sem,
    r1_sem,
    s2_sem,
    r2_sem,
    sx_sem,
    rx_sem,
    sy_sem,
    ry_sem,
):
    gx = lax.axis_index("gx")
    gy = lax.axis_index("gy")

    inputs = [
        pltpu.make_async_copy(src, dst, in_sem.at[n])
        for n, (src, dst) in enumerate(
            (
                (md_hbm, md_ref),
                (mq_hbm, mq_ref),
                (mf_hbm, mf_ref),
                (mc_hbm, mc_ref),
                (count_hbm, count_ref),
                (rq_hbm, rq_ref),
                (rf_hbm, rf_ref),
                (rc_hbm, rc_ref),
                (ft_hbm, ft_ref),
                (ct_hbm, ct_ref),
            )
        )
    ]
    for copy in inputs:
        copy.start()

    barrier = pltpu.get_barrier_semaphore()
    for k in range(1, ny):
        pl.semaphore_signal(
            barrier, inc=1, device_id=(gx, lax.rem(gy + k, ny)), device_id_type=MESH
        )
    for k in range(1, nx):
        pl.semaphore_signal(
            barrier, inc=1, device_id=(lax.rem(gx + k, nx), gy), device_id_type=MESH
        )
    for copy in inputs[:4]:
        copy.wait()

    with jax.named_scope("pack"):
        dest = md_ref[...]
        row_of = (dest & (ny - 1)) * nx + lax.div(dest, ny)
        hot = jnp.where(iota((nx * ny, MOV), 0) == row_of, 1.0, 0.0)
        hot16 = hot.astype(BF16)
        earlier = jnp.where(iota((MOV, MOV), 0) < iota((MOV, MOV), 1), 1.0, 0.0)
        counts = dot_nn(hot16, earlier.astype(BF16))
        slot = jnp.sum(hot * counts, axis=0, keepdims=True)
        pay_ref[0:1, :] = mq_ref[...]
        pay_ref[1:4, :] = mf_ref[...]
        pay_ref[4:5, :] = mc_ref[...].astype(F32) + 1.0
        at_slot = iota((8, MOV), 0).astype(F32) == slot
        spots = jnp.concatenate(
            [jnp.where(at_slot, pay_ref[n : n + 1, :], 0.0) for n in range(5)]
            + [jnp.zeros((24, MOV), F32)],
            axis=0,
        )
        hi, mid, lo = split3(spots)
        packed = dot_nt(hot16, hi) + dot_nt(hot16, mid) + dot_nt(hot16, lo)
        snd_ref[:, 0:64] = packed
        snd_ref[:, 64:128] = jnp.zeros((nx * ny, 64), F32)

    pl.semaphore_wait(barrier, nx + ny - 2)

    def hop1(k):
        to = lax.rem(gy + k, ny)
        return pltpu.make_async_remote_copy(
            src_ref=snd_ref.at[pl.ds(pl.multiple_of(to * nx, nx), nx), :],
            dst_ref=b1_ref.at[pl.ds(pl.multiple_of(gy * nx, nx), nx), :],
            send_sem=s1_sem.at[k],
            recv_sem=r1_sem.at[k],
            device_id=(gx, to),
            device_id_type=MESH,
        )

    for k in range(1, ny):
        hop1(k).start()
    mine = pl.ds(pl.multiple_of(gy * nx, nx), nx)
    b1_ref[mine, :] = snd_ref[mine, :]

    for copy in inputs[4:]:
        copy.wait()
    rb_ref[0] = jnp.where(iota((16, 128), 0) * 128 < count_ref[0], rq_ref[...], 0.0)
    for d in range(3):
        for g in range(RES // 128):
            rb_ref[1 + d, g : g + 1, :] = rf_ref[d : d + 1, g * 128 : (g + 1) * 128]
    rb_ref[4] = rc_ref[...].astype(F32) + 1.0

    def x_copy(n, dst, to):
        return pltpu.make_async_remote_copy(
            src_ref=rb_ref,
            dst_ref=dst,
            send_sem=sx_sem.at[n],
            recv_sem=rx_sem.at[n],
            device_id=(to, gy),
            device_id_type=MESH,
        )

    x_copies = [
        x_copy(0, rl_ref, lax.rem(gx + 1, nx)),
        x_copy(1, rr_ref, lax.rem(gx + nx - 1, nx)),
    ]
    for copy in x_copies:
        copy.start()

    acc_ref[...] = jnp.zeros_like(acc_ref)
    accl_ref[...] = jnp.zeros_like(accl_ref)
    accr_ref[...] = jnp.zeros_like(accr_ref)

    def residents(block, x0, acc, a, wz, own):
        for half in range(2):
            rows = slice(half * 8, half * 8 + 8)
            ready = prepare(
                block[0, rows, :], [block[1 + d, rows, :] for d in range(3)], block[4, rows, :], x0
            )
            for s in range(8):
                build_group(ready, s, half * 1024 + s * 128, a, wz, own)
            spread_chunk(half * 1024, 1024, acc, a, wz)

    residents(rb_ref, 0, acc_ref, a_ref, wz_ref, (wx_ref, wy_ref))

    for k in range(1, ny):
        hop1(k).wait()
    for g in range(nx):
        t2_ref[g + 1] = b1_ref[pl.ds(g, ny, stride=nx), :]
    t2_ref[0] = t2_ref[nx]
    t2_ref[nx + 1] = t2_ref[1]

    def hop2(k):
        to = lax.rem(gx + k, nx)
        return pltpu.make_async_remote_copy(
            src_ref=t2_ref.at[pl.ds(to, 3)],
            dst_ref=r2_ref.at[gx],
            send_sem=s2_sem.at[k],
            recv_sem=r2_sem.at[k],
            device_id=(to, gy),
            device_id_type=MESH,
        )

    for k in range(1, nx):
        hop2(k).start()
    r2_ref[gx] = t2_ref[pl.ds(gx, 3)]

    for copy in x_copies:
        copy.wait()

    residents(rl_ref, 20, accl_ref, al_ref, wl_ref, None)
    residents(rr_ref, 0, accr_ref, ar_ref, wr_ref, None)

    with jax.named_scope("matrices"):
        col = iota((64, 256), 1)
        part = jnp.where(col >= 160, 2, jnp.where(col >= 80, 1, 0))
        base = col - part * 80
        pos = jnp.where(base < 48, base, jnp.where(base < 64, base - 60, base - 32))
        out_x = iota((64, 256), 0)
        fine_t = pos - out_x + 6
        coarse_t = lax.shift_right_arithmetic(pos, 1) - (out_x - XP) + 6
        bx = jnp.where(out_x < XP, tap_sum(fine_t, ft_ref, 0), tap_sum(coarse_t, ct_ref, 0))
        bx_hi = bx.astype(BF16).astype(F32)
        bx = jnp.where(part == 2, bx - bx_hi, bx_hi)
        bx_ref[...] = jnp.where(col < 240, bx, 0.0).astype(BF16)
        t = (iota((NZ, NZ), 0) - iota((NZ, NZ), 1) + 6) & 127
        hi, lo = split2(tap_sum(t, ft_ref, 2))
        zf_ref[0:NZ, 0:NZ] = hi
        zf_ref[NZ : 2 * NZ, 0:NZ] = hi
        zf_ref[0:NZ, NZ : 2 * NZ] = lo
        zf_ref[NZ : 2 * NZ, NZ : 2 * NZ] = jnp.zeros((NZ, NZ), BF16)
        r, c = iota((NZ, 2 * NZ), 0), iota((NZ, 2 * NZ), 1)
        t = ((r & 63) - lax.shift_right_logical(c & 127, 1) + 6) & 63
        zc = tap_sum(t, ct_ref, 2)
        same = lax.shift_right_logical(r, 6) == lax.shift_right_logical(c, 7)
        hi, lo = split2(jnp.where(same, zc, 0.0))
        zc_ref[0:NZ, :] = hi
        zc_ref[NZ : 2 * NZ, :] = hi
        zc_ref[2 * NZ : 3 * NZ, :] = lo

    for k in range(1, nx):
        hop2(k).wait()

    for n in range(3):
        rt_ref[n] = r2_ref[:, n].reshape(nx * ny, 128).T

    for side, x0, a, wz, own in (
        (1, 0, a_ref, wz_ref, (wx_ref, wy_ref)),
        (0, 20, al_ref, wl_ref, None),
        (2, 0, ar_ref, wr_ref, None),
    ):
        field = [rt_ref[side, f * 8 : f * 8 + 8, :] for f in range(5)]
        ready = prepare(field[0], field[1:4], field[4], x0)
        for s in range(8):
            build_group(ready, s, RES + s * 128, a, wz, own)
    for acc, a, wz in ((acc_ref, a_ref, wz_ref), (accl_ref, al_ref, wl_ref), (accr_ref, ar_ref, wr_ref)):
        spread_chunk(RES, ARR, acc, a, wz)

    up_y = lax.rem(gy + 1, ny)
    down_y = lax.rem(gy + ny - 1, ny)
    for y in range(YR):
        lanes = slice(y * NZ, (y + 1) * NZ)
        rows = []
        for ref, count in ((acc_ref, XP), (accl_ref, 16), (accr_ref, 16)):
            part = ref[y * count : (y + 1) * count]
            rows.append(part[:, 0:NZ] + part[:, NZ : 2 * NZ])
            if count == XP:
                rows.append(jnp.zeros((8, NZ), F32))
        hi, lo = split2(jnp.concatenate(rows, axis=0))
        xh_ref[0:80, lanes] = hi
        xh_ref[80:160, lanes] = lo
        xh_ref[160:240, lanes] = hi
        xh_ref[240:256, lanes] = jnp.zeros((16, NZ), BF16)

    conv = dot_nn(bx_ref[...], xh_ref[...])
    f_ref[...] = conv[0:XP]

    r, c = iota((2 * NZ, NZ), 0), iota((2 * NZ, NZ), 1)
    pair = jnp.where(lax.shift_right_logical(r, 1) == c, 1.0, 0.0).astype(BF16)
    coarse = conv[XP : XP + CP]
    tiles = []
    for m in range(5):
        both = []
        for j in (2 * m, 2 * m + 1):
            row = coarse[:, 2 * j * NZ : (2 * j + 1) * NZ]
            if 2 * j + 1 < YR:
                row = row + coarse[:, (2 * j + 1) * NZ : (2 * j + 2) * NZ]
            both.append(row)
        tiles.append(jnp.concatenate(both, axis=1))
    packed = jnp.concatenate(tiles, axis=0)
    hi, lo = split2(packed)
    packed = dot_nn(hi, pair) + dot_nn(lo, pair)
    for m in range(5):
        c3_ref[m] = packed[m * CP : (m + 1) * CP]

    def y_copy(n, src, dst, to):
        return pltpu.make_async_remote_copy(
            src_ref=src,
            dst_ref=dst,
            send_sem=sy_sem.at[n],
            recv_sem=ry_sem.at[n],
            device_id=(gx, to),
            device_id_type=MESH,
        )

    y_copies = [
        y_copy(0, f_ref.at[:, pl.ds(10 * NZ, FH * NZ)], fl_ref, up_y),
        y_copy(1, f_ref.at[:, pl.ds(0, FH * NZ)], fr_ref, down_y),
        y_copy(2, c3_ref.at[pl.ds(1, CH)], cl_ref, up_y),
        y_copy(3, c3_ref.at[pl.ds(0, CH)], cr_ref, down_y),
    ]
    for copy in y_copies:
        copy.start()

    def fine_z(block):
        hi, lo = split2(block)
        both = dot_nn(jnp.concatenate([hi, lo], axis=1), zf_ref[...])
        return both[:, 0:NZ] + both[:, NZ : 2 * NZ]

    def coarse_z(block):
        hi, lo = split2(block)
        return dot_nn(jnp.concatenate([hi, lo], axis=1), zc_ref[0 : 2 * NZ, :]) + dot_nn(
            hi, zc_ref[2 * NZ : 3 * NZ, :]
        )

    def stacked(ref, count):
        return jnp.concatenate([ref[:, y * NZ : (y + 1) * NZ] for y in range(count)], axis=0)

    own = fine_z(stacked(f_ref, YR))
    for y in range(YR):
        fin_ref[:, (y + 6) * NZ : (y + 7) * NZ] = own[y * XP : (y + 1) * XP]
    zero = jnp.zeros((XP, 6 * NZ), F32)
    fin_ref[:, 0 : 6 * NZ] = zero
    fin_ref[:, 25 * NZ : 31 * NZ] = zero
    own = coarse_z(jnp.concatenate([c3_ref[m] for m in range(5)], axis=0))
    zero = jnp.zeros((CP, 6 * NZ), F32)
    cin_ref[:, 0 : 6 * NZ] = zero
    cin_ref[:, 16 * NZ : 22 * NZ] = zero
    for m in range(5):
        cin_ref[:, (2 * m + 6) * NZ : (2 * m + 8) * NZ] = own[m * CP : (m + 1) * CP]

    for copy in y_copies:
        copy.wait()
    for ref, at in ((fl_ref, 0), (fr_ref, 22)):
        halo = fine_z(stacked(ref, FH))
        for y in range(FH):
            fin_ref[:, (y + at) * NZ : (y + at + 1) * NZ] += halo[y * XP : (y + 1) * XP]
    for ref, at in ((cl_ref, 0), (cr_ref, 14)):
        halo = coarse_z(jnp.concatenate([ref[m] for m in range(CH)], axis=0))
        for m in range(CH):
            cin_ref[:, (2 * m + at) * NZ : (2 * m + at + 2) * NZ] += halo[m * CP : (m + 1) * CP]

    def fine_y(i, carry):
        rows = pl.ds(pl.multiple_of(i * 8, 8), 8)
        out = jnp.zeros((8, YR * NZ), F32)
        for k in range(TAPS):
            out = out + ft_ref[1, k] * fin_ref[rows, k * NZ : (k + YR) * NZ]
        fo_ref[rows, 0 : YR * NZ] = out
        fo_ref[rows, YR * NZ : YP * NZ] = jnp.zeros((8, NZ), F32)
        return carry

    lax.fori_loop(0, XP // 8, fine_y, 0)

    def coarse_y(i, carry):
        rows = pl.ds(pl.multiple_of(i * 8, 8), 8)
        out = jnp.zeros((8, 10 * NZ), F32)
        for k in range(TAPS):
            out = out + ct_ref[1, k] * cin_ref[rows, k * NZ : (k + 10) * NZ]
        for j in range(10):
            one = out[:, j * NZ : (j + 1) * NZ]
            up_ref[j, pl.ds(i * 16, 8, stride=2), :] = one
            up_ref[j, pl.ds(i * 16 + 1, 8, stride=2), :] = one
        return carry

    lax.fori_loop(0, CP // 8, coarse_y, 0)

    for p in range(YP // 2):
        add = up_ref[p, 0:XP, :]
        rows = []
        for y in (2 * p, 2 * p + 1):
            total = fo_ref[:, y * NZ : (y + 1) * NZ] + add
            if y < CY:
                for i in range(CX // 8):
                    grid_ref[pl.ds(y + i * 8 * CY, 8, stride=CY), :] = total[i * 8 : i * 8 + 8]
            rows.append(total)
        half = jnp.concatenate(rows, axis=0).astype(BF16)
        hb_ref[p * 2 * XP : (p + 1) * 2 * XP, 0:NZ] = half
        hb_ref[p * 2 * XP : (p + 1) * 2 * XP, NZ : 2 * NZ] = half

    outputs = [
        pltpu.make_async_copy(grid_ref, grid_hbm, out_sem.at[0]),
        pltpu.make_async_copy(res_ref, res_hbm, out_sem.at[1]),
        pltpu.make_async_copy(arr_ref, arr_hbm, out_sem.at[2]),
    ]
    outputs[0].start()

    def sample_at(c):
        lanes = pl.ds(pl.multiple_of(c * 256, 256), 256)
        values = dot_nn(hb_ref[...], wz_ref[:, lanes])
        wy = wy_ref[:, lanes]
        part = jnp.zeros((XP, 256), F32)
        for y in range(YR):
            part = part + wy[y : y + 1] * values[y * XP : (y + 1) * XP]
        return jnp.sum(part * wx_ref[:, lanes], axis=0, keepdims=True)

    def sample_res(c, carry):
        value = sample_at(c)
        live = iota((1, 256), 1) + c * 256 < count_ref[0]
        value = jnp.where(live, value, 0.0)
        res_ref[pl.ds(2 * c, 1), :] = value[:, 0:128]
        res_ref[pl.ds(2 * c + 1, 1), :] = value[:, 128:256]
        return carry

    def sample_arr(c, carry):
        value = sample_at(c + RES // 256)
        ao_ref[pl.ds(2 * c, 1), :] = value[:, 0:128]
        ao_ref[pl.ds(2 * c + 1, 1), :] = value[:, 128:256]
        return carry

    for c in range(RES // 256):
        sample_res(c, 0)
    outputs[1].start()
    for c in range(ARR // 256):
        sample_arr(c, 0)

    occupied = rt_ref[1, 32:40, :]
    value = jnp.where(occupied > 0.5, ao_ref[...], 0.0)
    hi, mid, lo = split3(value)
    wide = (NZ, ARR)
    spread_to = jnp.where(lax.shift_right_logical(iota(wide, 1), 3) == iota(wide, 0), 1.0, 0.0)
    spread_to = spread_to.astype(BF16)
    flat = dot_nn(hi, spread_to) + dot_nn(mid, spread_to) + dot_nn(lo, spread_to)
    keep = (iota((8, ARR), 1) & 7) == iota((8, ARR), 0)
    arr_ref[...] = jnp.sum(jnp.where(keep, flat, 0.0), axis=0, keepdims=True)
    outputs[2].start()
    for copy in outputs:
        copy.wait()


def hand_out(*refs):
    given, out, held, sems = refs[0:3], refs[3:6], refs[6:9], refs[9]
    reads = [pltpu.make_async_copy(given[n], held[n], sems.at[n]) for n in range(3)]
    writes = [pltpu.make_async_copy(held[n], out[n], sems.at[n + 3]) for n in range(3)]
    for copy in reads:
        copy.start()
    for read, write in zip(reads, writes):
        read.wait()
        write.start()
    for copy in writes:
        copy.wait()


def on_device(rq, rf, rc, count, mq, mf, mc, md, ft, ct):
    nx = lax.axis_size("gx")
    ny = lax.axis_size("gy")
    hbm = pl.BlockSpec(memory_space=pltpu.HBM)
    lanes = YR * NZ
    near = YP * 16
    dma = pltpu.SemaphoreType.DMA
    res, arr, grid = pl.pallas_call(
        functools.partial(kernel, nx, ny),
        out_shape=(
            jax.ShapeDtypeStruct((16, 128), F32),
            jax.ShapeDtypeStruct((1, ARR), F32),
            jax.ShapeDtypeStruct((CX * CY, NZ), F32),
        ),
        in_specs=[hbm] * 10,
        out_specs=(hbm, hbm, hbm),
        scratch_shapes=[
            pltpu.VMEM((16, 128), F32),
            pltpu.VMEM((1, ARR), F32),
            pltpu.VMEM((CX * CY, NZ), F32),
            pltpu.VMEM((16, 128), F32),
            pltpu.VMEM((3, RES), F32),
            pltpu.VMEM((16, 128), jnp.int32),
            pltpu.SMEM((1,), jnp.int32),
            pltpu.VMEM((1, MOV), F32),
            pltpu.VMEM((3, MOV), F32),
            pltpu.VMEM((1, MOV), jnp.int32),
            pltpu.VMEM((1, MOV), jnp.int32),
            pltpu.SMEM((3, TAPS), F32),
            pltpu.SMEM((3, TAPS), F32),
            pltpu.VMEM((8, MOV), F32),
            pltpu.VMEM((128, 128), F32),
            pltpu.VMEM((128, 128), F32),
            pltpu.VMEM((nx + 2, ny, 128), F32),
            pltpu.VMEM((nx, 3, ny, 128), F32),
            pltpu.VMEM((3, 128, 128), F32),
            pltpu.VMEM((5, 16, 128), F32),
            pltpu.VMEM((5, 16, 128), F32),
            pltpu.VMEM((5, 16, 128), F32),
            pltpu.VMEM((ROWS, ATOMS), BF16),
            pltpu.VMEM((near, ATOMS), BF16),
            pltpu.VMEM((near, ATOMS), BF16),
            pltpu.VMEM((XP, ATOMS), F32),
            pltpu.VMEM((CP, ATOMS), F32),
            pltpu.VMEM((2 * NZ, ATOMS), BF16),
            pltpu.VMEM((2 * NZ, ATOMS), BF16),
            pltpu.VMEM((2 * NZ, ATOMS), BF16),
            pltpu.VMEM((ROWS, 2 * NZ), F32),
            pltpu.VMEM((near, 2 * NZ), F32),
            pltpu.VMEM((near, 2 * NZ), F32),
            pltpu.VMEM((256, lanes), BF16),
            pltpu.VMEM((64, 256), BF16),
            pltpu.VMEM((2 * NZ, 2 * NZ), BF16),
            pltpu.VMEM((3 * NZ, 2 * NZ), BF16),
            pltpu.VMEM((XP, lanes), F32),
            pltpu.VMEM((5, CP, NZ), F32),
            pltpu.VMEM((XP, FH * NZ), F32),
            pltpu.VMEM((XP, FH * NZ), F32),
            pltpu.VMEM((CH, CP, NZ), F32),
            pltpu.VMEM((CH, CP, NZ), F32),
            pltpu.VMEM((XP, 31 * NZ), F32),
            pltpu.VMEM((CP, 22 * NZ), F32),
            pltpu.VMEM((XP, YP * NZ), F32),
            pltpu.VMEM((10, 2 * CP, NZ), F32),
            pltpu.VMEM((ROWS, 2 * NZ), BF16),
            pltpu.VMEM((8, 128), F32),
            dma((10,)),
            dma((3,)),
            dma((ny,)),
            dma((ny,)),
            dma((nx,)),
            dma((nx,)),
            dma((2,)),
            dma((2,)),
            dma((4,)),
            dma((4,)),
        ],
        compiler_params=pltpu.CompilerParams(
            collective_id=0, has_side_effects=True, vmem_limit_bytes=64 << 20
        ),
        name="multilevel",
    )(
        rq.reshape(16, 128),
        rf,
        rc.reshape(16, 128),
        count,
        mq.reshape(1, MOV),
        mf,
        mc.reshape(1, MOV),
        md.reshape(1, MOV),
        ft,
        ct,
    )
    res, arr, grid = pl.pallas_call(
        hand_out,
        out_shape=(
            jax.ShapeDtypeStruct((16, 128), F32),
            jax.ShapeDtypeStruct((1, ARR), F32),
            jax.ShapeDtypeStruct((CX * CY, NZ), F32),
        ),
        in_specs=[hbm] * 3,
        out_specs=(hbm, hbm, hbm),
        scratch_shapes=[
            pltpu.VMEM((16, 128), F32),
            pltpu.VMEM((1, ARR), F32),
            pltpu.VMEM((CX * CY, NZ), F32),
            dma((6,)),
        ],
        name="hand_out",
    )(res, arr, grid)
    return res.reshape(RES), arr, grid.reshape(CX, CY, NZ)


def solution(mesh):
    both = ("gx", "gy")
    return jax.shard_map(
        on_device,
        mesh=mesh,
        in_specs=(
            P(both),
            P(None, both),
            P(both),
            P(both),
            P(both),
            P(None, both),
            P(both),
            P(both, None),
            P(),
            P(),
        ),
        out_specs=(P(both), P(both, None), P("gx", "gy", None)),
        check_vma=False,
    )
```

```python
import functools

import jax
import jax.numpy as jnp
from jax import lax
from jax.experimental import pallas as pl
from jax.experimental.pallas import tpu as pltpu
from jax.sharding import PartitionSpec as P

F32 = jnp.float32
BF16 = jnp.bfloat16
MESH = pl.DeviceIdType.MESH
CX = 32
CY = 16
NZ = 128
TAPS = 13
XP = 40
YR = 19
YP = 20
CP = 24
ROWS = YP * XP
RES = 2048
ARR = 1024
ATOMS = RES + ARR
MOV = 512
FH = 9
CH = 4


def iota(shape, dim):
    return lax.broadcasted_iota(jnp.int32, shape, dim)


def split2(v):
    hi = v.astype(BF16)
    return hi, (v - hi.astype(F32)).astype(BF16)


def split3(v):
    hi = v.astype(BF16)
    rest = v - hi.astype(F32)
    mid = rest.astype(BF16)
    return hi, mid, (rest - mid.astype(F32)).astype(BF16)


def dot_nt(a, b):
    return lax.dot_general(a, b, (((1,), (1,)), ((), ())), preferred_element_type=F32)


def dot_nn(a, b):
    return lax.dot_general(a, b, (((1,), (0,)), ((), ())), preferred_element_type=F32)


def spline(u):
    r = 1.0 - u
    s = u * u
    c = s * u
    return (
        r * r * r * (1.0 / 6.0),
        (3.0 * c - 6.0 * s + 4.0) * (1.0 / 6.0),
        (-3.0 * c + 3.0 * s + 3.0 * u + 1.0) * (1.0 / 6.0),
        c * (1.0 / 6.0),
    )


def pick(rows, at, values):
    out = jnp.zeros(rows.shape, rows.dtype)
    for k in range(4):
        out = jnp.where(rows == at[k], values[k], out)
    return out


def prepare(charge, fracs, cells, x0):
    cell = jnp.maximum(cells - 1.0, 0.0).astype(jnp.int32)
    cx = lax.shift_right_logical(cell, 11) - x0
    cy = lax.shift_right_logical(cell, 7) & 15
    cz = cell & 127
    steps = range(4)
    at_x = [cx + k for k in steps]
    at_y = [cy + k for k in steps]
    at_z = [((cz + k) & 127).astype(F32) for k in steps]
    w_x, w_y, w_z = (spline(frac) for frac in fracs)
    hi = [w.astype(BF16).astype(F32) for w in w_z]
    lo = [w - h for w, h in zip(w_z, hi)]
    return charge, at_x, w_x, at_y, w_y, at_z, hi, lo


def build_group(rows, s, lane0, a_ref, wz_ref, own):
    charge, *lists = rows
    charge = charge[s : s + 1]
    at_x, w_x, at_y, w_y, at_z, hi, lo = ([v[s : s + 1] for v in each] for each in lists)
    lanes = lane_window(lane0, 128)
    xrows = XP if own is not None else 16
    wx = pick(iota((xrows, 128), 0), at_x, w_x)
    wy = pick(iota((CP, 128), 0), at_y, w_y)
    if own is not None:
        own[0][:, lanes] = wx
        own[1][:, lanes] = wy
    z = iota((NZ, 128), 0).astype(BF16)
    at_z, hi, lo = ([v.astype(BF16) for v in each] for each in (at_z, hi, lo))
    wz_ref[0:NZ, lanes] = pick(z, at_z, hi)
    if own is not None:
        wz_ref[NZ : 2 * NZ, lanes] = pick(z, at_z, lo)
    wxq = wx * charge
    for p in range(YP // 2):
        blk = jnp.concatenate(
            [wy[2 * p : 2 * p + 1] * wxq, wy[2 * p + 1 : 2 * p + 2] * wxq], axis=0
        )
        a_ref[p * 2 * xrows : (p + 1) * 2 * xrows, lanes] = blk.astype(BF16)


def lane_window(start, size):
    if isinstance(start, int):
        return slice(start, start + size)
    return pl.ds(pl.multiple_of(start, 128), size)


def spread_chunk(lane0, size, acc_ref, a_ref, wz_ref):
    lanes = lane_window(lane0, size)
    acc_ref[...] += dot_nt(a_ref[:, lanes], wz_ref[0:NZ, lanes])


def tap_sum(t, taps_ref, dim):
    out = jnp.zeros(t.shape, F32)
    for k in range(TAPS):
        out = jnp.where(t == k, taps_ref[dim, k], out)
    return out


def kernel(
    nx,
    ny,
    rq_hbm,
    rf_hbm,
    rc_hbm,
    count_hbm,
    mq_hbm,
    mf_hbm,
    mc_hbm,
    md_hbm,
    ft_hbm,
    ct_hbm,
    res_hbm,
    arr_hbm,
    grid_hbm,
    res_ref,
    arr_ref,
    grid_ref,
    rq_ref,
    rf_ref,
    rc_ref,
    count_ref,
    mq_ref,
    mf_ref,
    mc_ref,
    md_ref,
    ft_ref,
    ct_ref,
    pay_ref,
    snd_ref,
    b1_ref,
    t2_ref,
    r2_ref,
    rt_ref,
    rb_ref,
    rl_ref,
    rr_ref,
    a_ref,
    al_ref,
    ar_ref,
    wx_ref,
    wy_ref,
    wz_ref,
    wl_ref,
    wr_ref,
    acc_ref,
    accl_ref,
    accr_ref,
    xh_ref,
    bx_ref,
    zf_ref,
    zc_ref,
    f_ref,
    c3_ref,
    fl_ref,
    fr_ref,
    cl_ref,
    cr_ref,
    fin_ref,
    cin_ref,
    fo_ref,
    up_ref,
    hb_ref,
    ao_ref,
    in_sem,
    out_sem,
    s1_sem,
    r1_sem,
    s2_sem,
    r2_sem,
    sx_sem,
    rx_sem,
    sy_sem,
    ry_sem,
):
    gx = lax.axis_index("gx")
    gy = lax.axis_index("gy")

    barrier = pltpu.get_barrier_semaphore()
    for k in range(1, ny):
        pl.semaphore_signal(
            barrier, inc=1, device_id=(gx, lax.rem(gy + k, ny)), device_id_type=MESH
        )
    for k in range(1, nx):
        pl.semaphore_signal(
            barrier, inc=1, device_id=(lax.rem(gx + k, nx), gy), device_id_type=MESH
        )

    inputs = [
        pltpu.make_async_copy(src, dst, in_sem.at[n])
        for n, (src, dst) in enumerate(
            (
                (md_hbm, md_ref),
                (mq_hbm, mq_ref),
                (mf_hbm, mf_ref),
                (mc_hbm, mc_ref),
                (count_hbm, count_ref),
                (rq_hbm, rq_ref),
                (rf_hbm, rf_ref),
                (rc_hbm, rc_ref),
                (ft_hbm, ft_ref),
                (ct_hbm, ct_ref),
            )
        )
    ]
    for copy in inputs:
        copy.start()

    for copy in inputs[:4]:
        copy.wait()

    with jax.named_scope("pack"):
        dest = md_ref[...]
        row_of = (dest & (ny - 1)) * nx + lax.div(dest, ny)
        hot = jnp.where(iota((nx * ny, MOV), 0) == row_of, 1.0, 0.0)
        hot16 = hot.astype(BF16)
        earlier = jnp.where(iota((MOV, MOV), 0) < iota((MOV, MOV), 1), 1.0, 0.0)
        counts = dot_nn(hot16, earlier.astype(BF16))
        slot = jnp.sum(hot * counts, axis=0, keepdims=True)
        pay_ref[0:1, :] = mq_ref[...]
        pay_ref[1:4, :] = mf_ref[...]
        pay_ref[4:5, :] = mc_ref[...].astype(F32) + 1.0
        at_slot = iota((8, MOV), 0).astype(F32) == slot
        spots = jnp.concatenate(
            [jnp.where(at_slot, pay_ref[n : n + 1, :], 0.0) for n in range(5)]
            + [jnp.zeros((24, MOV), F32)],
            axis=0,
        )
        hi, mid, lo = split3(spots)
        packed = dot_nt(hot16, hi) + dot_nt(hot16, mid) + dot_nt(hot16, lo)
        snd_ref[:, 0:64] = packed
        snd_ref[:, 64:128] = jnp.zeros((nx * ny, 64), F32)

    pl.semaphore_wait(barrier, nx + ny - 2)

    def hop1(k):
        to = lax.rem(gy + k, ny)
        return pltpu.make_async_remote_copy(
            src_ref=snd_ref.at[pl.ds(pl.multiple_of(to * nx, nx), nx), :],
            dst_ref=b1_ref.at[pl.ds(pl.multiple_of(gy * nx, nx), nx), :],
            send_sem=s1_sem.at[k],
            recv_sem=r1_sem.at[k],
            device_id=(gx, to),
            device_id_type=MESH,
        )

    for k in range(1, ny):
        hop1(k).start()
    mine = pl.ds(pl.multiple_of(gy * nx, nx), nx)
    b1_ref[mine, :] = snd_ref[mine, :]

    for copy in inputs[4:]:
        copy.wait()
    rb_ref[0] = jnp.where(iota((16, 128), 0) * 128 < count_ref[0], rq_ref[...], 0.0)
    for d in range(3):
        for g in range(RES // 128):
            rb_ref[1 + d, g : g + 1, :] = rf_ref[d : d + 1, g * 128 : (g + 1) * 128]
    rb_ref[4] = rc_ref[...].astype(F32) + 1.0

    def x_copy(n, dst, to):
        return pltpu.make_async_remote_copy(
            src_ref=rb_ref,
            dst_ref=dst,
            send_sem=sx_sem.at[n],
            recv_sem=rx_sem.at[n],
            device_id=(to, gy),
            device_id_type=MESH,
        )

    x_copies = [
        x_copy(0, rl_ref, lax.rem(gx + 1, nx)),
        x_copy(1, rr_ref, lax.rem(gx + nx - 1, nx)),
    ]
    for copy in x_copies:
        copy.start()

    acc_ref[...] = jnp.zeros_like(acc_ref)
    accl_ref[...] = jnp.zeros_like(accl_ref)
    accr_ref[...] = jnp.zeros_like(accr_ref)

    def residents(block, x0, acc, a, wz, own):
        for half in range(2):
            rows = slice(half * 8, half * 8 + 8)
            ready = prepare(
                block[0, rows, :], [block[1 + d, rows, :] for d in range(3)], block[4, rows, :], x0
            )
            for s in range(8):
                build_group(ready, s, half * 1024 + s * 128, a, wz, own)
            spread_chunk(half * 1024, 1024, acc, a, wz)

    residents(rb_ref, 0, acc_ref, a_ref, wz_ref, (wx_ref, wy_ref))

    for k in range(1, ny):
        hop1(k).wait()
    for g in range(nx):
        t2_ref[g + 1] = b1_ref[pl.ds(g, ny, stride=nx), :]
    t2_ref[0] = t2_ref[nx]
    t2_ref[nx + 1] = t2_ref[1]

    def hop2(k):
        to = lax.rem(gx + k, nx)
        return pltpu.make_async_remote_copy(
            src_ref=t2_ref.at[pl.ds(to, 3)],
            dst_ref=r2_ref.at[gx],
            send_sem=s2_sem.at[k],
            recv_sem=r2_sem.at[k],
            device_id=(to, gy),
            device_id_type=MESH,
        )

    for k in range(1, nx):
        hop2(k).start()
    r2_ref[gx] = t2_ref[pl.ds(gx, 3)]

    for copy in x_copies:
        copy.wait()

    residents(rl_ref, 20, accl_ref, al_ref, wl_ref, None)
    residents(rr_ref, 0, accr_ref, ar_ref, wr_ref, None)

    with jax.named_scope("matrices"):
        col = iota((64, 256), 1)
        part = jnp.where(col >= 160, 2, jnp.where(col >= 80, 1, 0))
        base = col - part * 80
        pos = jnp.where(base < 48, base, jnp.where(base < 64, base - 60, base - 32))
        out_x = iota((64, 256), 0)
        fine_t = pos - out_x + 6
        coarse_t = lax.shift_right_arithmetic(pos, 1) - (out_x - XP) + 6
        bx = jnp.where(out_x < XP, tap_sum(fine_t, ft_ref, 0), tap_sum(coarse_t, ct_ref, 0))
        bx_hi = bx.astype(BF16).astype(F32)
        bx = jnp.where(part == 2, bx - bx_hi, bx_hi)
        bx_ref[...] = jnp.where(col < 240, bx, 0.0).astype(BF16)
        t = (iota((NZ, NZ), 0) - iota((NZ, NZ), 1) + 6) & 127
        hi, lo = split2(tap_sum(t, ft_ref, 2))
        zf_ref[0:NZ, 0:NZ] = hi
        zf_ref[NZ : 2 * NZ, 0:NZ] = hi
        zf_ref[0:NZ, NZ : 2 * NZ] = lo
        zf_ref[NZ : 2 * NZ, NZ : 2 * NZ] = jnp.zeros((NZ, NZ), BF16)
        r, c = iota((NZ, 2 * NZ), 0), iota((NZ, 2 * NZ), 1)
        t = ((r & 63) - lax.shift_right_logical(c & 127, 1) + 6) & 63
        zc = tap_sum(t, ct_ref, 2)
        same = lax.shift_right_logical(r, 6) == lax.shift_right_logical(c, 7)
        hi, lo = split2(jnp.where(same, zc, 0.0))
        zc_ref[0:NZ, :] = hi
        zc_ref[NZ : 2 * NZ, :] = hi
        zc_ref[2 * NZ : 3 * NZ, :] = lo

    for k in range(1, nx):
        hop2(k).wait()

    for n in range(3):
        rt_ref[n] = r2_ref[:, n].reshape(nx * ny, 128).T

    boxes = (
        (1, 0, acc_ref, a_ref, wz_ref, (wx_ref, wy_ref)),
        (0, 20, accl_ref, al_ref, wl_ref, None),
        (2, 0, accr_ref, ar_ref, wr_ref, None),
    )
    for n in range(len(boxes) + 1):
        if n < len(boxes):
            side, x0, _, a, wz, own = boxes[n]
            field = [rt_ref[side, f * 8 : f * 8 + 8, :] for f in range(5)]
            ready = prepare(field[0], field[1:4], field[4], x0)
        if n > 0:
            spread_chunk(RES, ARR, *boxes[n - 1][2:5])
        if n < len(boxes):
            for s in range(8):
                build_group(ready, s, RES + s * 128, a, wz, own)

    up_y = lax.rem(gy + 1, ny)
    down_y = lax.rem(gy + ny - 1, ny)
    for y in range(YR):
        lanes = slice(y * NZ, (y + 1) * NZ)
        rows = []
        for ref, count in ((acc_ref, XP), (accl_ref, 16), (accr_ref, 16)):
            part = ref[y * count : (y + 1) * count]
            rows.append(part)
            if count == XP:
                rows.append(jnp.zeros((8, NZ), F32))
        hi, lo = split2(jnp.concatenate(rows, axis=0))
        xh_ref[0:80, lanes] = hi
        xh_ref[80:160, lanes] = lo
        xh_ref[160:240, lanes] = hi
        xh_ref[240:256, lanes] = jnp.zeros((16, NZ), BF16)

    conv = dot_nn(bx_ref[...], xh_ref[...])
    f_ref[...] = conv[0:XP]

    r, c = iota((2 * NZ, NZ), 0), iota((2 * NZ, NZ), 1)
    pair = jnp.where(lax.shift_right_logical(r, 1) == c, 1.0, 0.0).astype(BF16)
    coarse = conv[XP : XP + CP]
    tiles = []
    for m in range(5):
        both = []
        for j in (2 * m, 2 * m + 1):
            row = coarse[:, 2 * j * NZ : (2 * j + 1) * NZ]
            if 2 * j + 1 < YR:
                row = row + coarse[:, (2 * j + 1) * NZ : (2 * j + 2) * NZ]
            both.append(row)
        tiles.append(jnp.concatenate(both, axis=1))
    packed = jnp.concatenate(tiles, axis=0)
    hi, lo = split2(packed)
    packed = dot_nn(hi, pair) + dot_nn(lo, pair)
    for m in range(5):
        c3_ref[m] = packed[m * CP : (m + 1) * CP]

    def y_copy(n, src, dst, to):
        return pltpu.make_async_remote_copy(
            src_ref=src,
            dst_ref=dst,
            send_sem=sy_sem.at[n],
            recv_sem=ry_sem.at[n],
            device_id=(gx, to),
            device_id_type=MESH,
        )

    y_copies = [
        y_copy(0, c3_ref.at[pl.ds(1, CH)], cl_ref, up_y),
        y_copy(1, c3_ref.at[pl.ds(0, CH)], cr_ref, down_y),
        y_copy(2, f_ref.at[:, pl.ds(10 * NZ, FH * NZ)], fl_ref, up_y),
        y_copy(3, f_ref.at[:, pl.ds(0, FH * NZ)], fr_ref, down_y),
    ]
    for copy in y_copies:
        copy.start()

    def fine_z(block):
        hi, lo = split2(block)
        both = dot_nn(jnp.concatenate([hi, lo], axis=1), zf_ref[...])
        return both[:, 0:NZ] + both[:, NZ : 2 * NZ]

    def coarse_z(block):
        hi, lo = split2(block)
        return dot_nn(jnp.concatenate([hi, lo], axis=1), zc_ref[0 : 2 * NZ, :]) + dot_nn(
            hi, zc_ref[2 * NZ : 3 * NZ, :]
        )

    def stacked(ref, count):
        return jnp.concatenate([ref[:, y * NZ : (y + 1) * NZ] for y in range(count)], axis=0)

    own = fine_z(stacked(f_ref, YR))
    for y in range(YR):
        fin_ref[:, (y + 6) * NZ : (y + 7) * NZ] = own[y * XP : (y + 1) * XP]
    zero = jnp.zeros((XP, 6 * NZ), F32)
    fin_ref[:, 0 : 6 * NZ] = zero
    fin_ref[:, 25 * NZ : 31 * NZ] = zero
    own = coarse_z(jnp.concatenate([c3_ref[m] for m in range(5)], axis=0))
    zero = jnp.zeros((CP, 6 * NZ), F32)
    cin_ref[:, 0 : 6 * NZ] = zero
    cin_ref[:, 16 * NZ : 22 * NZ] = zero
    for m in range(5):
        cin_ref[:, (2 * m + 6) * NZ : (2 * m + 8) * NZ] = own[m * CP : (m + 1) * CP]

    for copy in y_copies[0:2]:
        copy.wait()
    for ref, at in ((cl_ref, 0), (cr_ref, 14)):
        halo = coarse_z(jnp.concatenate([ref[m] for m in range(CH)], axis=0))
        for m in range(CH):
            cin_ref[:, (2 * m + at) * NZ : (2 * m + at + 2) * NZ] += halo[m * CP : (m + 1) * CP]

    def coarse_y(i, carry):
        rows = pl.ds(pl.multiple_of(i * 8, 8), 8)
        out = jnp.zeros((8, 10 * NZ), F32)
        for k in range(TAPS):
            out = out + ct_ref[1, k] * cin_ref[rows, k * NZ : (k + 10) * NZ]
        for j in range(10):
            one = out[:, j * NZ : (j + 1) * NZ]
            up_ref[j, pl.ds(i * 16, 8, stride=2), :] = one
            up_ref[j, pl.ds(i * 16 + 1, 8, stride=2), :] = one
        return carry

    lax.fori_loop(0, CP // 8, coarse_y, 0)

    for copy in y_copies[2:4]:
        copy.wait()
    for ref, at in ((fl_ref, 0), (fr_ref, 22)):
        halo = fine_z(stacked(ref, FH))
        for y in range(FH):
            fin_ref[:, (y + at) * NZ : (y + at + 1) * NZ] += halo[y * XP : (y + 1) * XP]

    def fine_y(i, carry):
        rows = pl.ds(pl.multiple_of(i * 8, 8), 8)
        out = jnp.zeros((8, YR * NZ), F32)
        for k in range(TAPS):
            out = out + ft_ref[1, k] * fin_ref[rows, k * NZ : (k + YR) * NZ]
        for y in range(YR):
            fo_ref[rows, y * NZ : (y + 1) * NZ] = (
                out[:, y * NZ : (y + 1) * NZ] + up_ref[y // 2, rows, :]
            )
        fo_ref[rows, YR * NZ : YP * NZ] = jnp.zeros((8, NZ), F32)
        return carry

    lax.fori_loop(0, XP // 8, fine_y, 0)

    for p in range(YP // 2):
        half = jnp.concatenate(
            [fo_ref[:, y * NZ : (y + 1) * NZ] for y in (2 * p, 2 * p + 1)], axis=0
        ).astype(BF16)
        hb_ref[p * 2 * XP : (p + 1) * 2 * XP, 0:NZ] = half
        hb_ref[p * 2 * XP : (p + 1) * 2 * XP, NZ : 2 * NZ] = half

    outputs = [
        pltpu.make_async_copy(grid_ref, grid_hbm, out_sem.at[0]),
        pltpu.make_async_copy(res_ref, res_hbm, out_sem.at[1]),
        pltpu.make_async_copy(arr_ref, arr_hbm, out_sem.at[2]),
    ]

    def values_of(c):
        return dot_nn(hb_ref[...], wz_ref[:, c * 256 : (c + 1) * 256])

    def reduced(c, values):
        lanes = slice(c * 256, (c + 1) * 256)
        wy = wy_ref[:, lanes]
        part = jnp.zeros((XP, 256), F32)
        for y in range(YR):
            part = part + wy[y : y + 1] * values[y * XP : (y + 1) * XP]
        value = jnp.sum(part * wx_ref[:, lanes], axis=0, keepdims=True)
        if c < RES // 256:
            live = iota((1, 256), 1) + c * 256 < count_ref[0]
            value = jnp.where(live, value, 0.0)
            at, ref = 2 * c, res_ref
        else:
            at, ref = 2 * (c - RES // 256), ao_ref
        ref[at : at + 1, :] = value[:, 0:128]
        ref[at + 1 : at + 2, :] = value[:, 128:256]

    for c in range(RES // 256, ATOMS // 256):
        reduced(c, values_of(c))
    for y in range(CY):
        for i in range(CX // 8):
            grid_ref[pl.ds(y + i * 8 * CY, 8, stride=CY), :] = fo_ref[
                i * 8 : i * 8 + 8, y * NZ : (y + 1) * NZ
            ]
    outputs[0].start()

    occupied = rt_ref[1, 32:40, :]
    value = jnp.where(occupied > 0.5, ao_ref[...], 0.0)
    hi, mid, lo = split3(value)
    wide = (NZ, ARR)
    spread_to = jnp.where(lax.shift_right_logical(iota(wide, 1), 3) == iota(wide, 0), 1.0, 0.0)
    spread_to = spread_to.astype(BF16)
    flat = dot_nn(hi, spread_to) + dot_nn(mid, spread_to) + dot_nn(lo, spread_to)
    keep = (iota((8, ARR), 1) & 7) == iota((8, ARR), 0)
    arr_ref[...] = jnp.sum(jnp.where(keep, flat, 0.0), axis=0, keepdims=True)
    outputs[2].start()

    for c in range(RES // 256):
        reduced(c, values_of(c))
    outputs[1].start()
    for copy in outputs:
        copy.wait()


def hand_out(*refs):
    given, out, held, sems = refs[0:3], refs[3:6], refs[6:9], refs[9]
    reads = [pltpu.make_async_copy(given[n], held[n], sems.at[n]) for n in range(3)]
    writes = [pltpu.make_async_copy(held[n], out[n], sems.at[n + 3]) for n in range(3)]
    for copy in reads:
        copy.start()
    for read, write in zip(reads, writes):
        read.wait()
        write.start()
    for copy in writes:
        copy.wait()


def on_device(rq, rf, rc, count, mq, mf, mc, md, ft, ct):
    nx = lax.axis_size("gx")
    ny = lax.axis_size("gy")
    hbm = pl.BlockSpec(memory_space=pltpu.HBM)
    lanes = YR * NZ
    near = YP * 16
    dma = pltpu.SemaphoreType.DMA
    res, arr, grid = pl.pallas_call(
        functools.partial(kernel, nx, ny),
        out_shape=(
            jax.ShapeDtypeStruct((16, 128), F32),
            jax.ShapeDtypeStruct((1, ARR), F32),
            jax.ShapeDtypeStruct((CX * CY, NZ), F32),
        ),
        in_specs=[hbm] * 10,
        out_specs=(hbm, hbm, hbm),
        scratch_shapes=[
            pltpu.VMEM((16, 128), F32),
            pltpu.VMEM((1, ARR), F32),
            pltpu.VMEM((CX * CY, NZ), F32),
            pltpu.VMEM((16, 128), F32),
            pltpu.VMEM((3, RES), F32),
            pltpu.VMEM((16, 128), jnp.int32),
            pltpu.SMEM((1,), jnp.int32),
            pltpu.VMEM((1, MOV), F32),
            pltpu.VMEM((3, MOV), F32),
            pltpu.VMEM((1, MOV), jnp.int32),
            pltpu.VMEM((1, MOV), jnp.int32),
            pltpu.SMEM((3, TAPS), F32),
            pltpu.SMEM((3, TAPS), F32),
            pltpu.VMEM((8, MOV), F32),
            pltpu.VMEM((128, 128), F32),
            pltpu.VMEM((128, 128), F32),
            pltpu.VMEM((nx + 2, ny, 128), F32),
            pltpu.VMEM((nx, 3, ny, 128), F32),
            pltpu.VMEM((3, 128, 128), F32),
            pltpu.VMEM((5, 16, 128), F32),
            pltpu.VMEM((5, 16, 128), F32),
            pltpu.VMEM((5, 16, 128), F32),
            pltpu.VMEM((ROWS, ATOMS), BF16),
            pltpu.VMEM((near, ATOMS), BF16),
            pltpu.VMEM((near, ATOMS), BF16),
            pltpu.VMEM((XP, ATOMS), F32),
            pltpu.VMEM((CP, ATOMS), F32),
            pltpu.VMEM((2 * NZ, ATOMS), BF16),
            pltpu.VMEM((NZ, ATOMS), BF16),
            pltpu.VMEM((NZ, ATOMS), BF16),
            pltpu.VMEM((ROWS, NZ), F32),
            pltpu.VMEM((near, NZ), F32),
            pltpu.VMEM((near, NZ), F32),
            pltpu.VMEM((256, lanes), BF16),
            pltpu.VMEM((64, 256), BF16),
            pltpu.VMEM((2 * NZ, 2 * NZ), BF16),
            pltpu.VMEM((3 * NZ, 2 * NZ), BF16),
            pltpu.VMEM((XP, lanes), F32),
            pltpu.VMEM((5, CP, NZ), F32),
            pltpu.VMEM((XP, FH * NZ), F32),
            pltpu.VMEM((XP, FH * NZ), F32),
            pltpu.VMEM((CH, CP, NZ), F32),
            pltpu.VMEM((CH, CP, NZ), F32),
            pltpu.VMEM((XP, 31 * NZ), F32),
            pltpu.VMEM((CP, 22 * NZ), F32),
            pltpu.VMEM((XP, YP * NZ), F32),
            pltpu.VMEM((10, 2 * CP, NZ), F32),
            pltpu.VMEM((ROWS, 2 * NZ), BF16),
            pltpu.VMEM((8, 128), F32),
            dma((10,)),
            dma((3,)),
            dma((ny,)),
            dma((ny,)),
            dma((nx,)),
            dma((nx,)),
            dma((2,)),
            dma((2,)),
            dma((4,)),
            dma((4,)),
        ],
        compiler_params=pltpu.CompilerParams(
            collective_id=0, has_side_effects=True, vmem_limit_bytes=64 << 20
        ),
        name="multilevel",
    )(
        rq.reshape(16, 128),
        rf,
        rc.reshape(16, 128),
        count,
        mq.reshape(1, MOV),
        mf,
        mc.reshape(1, MOV),
        md.reshape(1, MOV),
        ft,
        ct,
    )
    res, arr, grid = pl.pallas_call(
        hand_out,
        out_shape=(
            jax.ShapeDtypeStruct((16, 128), F32),
            jax.ShapeDtypeStruct((1, ARR), F32),
            jax.ShapeDtypeStruct((CX * CY, NZ), F32),
        ),
        in_specs=[hbm] * 3,
        out_specs=(hbm, hbm, hbm),
        scratch_shapes=[
            pltpu.VMEM((16, 128), F32),
            pltpu.VMEM((1, ARR), F32),
            pltpu.VMEM((CX * CY, NZ), F32),
            dma((6,)),
        ],
        name="hand_out",
    )(res, arr, grid)
    return res.reshape(RES), arr, grid.reshape(CX, CY, NZ)


def solution(mesh):
    both = ("gx", "gy")
    return jax.shard_map(
        on_device,
        mesh=mesh,
        in_specs=(
            P(both),
            P(None, both),
            P(both),
            P(both),
            P(both),
            P(None, both),
            P(both),
            P(both, None),
            P(),
            P(),
        ),
        out_specs=(P(both), P(both, None), P("gx", "gy", None)),
        check_vma=False,
    )
```

```python
import functools

import jax
import jax.numpy as jnp
from jax import lax
from jax.experimental import pallas as pl
from jax.experimental.pallas import tpu as pltpu
from jax.sharding import PartitionSpec as P

F32 = jnp.float32
BF16 = jnp.bfloat16
MESH = pl.DeviceIdType.MESH
CX = 32
CY = 16
NZ = 128
TAPS = 13
XP = 40
YR = 19
YP = 20
CP = 24
ROWS = YP * XP
RES = 2048
ARR = 1024
ATOMS = RES + ARR
MOV = 512
FH = 9
CH = 4


def iota(shape, dim):
    return lax.broadcasted_iota(jnp.int32, shape, dim)


def split2(v):
    hi = v.astype(BF16)
    return hi, (v - hi.astype(F32)).astype(BF16)


def split3(v):
    hi = v.astype(BF16)
    rest = v - hi.astype(F32)
    mid = rest.astype(BF16)
    return hi, mid, (rest - mid.astype(F32)).astype(BF16)


def dot_nt(a, b):
    return lax.dot_general(a, b, (((1,), (1,)), ((), ())), preferred_element_type=F32)


def dot_nn(a, b):
    return lax.dot_general(a, b, (((1,), (0,)), ((), ())), preferred_element_type=F32)


def spline(u):
    r = 1.0 - u
    s = u * u
    c = s * u
    return (
        r * r * r * (1.0 / 6.0),
        (3.0 * c - 6.0 * s + 4.0) * (1.0 / 6.0),
        (-3.0 * c + 3.0 * s + 3.0 * u + 1.0) * (1.0 / 6.0),
        c * (1.0 / 6.0),
    )


def pick(rows, at, values):
    out = jnp.zeros(rows.shape, rows.dtype)
    for k in range(4):
        out = jnp.where(rows == at[k], values[k], out)
    return out


def prepare(charge, fracs, cells, x0):
    cell = jnp.maximum(cells - 1.0, 0.0).astype(jnp.int32)
    cx = lax.shift_right_logical(cell, 11) - x0
    cy = lax.shift_right_logical(cell, 7) & 15
    cz = cell & 127
    steps = range(4)
    at_x = [cx + k for k in steps]
    at_y = [cy + k for k in steps]
    at_z = [((cz + k) & 127).astype(F32) for k in steps]
    w_x, w_y, w_z = (spline(frac) for frac in fracs)
    hi = [w.astype(BF16).astype(F32) for w in w_z]
    lo = [w - h for w, h in zip(w_z, hi)]
    return charge, at_x, w_x, at_y, w_y, at_z, hi, lo


def build_group(rows, s, lane0, a_ref, wz_ref, own):
    charge, *lists = rows
    charge = charge[s : s + 1]
    at_x, w_x, at_y, w_y, at_z, hi, lo = ([v[s : s + 1] for v in each] for each in lists)
    lanes = lane_window(lane0, 128)
    xrows = XP if own is not None else 16
    wx = pick(iota((xrows, 128), 0), at_x, w_x)
    wy = pick(iota((CP, 128), 0), at_y, w_y)
    if own is not None:
        own[0][:, lanes] = wx
        own[1][:, lanes] = wy
    z = iota((NZ, 128), 0).astype(BF16)
    at_z, hi, lo = ([v.astype(BF16) for v in each] for each in (at_z, hi, lo))
    wz_ref[0:NZ, lanes] = pick(z, at_z, hi)
    if own is not None:
        wz_ref[NZ : 2 * NZ, lanes] = pick(z, at_z, lo)
    wxq = wx * charge
    for p in range(YP // 2):
        blk = jnp.concatenate(
            [wy[2 * p : 2 * p + 1] * wxq, wy[2 * p + 1 : 2 * p + 2] * wxq], axis=0
        )
        a_ref[p * 2 * xrows : (p + 1) * 2 * xrows, lanes] = blk.astype(BF16)


def lane_window(start, size):
    if isinstance(start, int):
        return slice(start, start + size)
    return pl.ds(pl.multiple_of(start, 128), size)


def spread_chunk(lane0, size, acc_ref, a_ref, wz_ref):
    lanes = lane_window(lane0, size)
    acc_ref[...] += dot_nt(a_ref[:, lanes], wz_ref[0:NZ, lanes])


def tap_sum(t, taps_ref, dim):
    out = jnp.zeros(t.shape, F32)
    for k in range(TAPS):
        out = jnp.where(t == k, taps_ref[dim, k], out)
    return out


def kernel(
    nx,
    ny,
    rq_hbm,
    rf_hbm,
    rc_hbm,
    count_hbm,
    mq_hbm,
    mf_hbm,
    mc_hbm,
    md_hbm,
    ft_hbm,
    ct_hbm,
    res_hbm,
    arr_hbm,
    grid_hbm,
    res_ref,
    arr_ref,
    grid_ref,
    rq_ref,
    rf_ref,
    rc_ref,
    count_ref,
    mq_ref,
    mf_ref,
    mc_ref,
    md_ref,
    ft_ref,
    ct_ref,
    pay_ref,
    snd_ref,
    b1_ref,
    t2_ref,
    r2_ref,
    rt_ref,
    rb_ref,
    rl_ref,
    rr_ref,
    a_ref,
    al_ref,
    ar_ref,
    wx_ref,
    wy_ref,
    wz_ref,
    wl_ref,
    wr_ref,
    acc_ref,
    accl_ref,
    accr_ref,
    xh_ref,
    bx_ref,
    zf_ref,
    zc_ref,
    f_ref,
    c3_ref,
    fl_ref,
    fr_ref,
    cl_ref,
    cr_ref,
    edge_ref,
    el_ref,
    er_ref,
    fin_ref,
    cin_ref,
    fo_ref,
    up_ref,
    hb_ref,
    ao_ref,
    in_sem,
    out_sem,
    s1_sem,
    r1_sem,
    s2_sem,
    r2_sem,
    sx_sem,
    rx_sem,
    sy_sem,
    ry_sem,
):
    gx = lax.axis_index("gx")
    gy = lax.axis_index("gy")

    barrier = pltpu.get_barrier_semaphore()
    for k in range(1, ny):
        pl.semaphore_signal(
            barrier, inc=1, device_id=(gx, lax.rem(gy + k, ny)), device_id_type=MESH
        )
    for k in range(1, nx):
        pl.semaphore_signal(
            barrier, inc=1, device_id=(lax.rem(gx + k, nx), gy), device_id_type=MESH
        )

    inputs = [
        pltpu.make_async_copy(src, dst, in_sem.at[n])
        for n, (src, dst) in enumerate(
            (
                (md_hbm, md_ref),
                (mq_hbm, mq_ref),
                (mf_hbm, mf_ref),
                (mc_hbm, mc_ref),
                (count_hbm, count_ref),
                (rq_hbm, rq_ref),
                (rf_hbm, rf_ref),
                (rc_hbm, rc_ref),
                (ft_hbm, ft_ref),
                (ct_hbm, ct_ref),
            )
        )
    ]
    for copy in inputs:
        copy.start()

    for copy in inputs[:4]:
        copy.wait()

    with jax.named_scope("pack"):
        dest = md_ref[...]
        row_of = (dest & (ny - 1)) * nx + lax.div(dest, ny)
        hot = jnp.where(iota((nx * ny, MOV), 0) == row_of, 1.0, 0.0)
        hot16 = hot.astype(BF16)
        earlier = jnp.where(iota((MOV, MOV), 0) < iota((MOV, MOV), 1), 1.0, 0.0)
        counts = dot_nn(hot16, earlier.astype(BF16))
        slot = jnp.sum(hot * counts, axis=0, keepdims=True)
        pay_ref[0:1, :] = mq_ref[...]
        pay_ref[1:4, :] = mf_ref[...]
        pay_ref[4:5, :] = mc_ref[...].astype(F32) + 1.0
        at_slot = iota((8, MOV), 0).astype(F32) == slot
        spots = jnp.concatenate(
            [jnp.where(at_slot, pay_ref[n : n + 1, :], 0.0) for n in range(5)]
            + [jnp.zeros((24, MOV), F32)],
            axis=0,
        )
        hi, mid, lo = split3(spots)
        packed = dot_nt(hot16, hi) + dot_nt(hot16, mid) + dot_nt(hot16, lo)
        snd_ref[:, 0:64] = packed
        snd_ref[:, 64:128] = jnp.zeros((nx * ny, 64), F32)

    pl.semaphore_wait(barrier, nx + ny - 2)

    def hop1(k):
        to = lax.rem(gy + k, ny)
        return pltpu.make_async_remote_copy(
            src_ref=snd_ref.at[pl.ds(pl.multiple_of(to * nx, nx), nx), :],
            dst_ref=b1_ref.at[pl.ds(pl.multiple_of(gy * nx, nx), nx), :],
            send_sem=s1_sem.at[k],
            recv_sem=r1_sem.at[k],
            device_id=(gx, to),
            device_id_type=MESH,
        )

    for k in range(1, ny):
        hop1(k).start()
    mine = pl.ds(pl.multiple_of(gy * nx, nx), nx)
    b1_ref[mine, :] = snd_ref[mine, :]

    for copy in inputs[4:]:
        copy.wait()
    rb_ref[0] = jnp.where(iota((16, 128), 0) * 128 < count_ref[0], rq_ref[...], 0.0)
    for d in range(3):
        for g in range(RES // 128):
            rb_ref[1 + d, g : g + 1, :] = rf_ref[d : d + 1, g * 128 : (g + 1) * 128]
    rb_ref[4] = rc_ref[...].astype(F32) + 1.0

    def x_copy(n, dst, to):
        return pltpu.make_async_remote_copy(
            src_ref=rb_ref,
            dst_ref=dst,
            send_sem=sx_sem.at[n],
            recv_sem=rx_sem.at[n],
            device_id=(to, gy),
            device_id_type=MESH,
        )

    x_copies = [
        x_copy(0, rl_ref, lax.rem(gx + 1, nx)),
        x_copy(1, rr_ref, lax.rem(gx + nx - 1, nx)),
    ]
    for copy in x_copies:
        copy.start()

    acc_ref[...] = jnp.zeros_like(acc_ref)
    accl_ref[...] = jnp.zeros_like(accl_ref)
    accr_ref[...] = jnp.zeros_like(accr_ref)

    def residents(block, x0, acc, a, wz, own):
        for half in range(2):
            rows = slice(half * 8, half * 8 + 8)
            ready = prepare(
                block[0, rows, :], [block[1 + d, rows, :] for d in range(3)], block[4, rows, :], x0
            )
            for s in range(8):
                build_group(ready, s, half * 1024 + s * 128, a, wz, own)
            spread_chunk(half * 1024, 1024, acc, a, wz)

    residents(rb_ref, 0, acc_ref, a_ref, wz_ref, (wx_ref, wy_ref))

    for k in range(1, ny):
        hop1(k).wait()
    for g in range(nx):
        t2_ref[g + 1] = b1_ref[pl.ds(g, ny, stride=nx), :]
    t2_ref[0] = t2_ref[nx]
    t2_ref[nx + 1] = t2_ref[1]

    def hop2(k):
        to = lax.rem(gx + k, nx)
        return pltpu.make_async_remote_copy(
            src_ref=t2_ref.at[pl.ds(to, 3)],
            dst_ref=r2_ref.at[gx],
            send_sem=s2_sem.at[k],
            recv_sem=r2_sem.at[k],
            device_id=(to, gy),
            device_id_type=MESH,
        )

    for k in range(1, nx):
        hop2(k).start()
    r2_ref[gx] = t2_ref[pl.ds(gx, 3)]

    for copy in x_copies:
        copy.wait()

    residents(rl_ref, 20, accl_ref, al_ref, wl_ref, None)
    residents(rr_ref, 0, accr_ref, ar_ref, wr_ref, None)

    with jax.named_scope("matrices"):
        col = iota((64, 256), 1)
        part = jnp.where(col >= 160, 2, jnp.where(col >= 80, 1, 0))
        base = col - part * 80
        pos = jnp.where(base < 48, base, jnp.where(base < 64, base - 60, base - 32))
        out_x = iota((64, 256), 0)
        fine_t = pos - out_x + 6
        coarse_t = lax.shift_right_arithmetic(pos, 1) - (out_x - XP) + 6
        bx = jnp.where(out_x < XP, tap_sum(fine_t, ft_ref, 0), tap_sum(coarse_t, ct_ref, 0))
        bx_hi = bx.astype(BF16).astype(F32)
        bx = jnp.where(part == 2, bx - bx_hi, bx_hi)
        bx_ref[...] = jnp.where(col < 240, bx, 0.0).astype(BF16)
        t = (iota((NZ, NZ), 0) - iota((NZ, NZ), 1) + 6) & 127
        hi, lo = split2(tap_sum(t, ft_ref, 2))
        zf_ref[0:NZ, 0:NZ] = hi
        zf_ref[NZ : 2 * NZ, 0:NZ] = hi
        zf_ref[0:NZ, NZ : 2 * NZ] = lo
        zf_ref[NZ : 2 * NZ, NZ : 2 * NZ] = jnp.zeros((NZ, NZ), BF16)
        r, c = iota((NZ, 2 * NZ), 0), iota((NZ, 2 * NZ), 1)
        t = ((r & 63) - lax.shift_right_logical(c & 127, 1) + 6) & 63
        zc = tap_sum(t, ct_ref, 2)
        same = lax.shift_right_logical(r, 6) == lax.shift_right_logical(c, 7)
        hi, lo = split2(jnp.where(same, zc, 0.0))
        zc_ref[0:NZ, :] = hi
        zc_ref[NZ : 2 * NZ, :] = hi
        zc_ref[2 * NZ : 3 * NZ, :] = lo

    for k in range(1, nx):
        hop2(k).wait()

    for n in range(3):
        rt_ref[n] = r2_ref[:, n].reshape(nx * ny, 128).T

    boxes = (
        (1, 0, acc_ref, a_ref, wz_ref, (wx_ref, wy_ref)),
        (0, 20, accl_ref, al_ref, wl_ref, None),
        (2, 0, accr_ref, ar_ref, wr_ref, None),
    )
    for n in range(len(boxes) + 1):
        if n < len(boxes):
            side, x0, _, a, wz, own = boxes[n]
            field = [rt_ref[side, f * 8 : f * 8 + 8, :] for f in range(5)]
            ready = prepare(field[0], field[1:4], field[4], x0)
        if n > 0:
            spread_chunk(RES, ARR, *boxes[n - 1][2:5])
        if n < len(boxes):
            for s in range(8):
                build_group(ready, s, RES + s * 128, a, wz, own)

    up_y = lax.rem(gy + 1, ny)
    down_y = lax.rem(gy + ny - 1, ny)
    for y in range(YR):
        lanes = slice(y * NZ, (y + 1) * NZ)
        rows = []
        for ref, count in ((acc_ref, XP), (accl_ref, 16), (accr_ref, 16)):
            part = ref[y * count : (y + 1) * count]
            rows.append(part)
            if count == XP:
                rows.append(jnp.zeros((8, NZ), F32))
        hi, lo = split2(jnp.concatenate(rows, axis=0))
        xh_ref[0:80, lanes] = hi
        xh_ref[80:160, lanes] = lo
        xh_ref[160:240, lanes] = hi
        xh_ref[240:256, lanes] = jnp.zeros((16, NZ), BF16)

    conv = dot_nn(bx_ref[...], xh_ref[...])
    f_ref[...] = conv[0:XP]

    r, c = iota((2 * NZ, NZ), 0), iota((2 * NZ, NZ), 1)
    pair = jnp.where(lax.shift_right_logical(r, 1) == c, 1.0, 0.0).astype(BF16)
    coarse = conv[XP : XP + CP]
    tiles = []
    for m in range(5):
        both = []
        for j in (2 * m, 2 * m + 1):
            row = coarse[:, 2 * j * NZ : (2 * j + 1) * NZ]
            if 2 * j + 1 < YR:
                row = row + coarse[:, (2 * j + 1) * NZ : (2 * j + 2) * NZ]
            both.append(row)
        tiles.append(jnp.concatenate(both, axis=1))
    packed = jnp.concatenate(tiles, axis=0)
    hi, lo = split2(packed)
    packed = dot_nn(hi, pair) + dot_nn(lo, pair)
    for m in range(5):
        c3_ref[m] = packed[m * CP : (m + 1) * CP]

    def y_copy(n, src, dst, to):
        return pltpu.make_async_remote_copy(
            src_ref=src,
            dst_ref=dst,
            send_sem=sy_sem.at[n],
            recv_sem=ry_sem.at[n],
            device_id=(gx, to),
            device_id_type=MESH,
        )

    for n, (y0, m0) in enumerate(((10, 1), (0, 0))):
        for y in range(FH):
            edge_ref[n, 3 * y : 3 * y + 3, :] = f_ref[32:35, (y0 + y) * NZ : (y0 + y + 1) * NZ]
        edge_ref[n, 27:32, :] = jnp.zeros((5, NZ), F32)
        for m in range(CH):
            edge_ref[n, 32 + 2 * m : 34 + 2 * m, :] = c3_ref[m0 + m, 16:18, :]
    whole, half = pl.ds(0, 32), pl.ds(0, 16)
    y_copies = [
        y_copy(0, edge_ref.at[0], el_ref, up_y),
        y_copy(1, edge_ref.at[1], er_ref, down_y),
        y_copy(2, c3_ref.at[pl.ds(1, CH), half], cl_ref, up_y),
        y_copy(3, c3_ref.at[pl.ds(0, CH), half], cr_ref, down_y),
        y_copy(4, f_ref.at[whole, pl.ds(10 * NZ, FH * NZ)], fl_ref, up_y),
        y_copy(5, f_ref.at[whole, pl.ds(0, FH * NZ)], fr_ref, down_y),
    ]
    for copy in y_copies:
        copy.start()

    def fine_z(block):
        hi, lo = split2(block)
        both = dot_nn(jnp.concatenate([hi, lo], axis=1), zf_ref[...])
        return both[:, 0:NZ] + both[:, NZ : 2 * NZ]

    def coarse_z(block):
        hi, lo = split2(block)
        return dot_nn(jnp.concatenate([hi, lo], axis=1), zc_ref[0 : 2 * NZ, :]) + dot_nn(
            hi, zc_ref[2 * NZ : 3 * NZ, :]
        )

    def stacked(ref, count):
        return jnp.concatenate([ref[:, y * NZ : (y + 1) * NZ] for y in range(count)], axis=0)

    own = fine_z(stacked(f_ref, YR))
    for y in range(YR):
        fin_ref[:, (y + 6) * NZ : (y + 7) * NZ] = own[y * XP : (y + 1) * XP]
    zero = jnp.zeros((XP, 6 * NZ), F32)
    fin_ref[:, 0 : 6 * NZ] = zero
    fin_ref[:, 25 * NZ : 31 * NZ] = zero
    own = coarse_z(jnp.concatenate([c3_ref[m] for m in range(5)], axis=0))
    zero = jnp.zeros((CP, 6 * NZ), F32)
    cin_ref[:, 0 : 6 * NZ] = zero
    cin_ref[:, 16 * NZ : 22 * NZ] = zero
    for m in range(5):
        cin_ref[:, (2 * m + 6) * NZ : (2 * m + 8) * NZ] = own[m * CP : (m + 1) * CP]

    for copy in y_copies[0:4]:
        copy.wait()
    for ref, edge, at in ((cl_ref, el_ref, 0), (cr_ref, er_ref, 14)):
        halo = coarse_z(jnp.concatenate([ref[m] for m in range(CH)] + [edge[32:40, :]], axis=0))
        for m in range(CH):
            lanes = slice((2 * m + at) * NZ, (2 * m + at + 2) * NZ)
            cin_ref[0:16, lanes] += halo[m * 16 : (m + 1) * 16]
            cin_ref[16:18, lanes] += halo[64 + 2 * m : 66 + 2 * m]

    def coarse_y(i, carry):
        rows = pl.ds(pl.multiple_of(i * 8, 8), 8)
        out = jnp.zeros((8, 10 * NZ), F32)
        for k in range(TAPS):
            out = out + ct_ref[1, k] * cin_ref[rows, k * NZ : (k + 10) * NZ]
        for j in range(10):
            one = out[:, j * NZ : (j + 1) * NZ]
            up_ref[j, pl.ds(i * 16, 8, stride=2), :] = one
            up_ref[j, pl.ds(i * 16 + 1, 8, stride=2), :] = one
        return carry

    lax.fori_loop(0, CP // 8, coarse_y, 0)

    for copy in y_copies[4:6]:
        copy.wait()
    for ref, edge, at in ((fl_ref, el_ref, 0), (fr_ref, er_ref, 22)):
        halo = fine_z(jnp.concatenate([stacked(ref, FH), edge[0:32, :]], axis=0))
        for y in range(FH):
            lanes = slice((y + at) * NZ, (y + at + 1) * NZ)
            fin_ref[0:32, lanes] += halo[y * 32 : (y + 1) * 32]
            fin_ref[32:35, lanes] += halo[288 + 3 * y : 291 + 3 * y]

    def fine_y(i, carry):
        rows = pl.ds(pl.multiple_of(i * 8, 8), 8)
        out = jnp.zeros((8, YR * NZ), F32)
        for k in range(TAPS):
            out = out + ft_ref[1, k] * fin_ref[rows, k * NZ : (k + YR) * NZ]
        for y in range(YR):
            fo_ref[rows, y * NZ : (y + 1) * NZ] = (
                out[:, y * NZ : (y + 1) * NZ] + up_ref[y // 2, rows, :]
            )
        fo_ref[rows, YR * NZ : YP * NZ] = jnp.zeros((8, NZ), F32)
        return carry

    lax.fori_loop(0, XP // 8, fine_y, 0)

    for p in range(YP // 2):
        half = jnp.concatenate(
            [fo_ref[:, y * NZ : (y + 1) * NZ] for y in (2 * p, 2 * p + 1)], axis=0
        ).astype(BF16)
        hb_ref[p * 2 * XP : (p + 1) * 2 * XP, 0:NZ] = half
        hb_ref[p * 2 * XP : (p + 1) * 2 * XP, NZ : 2 * NZ] = half

    outputs = [
        pltpu.make_async_copy(grid_ref, grid_hbm, out_sem.at[0]),
        pltpu.make_async_copy(res_ref, res_hbm, out_sem.at[1]),
        pltpu.make_async_copy(arr_ref, arr_hbm, out_sem.at[2]),
    ]

    def values_of(c):
        return dot_nn(hb_ref[...], wz_ref[:, c * 256 : (c + 1) * 256])

    def reduced(c, values):
        lanes = slice(c * 256, (c + 1) * 256)
        wy = wy_ref[:, lanes]
        part = jnp.zeros((XP, 256), F32)
        for y in range(YR):
            part = part + wy[y : y + 1] * values[y * XP : (y + 1) * XP]
        value = jnp.sum(part * wx_ref[:, lanes], axis=0, keepdims=True)
        if c < RES // 256:
            live = iota((1, 256), 1) + c * 256 < count_ref[0]
            value = jnp.where(live, value, 0.0)
            at, ref = 2 * c, res_ref
        else:
            at, ref = 2 * (c - RES // 256), ao_ref
        ref[at : at + 1, :] = value[:, 0:128]
        ref[at + 1 : at + 2, :] = value[:, 128:256]

    for c in range(RES // 256, ATOMS // 256):
        reduced(c, values_of(c))
    for y in range(CY):
        for i in range(CX // 8):
            grid_ref[pl.ds(y + i * 8 * CY, 8, stride=CY), :] = fo_ref[
                i * 8 : i * 8 + 8, y * NZ : (y + 1) * NZ
            ]
    outputs[0].start()

    occupied = rt_ref[1, 32:40, :]
    value = jnp.where(occupied > 0.5, ao_ref[...], 0.0)
    hi, mid, lo = split3(value)
    wide = (NZ, ARR)
    spread_to = jnp.where(lax.shift_right_logical(iota(wide, 1), 3) == iota(wide, 0), 1.0, 0.0)
    spread_to = spread_to.astype(BF16)
    flat = dot_nn(hi, spread_to) + dot_nn(mid, spread_to) + dot_nn(lo, spread_to)
    keep = (iota((8, ARR), 1) & 7) == iota((8, ARR), 0)
    arr_ref[...] = jnp.sum(jnp.where(keep, flat, 0.0), axis=0, keepdims=True)
    outputs[2].start()

    for c in range(RES // 256):
        reduced(c, values_of(c))
    outputs[1].start()
    for copy in outputs:
        copy.wait()


def hand_out(*refs):
    given, out, held, sems = refs[0:3], refs[3:6], refs[6:9], refs[9]
    reads = [pltpu.make_async_copy(given[n], held[n], sems.at[n]) for n in range(3)]
    writes = [pltpu.make_async_copy(held[n], out[n], sems.at[n + 3]) for n in range(3)]
    for copy in reads:
        copy.start()
    for read, write in zip(reads, writes):
        read.wait()
        write.start()
    for copy in writes:
        copy.wait()


def on_device(rq, rf, rc, count, mq, mf, mc, md, ft, ct):
    nx = lax.axis_size("gx")
    ny = lax.axis_size("gy")
    hbm = pl.BlockSpec(memory_space=pltpu.HBM)
    lanes = YR * NZ
    near = YP * 16
    dma = pltpu.SemaphoreType.DMA
    res, arr, grid = pl.pallas_call(
        functools.partial(kernel, nx, ny),
        out_shape=(
            jax.ShapeDtypeStruct((16, 128), F32),
            jax.ShapeDtypeStruct((1, ARR), F32),
            jax.ShapeDtypeStruct((CX * CY, NZ), F32),
        ),
        in_specs=[hbm] * 10,
        out_specs=(hbm, hbm, hbm),
        scratch_shapes=[
            pltpu.VMEM((16, 128), F32),
            pltpu.VMEM((1, ARR), F32),
            pltpu.VMEM((CX * CY, NZ), F32),
            pltpu.VMEM((16, 128), F32),
            pltpu.VMEM((3, RES), F32),
            pltpu.VMEM((16, 128), jnp.int32),
            pltpu.SMEM((1,), jnp.int32),
            pltpu.VMEM((1, MOV), F32),
            pltpu.VMEM((3, MOV), F32),
            pltpu.VMEM((1, MOV), jnp.int32),
            pltpu.VMEM((1, MOV), jnp.int32),
            pltpu.SMEM((3, TAPS), F32),
            pltpu.SMEM((3, TAPS), F32),
            pltpu.VMEM((8, MOV), F32),
            pltpu.VMEM((128, 128), F32),
            pltpu.VMEM((128, 128), F32),
            pltpu.VMEM((nx + 2, ny, 128), F32),
            pltpu.VMEM((nx, 3, ny, 128), F32),
            pltpu.VMEM((3, 128, 128), F32),
            pltpu.VMEM((5, 16, 128), F32),
            pltpu.VMEM((5, 16, 128), F32),
            pltpu.VMEM((5, 16, 128), F32),
            pltpu.VMEM((ROWS, ATOMS), BF16),
            pltpu.VMEM((near, ATOMS), BF16),
            pltpu.VMEM((near, ATOMS), BF16),
            pltpu.VMEM((XP, ATOMS), F32),
            pltpu.VMEM((CP, ATOMS), F32),
            pltpu.VMEM((2 * NZ, ATOMS), BF16),
            pltpu.VMEM((NZ, ATOMS), BF16),
            pltpu.VMEM((NZ, ATOMS), BF16),
            pltpu.VMEM((ROWS, NZ), F32),
            pltpu.VMEM((near, NZ), F32),
            pltpu.VMEM((near, NZ), F32),
            pltpu.VMEM((256, lanes), BF16),
            pltpu.VMEM((64, 256), BF16),
            pltpu.VMEM((2 * NZ, 2 * NZ), BF16),
            pltpu.VMEM((3 * NZ, 2 * NZ), BF16),
            pltpu.VMEM((XP, lanes), F32),
            pltpu.VMEM((5, CP, NZ), F32),
            pltpu.VMEM((32, FH * NZ), F32),
            pltpu.VMEM((32, FH * NZ), F32),
            pltpu.VMEM((CH, 16, NZ), F32),
            pltpu.VMEM((CH, 16, NZ), F32),
            pltpu.VMEM((2, 40, NZ), F32),
            pltpu.VMEM((40, NZ), F32),
            pltpu.VMEM((40, NZ), F32),
            pltpu.VMEM((XP, 31 * NZ), F32),
            pltpu.VMEM((CP, 22 * NZ), F32),
            pltpu.VMEM((XP, YP * NZ), F32),
            pltpu.VMEM((10, 2 * CP, NZ), F32),
            pltpu.VMEM((ROWS, 2 * NZ), BF16),
            pltpu.VMEM((8, 128), F32),
            dma((10,)),
            dma((3,)),
            dma((ny,)),
            dma((ny,)),
            dma((nx,)),
            dma((nx,)),
            dma((2,)),
            dma((2,)),
            dma((6,)),
            dma((6,)),
        ],
        compiler_params=pltpu.CompilerParams(
            collective_id=0, has_side_effects=True, vmem_limit_bytes=64 << 20
        ),
        name="multilevel",
    )(
        rq.reshape(16, 128),
        rf,
        rc.reshape(16, 128),
        count,
        mq.reshape(1, MOV),
        mf,
        mc.reshape(1, MOV),
        md.reshape(1, MOV),
        ft,
        ct,
    )
    res, arr, grid = pl.pallas_call(
        hand_out,
        out_shape=(
            jax.ShapeDtypeStruct((16, 128), F32),
            jax.ShapeDtypeStruct((1, ARR), F32),
            jax.ShapeDtypeStruct((CX * CY, NZ), F32),
        ),
        in_specs=[hbm] * 3,
        out_specs=(hbm, hbm, hbm),
        scratch_shapes=[
            pltpu.VMEM((16, 128), F32),
            pltpu.VMEM((1, ARR), F32),
            pltpu.VMEM((CX * CY, NZ), F32),
            dma((6,)),
        ],
        name="hand_out",
    )(res, arr, grid)
    return res.reshape(RES), arr, grid.reshape(CX, CY, NZ)


def solution(mesh):
    both = ("gx", "gy")
    return jax.shard_map(
        on_device,
        mesh=mesh,
        in_specs=(
            P(both),
            P(None, both),
            P(both),
            P(both),
            P(both),
            P(None, both),
            P(both),
            P(both, None),
            P(),
            P(),
        ),
        out_specs=(P(both), P(both, None), P("gx", "gy", None)),
        check_vma=False,
    )
```

```python
import functools

import jax
import jax.numpy as jnp
from jax import lax
from jax.experimental import pallas as pl
from jax.experimental.pallas import tpu as pltpu
from jax.sharding import PartitionSpec as P

F32 = jnp.float32
BF16 = jnp.bfloat16
MESH = pl.DeviceIdType.MESH
CX = 32
CY = 16
NZ = 128
TAPS = 13
XP = 40
YR = 19
YP = 20
CP = 24
ROWS = YP * XP
RES = 2048
ARR = 1024
ATOMS = RES + ARR
MOV = 512
FH = 9
CH = 4


def iota(shape, dim):
    return lax.broadcasted_iota(jnp.int32, shape, dim)


def split2(v):
    hi = v.astype(BF16)
    return hi, (v - hi.astype(F32)).astype(BF16)


def split3(v):
    hi = v.astype(BF16)
    rest = v - hi.astype(F32)
    mid = rest.astype(BF16)
    return hi, mid, (rest - mid.astype(F32)).astype(BF16)


def dot_nt(a, b):
    return lax.dot_general(a, b, (((1,), (1,)), ((), ())), preferred_element_type=F32)


def dot_nn(a, b):
    return lax.dot_general(a, b, (((1,), (0,)), ((), ())), preferred_element_type=F32)


def spline(u):
    r = 1.0 - u
    s = u * u
    c = s * u
    return (
        r * r * r * (1.0 / 6.0),
        (3.0 * c - 6.0 * s + 4.0) * (1.0 / 6.0),
        (-3.0 * c + 3.0 * s + 3.0 * u + 1.0) * (1.0 / 6.0),
        c * (1.0 / 6.0),
    )


def pick(rows, at, values):
    out = jnp.zeros(rows.shape, rows.dtype)
    for k in range(4):
        out = jnp.where(rows == at[k], values[k], out)
    return out


def prepare(charge, fracs, cells, x0):
    cell = jnp.maximum(cells - 1.0, 0.0).astype(jnp.int32)
    cx = lax.shift_right_logical(cell, 11) - x0
    cy = lax.shift_right_logical(cell, 7) & 15
    cz = cell & 127
    steps = range(4)
    at_x = [cx + k for k in steps]
    at_y = [cy + k for k in steps]
    at_z = [((cz + k) & 127).astype(F32) for k in steps]
    w_x, w_y, w_z = (spline(frac) for frac in fracs)
    hi = [w.astype(BF16).astype(F32) for w in w_z]
    lo = [w - h for w, h in zip(w_z, hi)]
    return charge, at_x, w_x, at_y, w_y, at_z, hi, lo


def build_group(rows, s, lane0, a_ref, wz_ref, own):
    charge, *lists = rows
    charge = charge[s : s + 1]
    at_x, w_x, at_y, w_y, at_z, hi, lo = ([v[s : s + 1] for v in each] for each in lists)
    lanes = lane_window(lane0, 128)
    xrows = XP if own is not None else 16
    wx = pick(iota((xrows, 128), 0), at_x, w_x)
    wy = pick(iota((CP, 128), 0), at_y, w_y)
    if own is not None:
        own[0][:, lanes] = wx
        own[1][:, lanes] = wy
    z = iota((NZ, 128), 0).astype(BF16)
    at_z, hi, lo = ([v.astype(BF16) for v in each] for each in (at_z, hi, lo))
    wz_ref[0:NZ, lanes] = pick(z, at_z, hi)
    if own is not None:
        wz_ref[NZ : 2 * NZ, lanes] = pick(z, at_z, lo)
    wxq = wx * charge
    for p in range(YP // 2):
        blk = jnp.concatenate(
            [wy[2 * p : 2 * p + 1] * wxq, wy[2 * p + 1 : 2 * p + 2] * wxq], axis=0
        )
        a_ref[p * 2 * xrows : (p + 1) * 2 * xrows, lanes] = blk.astype(BF16)


def lane_window(start, size):
    if isinstance(start, int):
        return slice(start, start + size)
    return pl.ds(pl.multiple_of(start, 128), size)


def spread_chunk(lane0, size, acc_ref, a_ref, wz_ref):
    lanes = lane_window(lane0, size)
    acc_ref[...] += dot_nt(a_ref[:, lanes], wz_ref[0:NZ, lanes])


def tap_sum(t, taps_ref, dim):
    out = jnp.zeros(t.shape, F32)
    for k in range(TAPS):
        out = jnp.where(t == k, taps_ref[dim, k], out)
    return out


def kernel(
    nx,
    ny,
    rq_hbm,
    rf_hbm,
    rc_hbm,
    count_hbm,
    mq_hbm,
    mf_hbm,
    mc_hbm,
    md_hbm,
    ft_hbm,
    ct_hbm,
    res_hbm,
    arr_hbm,
    grid_hbm,
    res_ref,
    arr_ref,
    grid_ref,
    rq_ref,
    rf_ref,
    rc_ref,
    count_ref,
    mq_ref,
    mf_ref,
    mc_ref,
    md_ref,
    ft_ref,
    ct_ref,
    pay_ref,
    snd_ref,
    b1_ref,
    t2_ref,
    r2_ref,
    rt_ref,
    rb_ref,
    rl_ref,
    rr_ref,
    a_ref,
    al_ref,
    ar_ref,
    wx_ref,
    wy_ref,
    wz_ref,
    wl_ref,
    wr_ref,
    acc_ref,
    accl_ref,
    accr_ref,
    xh_ref,
    bx_ref,
    zf_ref,
    zc_ref,
    f_ref,
    c3_ref,
    fl_ref,
    fr_ref,
    cl_ref,
    cr_ref,
    edge_ref,
    el_ref,
    er_ref,
    fin_ref,
    cin_ref,
    fo_ref,
    up_ref,
    hb_ref,
    ao_ref,
    in_sem,
    out_sem,
    s1_sem,
    r1_sem,
    s2_sem,
    r2_sem,
    sx_sem,
    rx_sem,
    sy_sem,
    ry_sem,
):
    gx = lax.axis_index("gx")
    gy = lax.axis_index("gy")

    barrier = pltpu.get_barrier_semaphore()
    for k in range(1, ny):
        pl.semaphore_signal(
            barrier, inc=1, device_id=(gx, lax.rem(gy + k, ny)), device_id_type=MESH
        )
    for k in range(1, nx):
        pl.semaphore_signal(
            barrier, inc=1, device_id=(lax.rem(gx + k, nx), gy), device_id_type=MESH
        )

    inputs = [
        pltpu.make_async_copy(src, dst, in_sem.at[n])
        for n, (src, dst) in enumerate(
            (
                (md_hbm, md_ref),
                (mq_hbm, mq_ref),
                (mf_hbm, mf_ref),
                (mc_hbm, mc_ref),
                (count_hbm, count_ref),
                (rq_hbm, rq_ref),
                (rf_hbm, rf_ref),
                (rc_hbm, rc_ref),
                (ft_hbm, ft_ref),
                (ct_hbm, ct_ref),
            )
        )
    ]
    for copy in inputs:
        copy.start()

    for copy in inputs[:4]:
        copy.wait()

    with jax.named_scope("pack"):
        dest = md_ref[...]
        row_of = (dest & (ny - 1)) * nx + lax.div(dest, ny)
        hot = jnp.where(iota((nx * ny, MOV), 0) == row_of, 1.0, 0.0)
        hot16 = hot.astype(BF16)
        earlier = jnp.where(iota((MOV, MOV), 0) < iota((MOV, MOV), 1), 1.0, 0.0)
        counts = dot_nn(hot16, earlier.astype(BF16))
        slot = jnp.sum(hot * counts, axis=0, keepdims=True)
        pay_ref[0:1, :] = mq_ref[...]
        pay_ref[1:4, :] = mf_ref[...]
        pay_ref[4:5, :] = mc_ref[...].astype(F32) + 1.0
        at_slot = iota((8, MOV), 0).astype(F32) == slot
        spots = jnp.concatenate(
            [jnp.where(at_slot, pay_ref[n : n + 1, :], 0.0) for n in range(5)]
            + [jnp.zeros((24, MOV), F32)],
            axis=0,
        )
        hi, mid, lo = split3(spots)
        packed = dot_nt(hot16, hi) + dot_nt(hot16, mid) + dot_nt(hot16, lo)
        snd_ref[:, 0:64] = packed
        snd_ref[:, 64:128] = jnp.zeros((nx * ny, 64), F32)

    pl.semaphore_wait(barrier, nx + ny - 2)

    def hop1(k):
        to = lax.rem(gy + k, ny)
        return pltpu.make_async_remote_copy(
            src_ref=snd_ref.at[pl.ds(pl.multiple_of(to * nx, nx), nx), :],
            dst_ref=b1_ref.at[pl.ds(pl.multiple_of(gy * nx, nx), nx), :],
            send_sem=s1_sem.at[k],
            recv_sem=r1_sem.at[k],
            device_id=(gx, to),
            device_id_type=MESH,
        )

    for k in far_first(ny):
        hop1(k).start()
    mine = pl.ds(pl.multiple_of(gy * nx, nx), nx)
    b1_ref[mine, :] = snd_ref[mine, :]

    for copy in inputs[4:]:
        copy.wait()
    rb_ref[0] = jnp.where(iota((16, 128), 0) * 128 < count_ref[0], rq_ref[...], 0.0)
    for d in range(3):
        for g in range(RES // 128):
            rb_ref[1 + d, g : g + 1, :] = rf_ref[d : d + 1, g * 128 : (g + 1) * 128]
    rb_ref[4] = rc_ref[...].astype(F32) + 1.0

    def x_copy(n, dst, to):
        return pltpu.make_async_remote_copy(
            src_ref=rb_ref,
            dst_ref=dst,
            send_sem=sx_sem.at[n],
            recv_sem=rx_sem.at[n],
            device_id=(to, gy),
            device_id_type=MESH,
        )

    x_copies = [
        x_copy(0, rl_ref, lax.rem(gx + 1, nx)),
        x_copy(1, rr_ref, lax.rem(gx + nx - 1, nx)),
    ]
    for copy in x_copies:
        copy.start()

    acc_ref[...] = jnp.zeros_like(acc_ref)
    accl_ref[...] = jnp.zeros_like(accl_ref)
    accr_ref[...] = jnp.zeros_like(accr_ref)

    def residents(block, x0, acc, a, wz, own):
        for half in range(2):
            rows = slice(half * 8, half * 8 + 8)
            ready = prepare(
                block[0, rows, :], [block[1 + d, rows, :] for d in range(3)], block[4, rows, :], x0
            )
            for s in range(8):
                build_group(ready, s, half * 1024 + s * 128, a, wz, own)
            spread_chunk(half * 1024, 1024, acc, a, wz)

    residents(rb_ref, 0, acc_ref, a_ref, wz_ref, (wx_ref, wy_ref))

    for k in range(1, ny):
        hop1(k).wait()
    for g in range(nx):
        t2_ref[g + 1] = b1_ref[pl.ds(g, ny, stride=nx), :]
    t2_ref[0] = t2_ref[nx]
    t2_ref[nx + 1] = t2_ref[1]

    def hop2(k):
        to = lax.rem(gx + k, nx)
        return pltpu.make_async_remote_copy(
            src_ref=t2_ref.at[pl.ds(to, 3)],
            dst_ref=r2_ref.at[gx],
            send_sem=s2_sem.at[k],
            recv_sem=r2_sem.at[k],
            device_id=(to, gy),
            device_id_type=MESH,
        )

    for k in far_first(nx):
        hop2(k).start()
    r2_ref[gx] = t2_ref[pl.ds(gx, 3)]

    for copy in x_copies:
        copy.wait()

    residents(rl_ref, 20, accl_ref, al_ref, wl_ref, None)
    residents(rr_ref, 0, accr_ref, ar_ref, wr_ref, None)

    with jax.named_scope("matrices"):
        col = iota((64, 256), 1)
        part = jnp.where(col >= 160, 2, jnp.where(col >= 80, 1, 0))
        base = col - part * 80
        pos = jnp.where(base < 48, base, jnp.where(base < 64, base - 60, base - 32))
        out_x = iota((64, 256), 0)
        fine_t = pos - out_x + 6
        coarse_t = lax.shift_right_arithmetic(pos, 1) - (out_x - XP) + 6
        bx = jnp.where(out_x < XP, tap_sum(fine_t, ft_ref, 0), tap_sum(coarse_t, ct_ref, 0))
        bx_hi = bx.astype(BF16).astype(F32)
        bx = jnp.where(part == 2, bx - bx_hi, bx_hi)
        bx_ref[...] = jnp.where(col < 240, bx, 0.0).astype(BF16)
        t = (iota((NZ, NZ), 0) - iota((NZ, NZ), 1) + 6) & 127
        hi, lo = split2(tap_sum(t, ft_ref, 2))
        zf_ref[0:NZ, 0:NZ] = hi
        zf_ref[NZ : 2 * NZ, 0:NZ] = hi
        zf_ref[0:NZ, NZ : 2 * NZ] = lo
        zf_ref[NZ : 2 * NZ, NZ : 2 * NZ] = jnp.zeros((NZ, NZ), BF16)
        r, c = iota((NZ, 2 * NZ), 0), iota((NZ, 2 * NZ), 1)
        t = ((r & 63) - lax.shift_right_logical(c & 127, 1) + 6) & 63
        zc = tap_sum(t, ct_ref, 2)
        same = lax.shift_right_logical(r, 6) == lax.shift_right_logical(c, 7)
        hi, lo = split2(jnp.where(same, zc, 0.0))
        zc_ref[0:NZ, :] = hi
        zc_ref[NZ : 2 * NZ, :] = hi
        zc_ref[2 * NZ : 3 * NZ, :] = lo

    for k in range(1, nx):
        hop2(k).wait()

    for n in range(3):
        rt_ref[n] = r2_ref[:, n].reshape(nx * ny, 128).T

    boxes = (
        (1, 0, acc_ref, a_ref, wz_ref, (wx_ref, wy_ref)),
        (0, 20, accl_ref, al_ref, wl_ref, None),
        (2, 0, accr_ref, ar_ref, wr_ref, None),
    )
    for n in range(len(boxes) + 1):
        if n < len(boxes):
            side, x0, _, a, wz, own = boxes[n]
            field = [rt_ref[side, f * 8 : f * 8 + 8, :] for f in range(5)]
            ready = prepare(field[0], field[1:4], field[4], x0)
        if n > 0:
            spread_chunk(RES, ARR, *boxes[n - 1][2:5])
        if n < len(boxes):
            for s in range(8):
                build_group(ready, s, RES + s * 128, a, wz, own)

    up_y = lax.rem(gy + 1, ny)
    down_y = lax.rem(gy + ny - 1, ny)
    for y in range(YR):
        lanes = slice(y * NZ, (y + 1) * NZ)
        rows = []
        for ref, count in ((acc_ref, XP), (accl_ref, 16), (accr_ref, 16)):
            part = ref[y * count : (y + 1) * count]
            rows.append(part)
            if count == XP:
                rows.append(jnp.zeros((8, NZ), F32))
        hi, lo = split2(jnp.concatenate(rows, axis=0))
        xh_ref[0:80, lanes] = hi
        xh_ref[80:160, lanes] = lo
        xh_ref[160:240, lanes] = hi
        xh_ref[240:256, lanes] = jnp.zeros((16, NZ), BF16)

    conv = dot_nn(bx_ref[...], xh_ref[...])
    f_ref[...] = conv[0:XP]

    def y_copy(n, src, dst, to):
        return pltpu.make_async_remote_copy(
            src_ref=src,
            dst_ref=dst,
            send_sem=sy_sem.at[n],
            recv_sem=ry_sem.at[n],
            device_id=(gx, to),
            device_id_type=MESH,
        )

    def fine_copy(n, y0, first, count, dst, to):
        return y_copy(
            n,
            f_ref.at[pl.ds(0, 32), pl.ds((y0 + first) * NZ, count * NZ)],
            dst.at[:, pl.ds(first * NZ, count * NZ)],
            to,
        )

    fine_copies = [
        fine_copy(4, 10, 0, 5, fl_ref, up_y),
        fine_copy(5, 0, 0, 5, fr_ref, down_y),
        fine_copy(6, 10, 5, 4, fl_ref, up_y),
        fine_copy(7, 0, 5, 4, fr_ref, down_y),
    ]
    for copy in fine_copies[0:2]:
        copy.start()

    r, c = iota((2 * NZ, NZ), 0), iota((2 * NZ, NZ), 1)
    pair = jnp.where(lax.shift_right_logical(r, 1) == c, 1.0, 0.0).astype(BF16)
    coarse = conv[XP : XP + CP]
    tiles = []
    for m in range(5):
        both = []
        for j in (2 * m, 2 * m + 1):
            row = coarse[:, 2 * j * NZ : (2 * j + 1) * NZ]
            if 2 * j + 1 < YR:
                row = row + coarse[:, (2 * j + 1) * NZ : (2 * j + 2) * NZ]
            both.append(row)
        tiles.append(jnp.concatenate(both, axis=1))
    packed = jnp.concatenate(tiles, axis=0)
    hi, lo = split2(packed)
    packed = dot_nn(hi, pair) + dot_nn(lo, pair)
    for m in range(5):
        c3_ref[m] = packed[m * CP : (m + 1) * CP]

    for n, (y0, m0) in enumerate(((10, 1), (0, 0))):
        for y in range(FH):
            edge_ref[n, 3 * y : 3 * y + 3, :] = f_ref[32:35, (y0 + y) * NZ : (y0 + y + 1) * NZ]
        edge_ref[n, 27:32, :] = jnp.zeros((5, NZ), F32)
        for m in range(CH):
            edge_ref[n, 32 + 2 * m : 34 + 2 * m, :] = c3_ref[m0 + m, 16:18, :]
    half = pl.ds(0, 16)
    y_copies = [
        y_copy(0, edge_ref.at[0], el_ref, up_y),
        y_copy(1, edge_ref.at[1], er_ref, down_y),
        y_copy(2, c3_ref.at[pl.ds(1, CH), half], cl_ref, up_y),
        y_copy(3, c3_ref.at[pl.ds(0, CH), half], cr_ref, down_y),
    ]
    for copy in y_copies + fine_copies[2:4]:
        copy.start()

    def fine_z(block):
        hi, lo = split2(block)
        both = dot_nn(jnp.concatenate([hi, lo], axis=1), zf_ref[...])
        return both[:, 0:NZ] + both[:, NZ : 2 * NZ]

    def coarse_z(block):
        hi, lo = split2(block)
        return dot_nn(jnp.concatenate([hi, lo], axis=1), zc_ref[0 : 2 * NZ, :]) + dot_nn(
            hi, zc_ref[2 * NZ : 3 * NZ, :]
        )

    def stacked(ref, count):
        return jnp.concatenate([ref[:, y * NZ : (y + 1) * NZ] for y in range(count)], axis=0)

    own = fine_z(stacked(f_ref, YR))
    for y in range(YR):
        fin_ref[:, (y + 6) * NZ : (y + 7) * NZ] = own[y * XP : (y + 1) * XP]
    zero = jnp.zeros((XP, 6 * NZ), F32)
    fin_ref[:, 0 : 6 * NZ] = zero
    fin_ref[:, 25 * NZ : 31 * NZ] = zero
    own = coarse_z(jnp.concatenate([c3_ref[m] for m in range(5)], axis=0))
    zero = jnp.zeros((CP, 6 * NZ), F32)
    cin_ref[:, 0 : 6 * NZ] = zero
    cin_ref[:, 16 * NZ : 22 * NZ] = zero
    for m in range(5):
        cin_ref[:, (2 * m + 6) * NZ : (2 * m + 8) * NZ] = own[m * CP : (m + 1) * CP]

    for copy in y_copies:
        copy.wait()
    for ref, edge, at in ((cl_ref, el_ref, 0), (cr_ref, er_ref, 14)):
        halo = coarse_z(jnp.concatenate([ref[m] for m in range(CH)] + [edge[32:40, :]], axis=0))
        for m in range(CH):
            lanes = slice((2 * m + at) * NZ, (2 * m + at + 2) * NZ)
            cin_ref[0:16, lanes] += halo[m * 16 : (m + 1) * 16]
            cin_ref[16:18, lanes] += halo[64 + 2 * m : 66 + 2 * m]

    def coarse_y(i, carry):
        rows = pl.ds(pl.multiple_of(i * 8, 8), 8)
        out = jnp.zeros((8, 10 * NZ), F32)
        for k in range(TAPS):
            out = out + ct_ref[1, k] * cin_ref[rows, k * NZ : (k + 10) * NZ]
        for j in range(10):
            one = out[:, j * NZ : (j + 1) * NZ]
            up_ref[j, pl.ds(i * 16, 8, stride=2), :] = one
            up_ref[j, pl.ds(i * 16 + 1, 8, stride=2), :] = one
        return carry

    lax.fori_loop(0, CP // 8, coarse_y, 0)

    for copy in fine_copies:
        copy.wait()
    for ref, edge, at in ((fl_ref, el_ref, 0), (fr_ref, er_ref, 22)):
        halo = fine_z(jnp.concatenate([stacked(ref, FH), edge[0:32, :]], axis=0))
        for y in range(FH):
            lanes = slice((y + at) * NZ, (y + at + 1) * NZ)
            fin_ref[0:32, lanes] += halo[y * 32 : (y + 1) * 32]
            fin_ref[32:35, lanes] += halo[288 + 3 * y : 291 + 3 * y]

    def fine_y(i, carry):
        rows = pl.ds(pl.multiple_of(i * 8, 8), 8)
        out = jnp.zeros((8, YR * NZ), F32)
        for k in range(TAPS):
            out = out + ft_ref[1, k] * fin_ref[rows, k * NZ : (k + YR) * NZ]
        for y in range(YR):
            fo_ref[rows, y * NZ : (y + 1) * NZ] = (
                out[:, y * NZ : (y + 1) * NZ] + up_ref[y // 2, rows, :]
            )
        fo_ref[rows, YR * NZ : YP * NZ] = jnp.zeros((8, NZ), F32)
        return carry

    lax.fori_loop(0, XP // 8, fine_y, 0)

    for p in range(YP // 2):
        half = jnp.concatenate(
            [fo_ref[:, y * NZ : (y + 1) * NZ] for y in (2 * p, 2 * p + 1)], axis=0
        ).astype(BF16)
        hb_ref[p * 2 * XP : (p + 1) * 2 * XP, 0:NZ] = half
        hb_ref[p * 2 * XP : (p + 1) * 2 * XP, NZ : 2 * NZ] = half

    outputs = [
        pltpu.make_async_copy(grid_ref, grid_hbm, out_sem.at[0]),
        pltpu.make_async_copy(res_ref, res_hbm, out_sem.at[1]),
        pltpu.make_async_copy(arr_ref, arr_hbm, out_sem.at[2]),
    ]

    def values_of(c):
        return dot_nn(hb_ref[...], wz_ref[:, c * 256 : (c + 1) * 256])

    def reduced(c, values):
        lanes = slice(c * 256, (c + 1) * 256)
        wy = wy_ref[:, lanes]
        part = jnp.zeros((XP, 256), F32)
        for y in range(YR):
            part = part + wy[y : y + 1] * values[y * XP : (y + 1) * XP]
        value = jnp.sum(part * wx_ref[:, lanes], axis=0, keepdims=True)
        if c < RES // 256:
            live = iota((1, 256), 1) + c * 256 < count_ref[0]
            value = jnp.where(live, value, 0.0)
            at, ref = 2 * c, res_ref
        else:
            at, ref = 2 * (c - RES // 256), ao_ref
        ref[at : at + 1, :] = value[:, 0:128]
        ref[at + 1 : at + 2, :] = value[:, 128:256]

    for c in range(RES // 256, ATOMS // 256):
        reduced(c, values_of(c))
    for y in range(CY):
        for i in range(CX // 8):
            grid_ref[pl.ds(y + i * 8 * CY, 8, stride=CY), :] = fo_ref[
                i * 8 : i * 8 + 8, y * NZ : (y + 1) * NZ
            ]
    outputs[0].start()

    occupied = rt_ref[1, 32:40, :]
    value = jnp.where(occupied > 0.5, ao_ref[...], 0.0)
    hi, mid, lo = split3(value)
    wide = (NZ, ARR)
    spread_to = jnp.where(lax.shift_right_logical(iota(wide, 1), 3) == iota(wide, 0), 1.0, 0.0)
    spread_to = spread_to.astype(BF16)
    flat = dot_nn(hi, spread_to) + dot_nn(mid, spread_to) + dot_nn(lo, spread_to)
    keep = (iota((8, ARR), 1) & 7) == iota((8, ARR), 0)
    arr_ref[...] = jnp.sum(jnp.where(keep, flat, 0.0), axis=0, keepdims=True)
    outputs[2].start()

    for c in range(RES // 256):
        reduced(c, values_of(c))
    outputs[1].start()
    for copy in outputs:
        copy.wait()


def far_first(count):
    turn = count // 2
    return sorted(range(1, count), key=lambda k: (-min(k % turn, turn - k % turn), -k))


def hand_out(*refs):
    given, out, held, sems = refs[0:3], refs[3:6], refs[6:9], refs[9]
    reads = [pltpu.make_async_copy(given[n], held[n], sems.at[n]) for n in range(3)]
    writes = [pltpu.make_async_copy(held[n], out[n], sems.at[n + 3]) for n in range(3)]
    for copy in reads:
        copy.start()
    for read, write in zip(reads, writes):
        read.wait()
        write.start()
    for copy in writes:
        copy.wait()


def on_device(rq, rf, rc, count, mq, mf, mc, md, ft, ct):
    nx = lax.axis_size("gx")
    ny = lax.axis_size("gy")
    hbm = pl.BlockSpec(memory_space=pltpu.HBM)
    lanes = YR * NZ
    near = YP * 16
    dma = pltpu.SemaphoreType.DMA
    res, arr, grid = pl.pallas_call(
        functools.partial(kernel, nx, ny),
        out_shape=(
            jax.ShapeDtypeStruct((16, 128), F32),
            jax.ShapeDtypeStruct((1, ARR), F32),
            jax.ShapeDtypeStruct((CX * CY, NZ), F32),
        ),
        in_specs=[hbm] * 10,
        out_specs=(hbm, hbm, hbm),
        scratch_shapes=[
            pltpu.VMEM((16, 128), F32),
            pltpu.VMEM((1, ARR), F32),
            pltpu.VMEM((CX * CY, NZ), F32),
            pltpu.VMEM((16, 128), F32),
            pltpu.VMEM((3, RES), F32),
            pltpu.VMEM((16, 128), jnp.int32),
            pltpu.SMEM((1,), jnp.int32),
            pltpu.VMEM((1, MOV), F32),
            pltpu.VMEM((3, MOV), F32),
            pltpu.VMEM((1, MOV), jnp.int32),
            pltpu.VMEM((1, MOV), jnp.int32),
            pltpu.SMEM((3, TAPS), F32),
            pltpu.SMEM((3, TAPS), F32),
            pltpu.VMEM((8, MOV), F32),
            pltpu.VMEM((128, 128), F32),
            pltpu.VMEM((128, 128), F32),
            pltpu.VMEM((nx + 2, ny, 128), F32),
            pltpu.VMEM((nx, 3, ny, 128), F32),
            pltpu.VMEM((3, 128, 128), F32),
            pltpu.VMEM((5, 16, 128), F32),
            pltpu.VMEM((5, 16, 128), F32),
            pltpu.VMEM((5, 16, 128), F32),
            pltpu.VMEM((ROWS, ATOMS), BF16),
            pltpu.VMEM((near, ATOMS), BF16),
            pltpu.VMEM((near, ATOMS), BF16),
            pltpu.VMEM((XP, ATOMS), F32),
            pltpu.VMEM((CP, ATOMS), F32),
            pltpu.VMEM((2 * NZ, ATOMS), BF16),
            pltpu.VMEM((NZ, ATOMS), BF16),
            pltpu.VMEM((NZ, ATOMS), BF16),
            pltpu.VMEM((ROWS, NZ), F32),
            pltpu.VMEM((near, NZ), F32),
            pltpu.VMEM((near, NZ), F32),
            pltpu.VMEM((256, lanes), BF16),
            pltpu.VMEM((64, 256), BF16),
            pltpu.VMEM((2 * NZ, 2 * NZ), BF16),
            pltpu.VMEM((3 * NZ, 2 * NZ), BF16),
            pltpu.VMEM((XP, lanes), F32),
            pltpu.VMEM((5, CP, NZ), F32),
            pltpu.VMEM((32, FH * NZ), F32),
            pltpu.VMEM((32, FH * NZ), F32),
            pltpu.VMEM((CH, 16, NZ), F32),
            pltpu.VMEM((CH, 16, NZ), F32),
            pltpu.VMEM((2, 40, NZ), F32),
            pltpu.VMEM((40, NZ), F32),
            pltpu.VMEM((40, NZ), F32),
            pltpu.VMEM((XP, 31 * NZ), F32),
            pltpu.VMEM((CP, 22 * NZ), F32),
            pltpu.VMEM((XP, YP * NZ), F32),
            pltpu.VMEM((10, 2 * CP, NZ), F32),
            pltpu.VMEM((ROWS, 2 * NZ), BF16),
            pltpu.VMEM((8, 128), F32),
            dma((10,)),
            dma((3,)),
            dma((ny,)),
            dma((ny,)),
            dma((nx,)),
            dma((nx,)),
            dma((2,)),
            dma((2,)),
            dma((8,)),
            dma((8,)),
        ],
        compiler_params=pltpu.CompilerParams(
            collective_id=0, has_side_effects=True, vmem_limit_bytes=64 << 20
        ),
        name="multilevel",
    )(
        rq.reshape(16, 128),
        rf,
        rc.reshape(16, 128),
        count,
        mq.reshape(1, MOV),
        mf,
        mc.reshape(1, MOV),
        md.reshape(1, MOV),
        ft,
        ct,
    )
    res, arr, grid = pl.pallas_call(
        hand_out,
        out_shape=(
            jax.ShapeDtypeStruct((16, 128), F32),
            jax.ShapeDtypeStruct((1, ARR), F32),
            jax.ShapeDtypeStruct((CX * CY, NZ), F32),
        ),
        in_specs=[hbm] * 3,
        out_specs=(hbm, hbm, hbm),
        scratch_shapes=[
            pltpu.VMEM((16, 128), F32),
            pltpu.VMEM((1, ARR), F32),
            pltpu.VMEM((CX * CY, NZ), F32),
            dma((6,)),
        ],
        name="hand_out",
    )(res, arr, grid)
    return res.reshape(RES), arr, grid.reshape(CX, CY, NZ)


def solution(mesh):
    both = ("gx", "gy")
    return jax.shard_map(
        on_device,
        mesh=mesh,
        in_specs=(
            P(both),
            P(None, both),
            P(both),
            P(both),
            P(both),
            P(None, both),
            P(both),
            P(both, None),
            P(),
            P(),
        ),
        out_specs=(P(both), P(both, None), P("gx", "gy", None)),
        check_vma=False,
    )
```

```python
import functools

import jax
import jax.numpy as jnp
from jax import lax
from jax.experimental import pallas as pl
from jax.experimental.pallas import tpu as pltpu
from jax.sharding import PartitionSpec as P

F32 = jnp.float32
BF16 = jnp.bfloat16
MESH = pl.DeviceIdType.MESH
CX = 32
CY = 16
NZ = 128
TAPS = 13
XP = 40
YR = 19
YP = 20
CP = 24
ROWS = YP * XP
RES = 2048
ARR = 1024
ATOMS = RES + ARR
MOV = 512
FH = 9
CH = 4


def iota(shape, dim):
    return lax.broadcasted_iota(jnp.int32, shape, dim)


def split2(v):
    hi = v.astype(BF16)
    return hi, (v - hi.astype(F32)).astype(BF16)


def split3(v):
    hi = v.astype(BF16)
    rest = v - hi.astype(F32)
    mid = rest.astype(BF16)
    return hi, mid, (rest - mid.astype(F32)).astype(BF16)


def dot_nt(a, b):
    return lax.dot_general(a, b, (((1,), (1,)), ((), ())), preferred_element_type=F32)


def dot_nn(a, b):
    return lax.dot_general(a, b, (((1,), (0,)), ((), ())), preferred_element_type=F32)


def spline(u):
    r = 1.0 - u
    s = u * u
    c = s * u
    return (
        r * r * r * (1.0 / 6.0),
        (3.0 * c - 6.0 * s + 4.0) * (1.0 / 6.0),
        (-3.0 * c + 3.0 * s + 3.0 * u + 1.0) * (1.0 / 6.0),
        c * (1.0 / 6.0),
    )


def pick(rows, at, values):
    out = jnp.zeros(rows.shape, rows.dtype)
    for k in range(4):
        out = jnp.where(rows == at[k], values[k], out)
    return out


def prepare(charge, fracs, cells, x0):
    cell = jnp.maximum(cells - 1.0, 0.0).astype(jnp.int32)
    cx = lax.shift_right_logical(cell, 11) - x0
    cy = lax.shift_right_logical(cell, 7) & 15
    cz = cell & 127
    steps = range(4)
    at_x = [cx + k for k in steps]
    at_y = [cy + k for k in steps]
    at_z = [((cz + k) & 127).astype(F32) for k in steps]
    w_x, w_y, w_z = (spline(frac) for frac in fracs)
    hi = [w.astype(BF16).astype(F32) for w in w_z]
    lo = [w - h for w, h in zip(w_z, hi)]
    return charge, at_x, w_x, at_y, w_y, at_z, hi, lo


def build_group(rows, s, lane0, a_ref, wz_ref, own):
    charge, *lists = rows
    charge = charge[s : s + 1]
    at_x, w_x, at_y, w_y, at_z, hi, lo = ([v[s : s + 1] for v in each] for each in lists)
    lanes = lane_window(lane0, 128)
    xrows = XP if own is not None else 16
    wx = pick(iota((xrows, 128), 0), at_x, w_x)
    wy = pick(iota((CP, 128), 0), at_y, w_y)
    if own is not None:
        own[0][:, lanes] = wx
        own[1][:, lanes] = wy
    z = iota((NZ, 128), 0).astype(BF16)
    at_z, hi, lo = ([v.astype(BF16) for v in each] for each in (at_z, hi, lo))
    wz_ref[0:NZ, lanes] = pick(z, at_z, hi)
    if own is not None:
        wz_ref[NZ : 2 * NZ, lanes] = pick(z, at_z, lo)
    wxq = wx * charge
    for p in range(YP // 2):
        blk = jnp.concatenate(
            [wy[2 * p : 2 * p + 1] * wxq, wy[2 * p + 1 : 2 * p + 2] * wxq], axis=0
        )
        a_ref[p * 2 * xrows : (p + 1) * 2 * xrows, lanes] = blk.astype(BF16)


def lane_window(start, size):
    if isinstance(start, int):
        return slice(start, start + size)
    return pl.ds(pl.multiple_of(start, 128), size)


def spread_chunk(lane0, size, acc_ref, a_ref, wz_ref):
    lanes = lane_window(lane0, size)
    acc_ref[...] += dot_nt(a_ref[:, lanes], wz_ref[0:NZ, lanes])


def tap_sum(t, taps_ref, dim):
    out = jnp.zeros(t.shape, F32)
    for k in range(TAPS):
        out = jnp.where(t == k, taps_ref[dim, k], out)
    return out


def kernel(
    nx,
    ny,
    rq_hbm,
    rf_hbm,
    rc_hbm,
    count_hbm,
    mq_hbm,
    mf_hbm,
    mc_hbm,
    md_hbm,
    ft_hbm,
    ct_hbm,
    res_hbm,
    arr_hbm,
    grid_hbm,
    res_ref,
    arr_ref,
    grid_ref,
    rq_ref,
    rf_ref,
    rc_ref,
    count_ref,
    mq_ref,
    mf_ref,
    mc_ref,
    md_ref,
    ft_ref,
    ct_ref,
    pay_ref,
    snd_ref,
    b1_ref,
    t2_ref,
    r2_ref,
    rt_ref,
    rb_ref,
    rl_ref,
    rr_ref,
    a_ref,
    al_ref,
    ar_ref,
    wx_ref,
    wy_ref,
    wz_ref,
    wl_ref,
    wr_ref,
    acc_ref,
    accl_ref,
    accr_ref,
    xh_ref,
    bx_ref,
    zf_ref,
    zc_ref,
    f_ref,
    co_ref,
    c3_ref,
    fl_ref,
    fr_ref,
    cl_ref,
    cr_ref,
    edge_ref,
    el_ref,
    er_ref,
    fin_ref,
    cin_ref,
    fo_ref,
    up_ref,
    hb_ref,
    ao_ref,
    in_sem,
    out_sem,
    s1_sem,
    r1_sem,
    s2_sem,
    r2_sem,
    sx_sem,
    rx_sem,
    sy_sem,
    ry_sem,
):
    gx = lax.axis_index("gx")
    gy = lax.axis_index("gy")

    barrier = pltpu.get_barrier_semaphore()
    for k in range(1, ny):
        pl.semaphore_signal(
            barrier, inc=1, device_id=(gx, lax.rem(gy + k, ny)), device_id_type=MESH
        )
    for k in range(1, nx):
        pl.semaphore_signal(
            barrier, inc=1, device_id=(lax.rem(gx + k, nx), gy), device_id_type=MESH
        )

    inputs = [
        pltpu.make_async_copy(src, dst, in_sem.at[n])
        for n, (src, dst) in enumerate(
            (
                (md_hbm, md_ref),
                (mq_hbm, mq_ref),
                (mf_hbm, mf_ref),
                (mc_hbm, mc_ref),
                (count_hbm, count_ref),
                (rq_hbm, rq_ref),
                (rf_hbm, rf_ref),
                (rc_hbm, rc_ref),
                (ft_hbm, ft_ref),
                (ct_hbm, ct_ref),
            )
        )
    ]
    for copy in inputs:
        copy.start()

    for copy in inputs[:4]:
        copy.wait()

    with jax.named_scope("pack"):
        dest = md_ref[...]
        row_of = (dest & (ny - 1)) * nx + lax.div(dest, ny)
        hot = jnp.where(iota((nx * ny, MOV), 0) == row_of, 1.0, 0.0)
        hot16 = hot.astype(BF16)
        earlier = jnp.where(iota((MOV, MOV), 0) < iota((MOV, MOV), 1), 1.0, 0.0)
        counts = dot_nn(hot16, earlier.astype(BF16))
        slot = jnp.sum(hot * counts, axis=0, keepdims=True)
        pay_ref[0:1, :] = mq_ref[...]
        pay_ref[1:4, :] = mf_ref[...]
        pay_ref[4:5, :] = mc_ref[...].astype(F32) + 1.0
        at_slot = iota((8, MOV), 0).astype(F32) == slot
        spots = jnp.concatenate(
            [jnp.where(at_slot, pay_ref[n : n + 1, :], 0.0) for n in range(5)]
            + [jnp.zeros((24, MOV), F32)],
            axis=0,
        )
        hi, mid, lo = split3(spots)
        packed = dot_nt(hot16, hi) + dot_nt(hot16, mid) + dot_nt(hot16, lo)
        snd_ref[:, 0:64] = packed
        snd_ref[:, 64:128] = jnp.zeros((nx * ny, 64), F32)

    pl.semaphore_wait(barrier, nx + ny - 2)

    def hop1(k):
        to = lax.rem(gy + k, ny)
        return pltpu.make_async_remote_copy(
            src_ref=snd_ref.at[pl.ds(pl.multiple_of(to * nx, nx), nx), :],
            dst_ref=b1_ref.at[pl.ds(pl.multiple_of(gy * nx, nx), nx), :],
            send_sem=s1_sem.at[k],
            recv_sem=r1_sem.at[k],
            device_id=(gx, to),
            device_id_type=MESH,
        )

    for k in far_first(ny):
        hop1(k).start()
    mine = pl.ds(pl.multiple_of(gy * nx, nx), nx)
    b1_ref[mine, :] = snd_ref[mine, :]

    for copy in inputs[4:]:
        copy.wait()
    rb_ref[0] = jnp.where(iota((16, 128), 0) * 128 < count_ref[0], rq_ref[...], 0.0)
    for d in range(3):
        for g in range(RES // 128):
            rb_ref[1 + d, g : g + 1, :] = rf_ref[d : d + 1, g * 128 : (g + 1) * 128]
    rb_ref[4] = rc_ref[...].astype(F32) + 1.0

    def x_copy(n, dst, to):
        return pltpu.make_async_remote_copy(
            src_ref=rb_ref,
            dst_ref=dst,
            send_sem=sx_sem.at[n],
            recv_sem=rx_sem.at[n],
            device_id=(to, gy),
            device_id_type=MESH,
        )

    x_copies = [
        x_copy(0, rl_ref, lax.rem(gx + 1, nx)),
        x_copy(1, rr_ref, lax.rem(gx + nx - 1, nx)),
    ]
    for copy in x_copies:
        copy.start()

    acc_ref[...] = jnp.zeros_like(acc_ref)
    accl_ref[...] = jnp.zeros_like(accl_ref)
    accr_ref[...] = jnp.zeros_like(accr_ref)

    def residents(block, x0, acc, a, wz, own):
        for half in range(2):
            rows = slice(half * 8, half * 8 + 8)
            ready = prepare(
                block[0, rows, :], [block[1 + d, rows, :] for d in range(3)], block[4, rows, :], x0
            )
            for s in range(8):
                build_group(ready, s, half * 1024 + s * 128, a, wz, own)
            spread_chunk(half * 1024, 1024, acc, a, wz)

    residents(rb_ref, 0, acc_ref, a_ref, wz_ref, (wx_ref, wy_ref))

    for k in range(1, ny):
        hop1(k).wait()
    for g in range(nx):
        t2_ref[g + 1] = b1_ref[pl.ds(g, ny, stride=nx), :]
    t2_ref[0] = t2_ref[nx]
    t2_ref[nx + 1] = t2_ref[1]

    def hop2(k):
        to = lax.rem(gx + k, nx)
        return pltpu.make_async_remote_copy(
            src_ref=t2_ref.at[pl.ds(to, 3)],
            dst_ref=r2_ref.at[gx],
            send_sem=s2_sem.at[k],
            recv_sem=r2_sem.at[k],
            device_id=(to, gy),
            device_id_type=MESH,
        )

    for k in far_first(nx):
        hop2(k).start()
    r2_ref[gx] = t2_ref[pl.ds(gx, 3)]

    for copy in x_copies:
        copy.wait()

    residents(rl_ref, 20, accl_ref, al_ref, wl_ref, None)
    residents(rr_ref, 0, accr_ref, ar_ref, wr_ref, None)

    with jax.named_scope("matrices"):
        col = iota((64, 256), 1)
        part = jnp.where(col >= 160, 2, jnp.where(col >= 80, 1, 0))
        base = col - part * 80
        pos = jnp.where(base < 48, base, jnp.where(base < 64, base - 60, base - 32))
        out_x = iota((64, 256), 0)
        fine_t = pos - out_x + 6
        coarse_t = lax.shift_right_arithmetic(pos, 1) - (out_x - XP) + 6
        bx = jnp.where(out_x < XP, tap_sum(fine_t, ft_ref, 0), tap_sum(coarse_t, ct_ref, 0))
        bx_hi = bx.astype(BF16).astype(F32)
        bx = jnp.where(part == 2, bx - bx_hi, bx_hi)
        bx_ref[...] = jnp.where(col < 240, bx, 0.0).astype(BF16)
        t = (iota((NZ, NZ), 0) - iota((NZ, NZ), 1) + 6) & 127
        hi, lo = split2(tap_sum(t, ft_ref, 2))
        zf_ref[0:NZ, 0:NZ] = hi
        zf_ref[NZ : 2 * NZ, 0:NZ] = hi
        zf_ref[0:NZ, NZ : 2 * NZ] = lo
        zf_ref[NZ : 2 * NZ, NZ : 2 * NZ] = jnp.zeros((NZ, NZ), BF16)
        r, c = iota((NZ, 2 * NZ), 0), iota((NZ, 2 * NZ), 1)
        t = ((r & 63) - lax.shift_right_logical(c & 127, 1) + 6) & 63
        zc = tap_sum(t, ct_ref, 2)
        same = lax.shift_right_logical(r, 6) == lax.shift_right_logical(c, 7)
        hi, lo = split2(jnp.where(same, zc, 0.0))
        zc_ref[0:NZ, :] = hi
        zc_ref[NZ : 2 * NZ, :] = hi
        zc_ref[2 * NZ : 3 * NZ, :] = lo

    for k in range(1, nx):
        hop2(k).wait()

    for n in range(3):
        rt_ref[n] = r2_ref[:, n].reshape(nx * ny, 128).T

    boxes = (
        (1, 0, acc_ref, a_ref, wz_ref, (wx_ref, wy_ref)),
        (0, 20, accl_ref, al_ref, wl_ref, None),
        (2, 0, accr_ref, ar_ref, wr_ref, None),
    )
    for n in range(len(boxes) + 1):
        if n < len(boxes):
            side, x0, _, a, wz, own = boxes[n]
            field = [rt_ref[side, f * 8 : f * 8 + 8, :] for f in range(5)]
            ready = prepare(field[0], field[1:4], field[4], x0)
        if n > 0:
            spread_chunk(RES, ARR, *boxes[n - 1][2:5])
        if n < len(boxes):
            for s in range(8):
                build_group(ready, s, RES + s * 128, a, wz, own)

    up_y = lax.rem(gy + 1, ny)
    down_y = lax.rem(gy + ny - 1, ny)
    def x_pass(y0, y1):
        for y in range(y0, y1):
            lanes = slice(y * NZ, (y + 1) * NZ)
            rows = []
            for ref, count in ((acc_ref, XP), (accl_ref, 16), (accr_ref, 16)):
                rows.append(ref[y * count : (y + 1) * count])
                if count == XP:
                    rows.append(jnp.zeros((8, NZ), F32))
            hi, lo = split2(jnp.concatenate(rows, axis=0))
            xh_ref[0:80, lanes] = hi
            xh_ref[80:160, lanes] = lo
            xh_ref[160:240, lanes] = hi
            xh_ref[240:256, lanes] = jnp.zeros((16, NZ), BF16)
        lanes = slice(y0 * NZ, y1 * NZ)
        conv = dot_nn(bx_ref[...], xh_ref[:, lanes])
        f_ref[:, lanes] = conv[0:XP]
        co_ref[:, lanes] = conv[XP : XP + CP]

    def y_copy(n, src, dst, to):
        return pltpu.make_async_remote_copy(
            src_ref=src,
            dst_ref=dst,
            send_sem=sy_sem.at[n],
            recv_sem=ry_sem.at[n],
            device_id=(gx, to),
            device_id_type=MESH,
        )

    def fine_copy(n, y0, first, count, dst, to):
        return y_copy(
            n,
            f_ref.at[pl.ds(0, 32), pl.ds((y0 + first) * NZ, count * NZ)],
            dst.at[:, pl.ds(first * NZ, count * NZ)],
            to,
        )

    fine_copies = [
        fine_copy(4, 10, 0, 5, fl_ref, up_y),
        fine_copy(5, 0, 0, 5, fr_ref, down_y),
        fine_copy(6, 10, 5, 4, fl_ref, up_y),
        fine_copy(7, 0, 5, 4, fr_ref, down_y),
    ]
    x_pass(10, 15)
    fine_copies[0].start()
    x_pass(0, 5)
    fine_copies[1].start()
    x_pass(15, 19)
    x_pass(5, 10)

    r, c = iota((2 * NZ, NZ), 0), iota((2 * NZ, NZ), 1)
    pair = jnp.where(lax.shift_right_logical(r, 1) == c, 1.0, 0.0).astype(BF16)
    coarse = co_ref[...]
    tiles = []
    for m in range(5):
        both = []
        for j in (2 * m, 2 * m + 1):
            row = coarse[:, 2 * j * NZ : (2 * j + 1) * NZ]
            if 2 * j + 1 < YR:
                row = row + coarse[:, (2 * j + 1) * NZ : (2 * j + 2) * NZ]
            both.append(row)
        tiles.append(jnp.concatenate(both, axis=1))
    packed = jnp.concatenate(tiles, axis=0)
    hi, lo = split2(packed)
    packed = dot_nn(hi, pair) + dot_nn(lo, pair)
    for m in range(5):
        c3_ref[m] = packed[m * CP : (m + 1) * CP]

    for n, (y0, m0) in enumerate(((10, 1), (0, 0))):
        for y in range(FH):
            edge_ref[n, 3 * y : 3 * y + 3, :] = f_ref[32:35, (y0 + y) * NZ : (y0 + y + 1) * NZ]
        edge_ref[n, 27:32, :] = jnp.zeros((5, NZ), F32)
        for m in range(CH):
            edge_ref[n, 32 + 2 * m : 34 + 2 * m, :] = c3_ref[m0 + m, 16:18, :]
    half = pl.ds(0, 16)
    y_copies = [
        y_copy(0, edge_ref.at[0], el_ref, up_y),
        y_copy(1, edge_ref.at[1], er_ref, down_y),
        y_copy(2, c3_ref.at[pl.ds(1, CH), half], cl_ref, up_y),
        y_copy(3, c3_ref.at[pl.ds(0, CH), half], cr_ref, down_y),
    ]
    for copy in y_copies + fine_copies[2:4]:
        copy.start()

    def fine_z(block):
        hi, lo = split2(block)
        both = dot_nn(jnp.concatenate([hi, lo], axis=1), zf_ref[...])
        return both[:, 0:NZ] + both[:, NZ : 2 * NZ]

    def coarse_z(block):
        hi, lo = split2(block)
        return dot_nn(jnp.concatenate([hi, lo], axis=1), zc_ref[0 : 2 * NZ, :]) + dot_nn(
            hi, zc_ref[2 * NZ : 3 * NZ, :]
        )

    def stacked(ref, count):
        return jnp.concatenate([ref[:, y * NZ : (y + 1) * NZ] for y in range(count)], axis=0)

    own = fine_z(stacked(f_ref, YR))
    for y in range(YR):
        fin_ref[:, (y + 6) * NZ : (y + 7) * NZ] = own[y * XP : (y + 1) * XP]
    zero = jnp.zeros((XP, 6 * NZ), F32)
    fin_ref[:, 0 : 6 * NZ] = zero
    fin_ref[:, 25 * NZ : 31 * NZ] = zero
    own = coarse_z(jnp.concatenate([c3_ref[m] for m in range(5)], axis=0))
    zero = jnp.zeros((CP, 6 * NZ), F32)
    cin_ref[:, 0 : 6 * NZ] = zero
    cin_ref[:, 16 * NZ : 22 * NZ] = zero
    for m in range(5):
        cin_ref[:, (2 * m + 6) * NZ : (2 * m + 8) * NZ] = own[m * CP : (m + 1) * CP]

    for copy in y_copies:
        copy.wait()
    for ref, edge, at in ((cl_ref, el_ref, 0), (cr_ref, er_ref, 14)):
        halo = coarse_z(jnp.concatenate([ref[m] for m in range(CH)] + [edge[32:40, :]], axis=0))
        for m in range(CH):
            lanes = slice((2 * m + at) * NZ, (2 * m + at + 2) * NZ)
            cin_ref[0:16, lanes] += halo[m * 16 : (m + 1) * 16]
            cin_ref[16:18, lanes] += halo[64 + 2 * m : 66 + 2 * m]

    def coarse_y(i, carry):
        rows = pl.ds(pl.multiple_of(i * 8, 8), 8)
        out = jnp.zeros((8, 10 * NZ), F32)
        for k in range(TAPS):
            out = out + ct_ref[1, k] * cin_ref[rows, k * NZ : (k + 10) * NZ]
        for j in range(10):
            one = out[:, j * NZ : (j + 1) * NZ]
            up_ref[j, pl.ds(i * 16, 8, stride=2), :] = one
            up_ref[j, pl.ds(i * 16 + 1, 8, stride=2), :] = one
        return carry

    lax.fori_loop(0, CP // 8, coarse_y, 0)

    for copy in fine_copies:
        copy.wait()
    for ref, edge, at in ((fl_ref, el_ref, 0), (fr_ref, er_ref, 22)):
        halo = fine_z(jnp.concatenate([stacked(ref, FH), edge[0:32, :]], axis=0))
        for y in range(FH):
            lanes = slice((y + at) * NZ, (y + at + 1) * NZ)
            fin_ref[0:32, lanes] += halo[y * 32 : (y + 1) * 32]
            fin_ref[32:35, lanes] += halo[288 + 3 * y : 291 + 3 * y]

    def fine_y(i, carry):
        rows = pl.ds(pl.multiple_of(i * 8, 8), 8)
        out = jnp.zeros((8, YR * NZ), F32)
        for k in range(TAPS):
            out = out + ft_ref[1, k] * fin_ref[rows, k * NZ : (k + YR) * NZ]
        for y in range(YR):
            fo_ref[rows, y * NZ : (y + 1) * NZ] = (
                out[:, y * NZ : (y + 1) * NZ] + up_ref[y // 2, rows, :]
            )
        fo_ref[rows, YR * NZ : YP * NZ] = jnp.zeros((8, NZ), F32)
        return carry

    lax.fori_loop(0, XP // 8, fine_y, 0)

    for p in range(YP // 2):
        half = jnp.concatenate(
            [fo_ref[:, y * NZ : (y + 1) * NZ] for y in (2 * p, 2 * p + 1)], axis=0
        ).astype(BF16)
        hb_ref[p * 2 * XP : (p + 1) * 2 * XP, 0:NZ] = half
        hb_ref[p * 2 * XP : (p + 1) * 2 * XP, NZ : 2 * NZ] = half

    outputs = [
        pltpu.make_async_copy(grid_ref, grid_hbm, out_sem.at[0]),
        pltpu.make_async_copy(res_ref, res_hbm, out_sem.at[1]),
        pltpu.make_async_copy(arr_ref, arr_hbm, out_sem.at[2]),
    ]

    def values_of(c):
        return dot_nn(hb_ref[...], wz_ref[:, c * 256 : (c + 1) * 256])

    def reduced(c, values):
        lanes = slice(c * 256, (c + 1) * 256)
        wy = wy_ref[:, lanes]
        part = jnp.zeros((XP, 256), F32)
        for y in range(YR):
            part = part + wy[y : y + 1] * values[y * XP : (y + 1) * XP]
        value = jnp.sum(part * wx_ref[:, lanes], axis=0, keepdims=True)
        if c < RES // 256:
            live = iota((1, 256), 1) + c * 256 < count_ref[0]
            value = jnp.where(live, value, 0.0)
            at, ref = 2 * c, res_ref
        else:
            at, ref = 2 * (c - RES // 256), ao_ref
        ref[at : at + 1, :] = value[:, 0:128]
        ref[at + 1 : at + 2, :] = value[:, 128:256]

    for c in range(RES // 256, ATOMS // 256):
        reduced(c, values_of(c))
    for y in range(CY):
        for i in range(CX // 8):
            grid_ref[pl.ds(y + i * 8 * CY, 8, stride=CY), :] = fo_ref[
                i * 8 : i * 8 + 8, y * NZ : (y + 1) * NZ
            ]
    outputs[0].start()

    occupied = rt_ref[1, 32:40, :]
    value = jnp.where(occupied > 0.5, ao_ref[...], 0.0)
    hi, mid, lo = split3(value)
    wide = (NZ, ARR)
    spread_to = jnp.where(lax.shift_right_logical(iota(wide, 1), 3) == iota(wide, 0), 1.0, 0.0)
    spread_to = spread_to.astype(BF16)
    flat = dot_nn(hi, spread_to) + dot_nn(mid, spread_to) + dot_nn(lo, spread_to)
    keep = (iota((8, ARR), 1) & 7) == iota((8, ARR), 0)
    arr_ref[...] = jnp.sum(jnp.where(keep, flat, 0.0), axis=0, keepdims=True)
    outputs[2].start()

    for c in range(RES // 256):
        reduced(c, values_of(c))
    outputs[1].start()
    for copy in outputs:
        copy.wait()


def far_first(count):
    turn = count // 2
    return sorted(range(1, count), key=lambda k: (-min(k % turn, turn - k % turn), -k))


def hand_out(*refs):
    given, out, held, sems = refs[0:3], refs[3:6], refs[6:9], refs[9]
    reads = [pltpu.make_async_copy(given[n], held[n], sems.at[n]) for n in range(3)]
    writes = [pltpu.make_async_copy(held[n], out[n], sems.at[n + 3]) for n in range(3)]
    for copy in reads:
        copy.start()
    for read, write in zip(reads, writes):
        read.wait()
        write.start()
    for copy in writes:
        copy.wait()


def on_device(rq, rf, rc, count, mq, mf, mc, md, ft, ct):
    nx = lax.axis_size("gx")
    ny = lax.axis_size("gy")
    hbm = pl.BlockSpec(memory_space=pltpu.HBM)
    lanes = YR * NZ
    near = YP * 16
    dma = pltpu.SemaphoreType.DMA
    res, arr, grid = pl.pallas_call(
        functools.partial(kernel, nx, ny),
        out_shape=(
            jax.ShapeDtypeStruct((16, 128), F32),
            jax.ShapeDtypeStruct((1, ARR), F32),
            jax.ShapeDtypeStruct((CX * CY, NZ), F32),
        ),
        in_specs=[hbm] * 10,
        out_specs=(hbm, hbm, hbm),
        scratch_shapes=[
            pltpu.VMEM((16, 128), F32),
            pltpu.VMEM((1, ARR), F32),
            pltpu.VMEM((CX * CY, NZ), F32),
            pltpu.VMEM((16, 128), F32),
            pltpu.VMEM((3, RES), F32),
            pltpu.VMEM((16, 128), jnp.int32),
            pltpu.SMEM((1,), jnp.int32),
            pltpu.VMEM((1, MOV), F32),
            pltpu.VMEM((3, MOV), F32),
            pltpu.VMEM((1, MOV), jnp.int32),
            pltpu.VMEM((1, MOV), jnp.int32),
            pltpu.SMEM((3, TAPS), F32),
            pltpu.SMEM((3, TAPS), F32),
            pltpu.VMEM((8, MOV), F32),
            pltpu.VMEM((128, 128), F32),
            pltpu.VMEM((128, 128), F32),
            pltpu.VMEM((nx + 2, ny, 128), F32),
            pltpu.VMEM((nx, 3, ny, 128), F32),
            pltpu.VMEM((3, 128, 128), F32),
            pltpu.VMEM((5, 16, 128), F32),
            pltpu.VMEM((5, 16, 128), F32),
            pltpu.VMEM((5, 16, 128), F32),
            pltpu.VMEM((ROWS, ATOMS), BF16),
            pltpu.VMEM((near, ATOMS), BF16),
            pltpu.VMEM((near, ATOMS), BF16),
            pltpu.VMEM((XP, ATOMS), F32),
            pltpu.VMEM((CP, ATOMS), F32),
            pltpu.VMEM((2 * NZ, ATOMS), BF16),
            pltpu.VMEM((NZ, ATOMS), BF16),
            pltpu.VMEM((NZ, ATOMS), BF16),
            pltpu.VMEM((ROWS, NZ), F32),
            pltpu.VMEM((near, NZ), F32),
            pltpu.VMEM((near, NZ), F32),
            pltpu.VMEM((256, lanes), BF16),
            pltpu.VMEM((64, 256), BF16),
            pltpu.VMEM((2 * NZ, 2 * NZ), BF16),
            pltpu.VMEM((3 * NZ, 2 * NZ), BF16),
            pltpu.VMEM((XP, lanes), F32),
            pltpu.VMEM((CP, lanes), F32),
            pltpu.VMEM((5, CP, NZ), F32),
            pltpu.VMEM((32, FH * NZ), F32),
            pltpu.VMEM((32, FH * NZ), F32),
            pltpu.VMEM((CH, 16, NZ), F32),
            pltpu.VMEM((CH, 16, NZ), F32),
            pltpu.VMEM((2, 40, NZ), F32),
            pltpu.VMEM((40, NZ), F32),
            pltpu.VMEM((40, NZ), F32),
            pltpu.VMEM((XP, 31 * NZ), F32),
            pltpu.VMEM((CP, 22 * NZ), F32),
            pltpu.VMEM((XP, YP * NZ), F32),
            pltpu.VMEM((10, 2 * CP, NZ), F32),
            pltpu.VMEM((ROWS, 2 * NZ), BF16),
            pltpu.VMEM((8, 128), F32),
            dma((10,)),
            dma((3,)),
            dma((ny,)),
            dma((ny,)),
            dma((nx,)),
            dma((nx,)),
            dma((2,)),
            dma((2,)),
            dma((8,)),
            dma((8,)),
        ],
        compiler_params=pltpu.CompilerParams(
            collective_id=0, has_side_effects=True, vmem_limit_bytes=64 << 20
        ),
        name="multilevel",
    )(
        rq.reshape(16, 128),
        rf,
        rc.reshape(16, 128),
        count,
        mq.reshape(1, MOV),
        mf,
        mc.reshape(1, MOV),
        md.reshape(1, MOV),
        ft,
        ct,
    )
    res, arr, grid = pl.pallas_call(
        hand_out,
        out_shape=(
            jax.ShapeDtypeStruct((16, 128), F32),
            jax.ShapeDtypeStruct((1, ARR), F32),
            jax.ShapeDtypeStruct((CX * CY, NZ), F32),
        ),
        in_specs=[hbm] * 3,
        out_specs=(hbm, hbm, hbm),
        scratch_shapes=[
            pltpu.VMEM((16, 128), F32),
            pltpu.VMEM((1, ARR), F32),
            pltpu.VMEM((CX * CY, NZ), F32),
            dma((6,)),
        ],
        name="hand_out",
    )(res, arr, grid)
    return res.reshape(RES), arr, grid.reshape(CX, CY, NZ)


def solution(mesh):
    both = ("gx", "gy")
    return jax.shard_map(
        on_device,
        mesh=mesh,
        in_specs=(
            P(both),
            P(None, both),
            P(both),
            P(both),
            P(both),
            P(None, both),
            P(both),
            P(both, None),
            P(),
            P(),
        ),
        out_specs=(P(both), P(both, None), P("gx", "gy", None)),
        check_vma=False,
    )
```

```python
import functools

import jax
import jax.numpy as jnp
from jax import lax
from jax.experimental import pallas as pl
from jax.experimental.pallas import tpu as pltpu
from jax.sharding import PartitionSpec as P

F32 = jnp.float32
BF16 = jnp.bfloat16
MESH = pl.DeviceIdType.MESH
CX = 32
CY = 16
NZ = 128
TAPS = 13
XP = 40
YR = 19
YP = 20
CP = 24
ROWS = YP * XP
RES = 2048
ARR = 1024
ATOMS = RES + ARR
MOV = 512
FH = 9
CH = 4


def iota(shape, dim):
    return lax.broadcasted_iota(jnp.int32, shape, dim)


def split2(v):
    hi = v.astype(BF16)
    return hi, (v - hi.astype(F32)).astype(BF16)


def split3(v):
    hi = v.astype(BF16)
    rest = v - hi.astype(F32)
    mid = rest.astype(BF16)
    return hi, mid, (rest - mid.astype(F32)).astype(BF16)


def dot_nt(a, b):
    return lax.dot_general(a, b, (((1,), (1,)), ((), ())), preferred_element_type=F32)


def dot_nn(a, b):
    return lax.dot_general(a, b, (((1,), (0,)), ((), ())), preferred_element_type=F32)


def spline(u):
    r = 1.0 - u
    s = u * u
    c = s * u
    return (
        r * r * r * (1.0 / 6.0),
        (3.0 * c - 6.0 * s + 4.0) * (1.0 / 6.0),
        (-3.0 * c + 3.0 * s + 3.0 * u + 1.0) * (1.0 / 6.0),
        c * (1.0 / 6.0),
    )


def pick(rows, at, values):
    out = jnp.zeros(rows.shape, rows.dtype)
    for k in range(4):
        out = jnp.where(rows == at[k], values[k], out)
    return out


def prepare(charge, fracs, cells, x0):
    cell = jnp.maximum(cells - 1.0, 0.0).astype(jnp.int32)
    cx = lax.shift_right_logical(cell, 11) - x0
    cy = lax.shift_right_logical(cell, 7) & 15
    cz = cell & 127
    steps = range(4)
    at_x = [cx + k for k in steps]
    at_y = [cy + k for k in steps]
    at_z = [((cz + k) & 127).astype(F32) for k in steps]
    w_x, w_y, w_z = (spline(frac) for frac in fracs)
    hi = [w.astype(BF16).astype(F32) for w in w_z]
    lo = [w - h for w, h in zip(w_z, hi)]
    return charge, at_x, w_x, at_y, w_y, at_z, hi, lo


def build_group(rows, s, lane0, a_ref, wz_ref, own):
    charge, *lists = rows
    charge = charge[s : s + 1]
    at_x, w_x, at_y, w_y, at_z, hi, lo = ([v[s : s + 1] for v in each] for each in lists)
    lanes = lane_window(lane0, 128)
    xrows = XP if own is not None else 16
    wx = pick(iota((xrows, 128), 0), at_x, w_x)
    wy = pick(iota((CP, 128), 0), at_y, w_y)
    if own is not None:
        own[0][:, lanes] = wx
        own[1][:, lanes] = wy
    z = iota((NZ, 128), 0).astype(BF16)
    at_z, hi, lo = ([v.astype(BF16) for v in each] for each in (at_z, hi, lo))
    wz_ref[0:NZ, lanes] = pick(z, at_z, hi)
    if own is not None:
        wz_ref[NZ : 2 * NZ, lanes] = pick(z, at_z, lo)
    wxq = wx * charge
    for p in range(YP // 2):
        blk = jnp.concatenate(
            [wy[2 * p : 2 * p + 1] * wxq, wy[2 * p + 1 : 2 * p + 2] * wxq], axis=0
        )
        a_ref[p * 2 * xrows : (p + 1) * 2 * xrows, lanes] = blk.astype(BF16)


def lane_window(start, size):
    if isinstance(start, int):
        return slice(start, start + size)
    return pl.ds(pl.multiple_of(start, 128), size)


def spread_chunk(lane0, size, acc_ref, a_ref, wz_ref):
    lanes = lane_window(lane0, size)
    acc_ref[...] += dot_nt(a_ref[:, lanes], wz_ref[0:NZ, lanes])


def tap_sum(t, taps_ref, dim):
    out = jnp.zeros(t.shape, F32)
    for k in range(TAPS):
        out = jnp.where(t == k, taps_ref[dim, k], out)
    return out


def kernel(
    nx,
    ny,
    rq_hbm,
    rf_hbm,
    rc_hbm,
    count_hbm,
    mq_hbm,
    mf_hbm,
    mc_hbm,
    md_hbm,
    ft_hbm,
    ct_hbm,
    res_hbm,
    arr_hbm,
    grid_hbm,
    res_ref,
    arr_ref,
    grid_ref,
    rq_ref,
    rf_ref,
    rc_ref,
    count_ref,
    mq_ref,
    mf_ref,
    mc_ref,
    md_ref,
    ft_ref,
    ct_ref,
    pay_ref,
    snd_ref,
    b1_ref,
    t2_ref,
    r2_ref,
    rt_ref,
    rb_ref,
    rl_ref,
    rr_ref,
    a_ref,
    al_ref,
    ar_ref,
    wx_ref,
    wy_ref,
    wz_ref,
    wl_ref,
    wr_ref,
    acc_ref,
    accl_ref,
    accr_ref,
    xh_ref,
    bx_ref,
    zf_ref,
    zc_ref,
    f_ref,
    co_ref,
    c3_ref,
    fl_ref,
    fr_ref,
    cl_ref,
    cr_ref,
    edge_ref,
    el_ref,
    er_ref,
    fin_ref,
    cin_ref,
    fo_ref,
    up_ref,
    hb_ref,
    ao_ref,
    in_sem,
    out_sem,
    s1_sem,
    r1_sem,
    s2_sem,
    r2_sem,
    sx_sem,
    rx_sem,
    sy_sem,
    ry_sem,
):
    gx = lax.axis_index("gx")
    gy = lax.axis_index("gy")

    barrier = pltpu.get_barrier_semaphore()
    for k in far_first(ny):
        pl.semaphore_signal(
            barrier, inc=1, device_id=(gx, lax.rem(gy + k, ny)), device_id_type=MESH
        )
    for k in far_first(nx):
        pl.semaphore_signal(
            barrier, inc=1, device_id=(lax.rem(gx + k, nx), gy), device_id_type=MESH
        )

    inputs = [
        pltpu.make_async_copy(src, dst, in_sem.at[n])
        for n, (src, dst) in enumerate(
            (
                (md_hbm, md_ref),
                (mq_hbm, mq_ref),
                (mf_hbm, mf_ref),
                (mc_hbm, mc_ref),
                (count_hbm, count_ref),
                (rq_hbm, rq_ref),
                (rf_hbm, rf_ref),
                (rc_hbm, rc_ref),
                (ft_hbm, ft_ref),
                (ct_hbm, ct_ref),
            )
        )
    ]
    for copy in inputs:
        copy.start()

    for copy in inputs[:4]:
        copy.wait()

    with jax.named_scope("pack"):
        dest = md_ref[...]
        row_of = (dest & (ny - 1)) * nx + lax.div(dest, ny)
        hot = jnp.where(iota((nx * ny, MOV), 0) == row_of, 1.0, 0.0)
        hot16 = hot.astype(BF16)
        earlier = jnp.where(iota((MOV, MOV), 0) < iota((MOV, MOV), 1), 1.0, 0.0)
        counts = dot_nn(hot16, earlier.astype(BF16))
        slot = jnp.sum(hot * counts, axis=0, keepdims=True)
        pay_ref[0:1, :] = mq_ref[...]
        pay_ref[1:4, :] = mf_ref[...]
        pay_ref[4:5, :] = mc_ref[...].astype(F32) + 1.0
        at_slot = iota((8, MOV), 0).astype(F32) == slot
        spots = jnp.concatenate(
            [jnp.where(at_slot, pay_ref[n : n + 1, :], 0.0) for n in range(5)]
            + [jnp.zeros((24, MOV), F32)],
            axis=0,
        )
        hi, mid, lo = split3(spots)
        packed = dot_nt(hot16, hi) + dot_nt(hot16, mid) + dot_nt(hot16, lo)
        snd_ref[:, 0:64] = packed
        snd_ref[:, 64:128] = jnp.zeros((nx * ny, 64), F32)

    pl.semaphore_wait(barrier, nx + ny - 2)

    def hop1(k):
        to = lax.rem(gy + k, ny)
        return pltpu.make_async_remote_copy(
            src_ref=snd_ref.at[pl.ds(pl.multiple_of(to * nx, nx), nx), :],
            dst_ref=b1_ref.at[pl.ds(pl.multiple_of(gy * nx, nx), nx), :],
            send_sem=s1_sem.at[k],
            recv_sem=r1_sem.at[k],
            device_id=(gx, to),
            device_id_type=MESH,
        )

    for k in far_first(ny):
        hop1(k).start()
    mine = pl.ds(pl.multiple_of(gy * nx, nx), nx)
    b1_ref[mine, :] = snd_ref[mine, :]

    for copy in inputs[4:]:
        copy.wait()
    rb_ref[0] = jnp.where(iota((16, 128), 0) * 128 < count_ref[0], rq_ref[...], 0.0)
    for d in range(3):
        for g in range(RES // 128):
            rb_ref[1 + d, g : g + 1, :] = rf_ref[d : d + 1, g * 128 : (g + 1) * 128]
    rb_ref[4] = rc_ref[...].astype(F32) + 1.0

    def x_copy(n, dst, to):
        return pltpu.make_async_remote_copy(
            src_ref=rb_ref,
            dst_ref=dst,
            send_sem=sx_sem.at[n],
            recv_sem=rx_sem.at[n],
            device_id=(to, gy),
            device_id_type=MESH,
        )

    x_copies = [
        x_copy(0, rl_ref, lax.rem(gx + 1, nx)),
        x_copy(1, rr_ref, lax.rem(gx + nx - 1, nx)),
    ]
    for copy in x_copies:
        copy.start()

    acc_ref[...] = jnp.zeros_like(acc_ref)
    accl_ref[...] = jnp.zeros_like(accl_ref)
    accr_ref[...] = jnp.zeros_like(accr_ref)

    def residents(block, x0, acc, a, wz, own):
        for half in range(2):
            rows = slice(half * 8, half * 8 + 8)
            ready = prepare(
                block[0, rows, :], [block[1 + d, rows, :] for d in range(3)], block[4, rows, :], x0
            )
            for s in range(8):
                build_group(ready, s, half * 1024 + s * 128, a, wz, own)
            spread_chunk(half * 1024, 1024, acc, a, wz)

    residents(rb_ref, 0, acc_ref, a_ref, wz_ref, (wx_ref, wy_ref))

    for k in range(1, ny):
        hop1(k).wait()
    for g in range(nx):
        t2_ref[g + 1] = b1_ref[pl.ds(g, ny, stride=nx), :]
    t2_ref[0] = t2_ref[nx]
    t2_ref[nx + 1] = t2_ref[1]

    def hop2(k):
        to = lax.rem(gx + k, nx)
        return pltpu.make_async_remote_copy(
            src_ref=t2_ref.at[pl.ds(to, 3)],
            dst_ref=r2_ref.at[gx],
            send_sem=s2_sem.at[k],
            recv_sem=r2_sem.at[k],
            device_id=(to, gy),
            device_id_type=MESH,
        )

    for k in far_first(nx):
        hop2(k).start()
    r2_ref[gx] = t2_ref[pl.ds(gx, 3)]

    for copy in x_copies:
        copy.wait()

    residents(rl_ref, 20, accl_ref, al_ref, wl_ref, None)
    residents(rr_ref, 0, accr_ref, ar_ref, wr_ref, None)

    with jax.named_scope("matrices"):
        col = iota((64, 256), 1)
        part = jnp.where(col >= 160, 2, jnp.where(col >= 80, 1, 0))
        base = col - part * 80
        pos = jnp.where(base < 48, base, jnp.where(base < 64, base - 60, base - 32))
        out_x = iota((64, 256), 0)
        fine_t = pos - out_x + 6
        coarse_t = lax.shift_right_arithmetic(pos, 1) - (out_x - XP) + 6
        bx = jnp.where(out_x < XP, tap_sum(fine_t, ft_ref, 0), tap_sum(coarse_t, ct_ref, 0))
        bx_hi = bx.astype(BF16).astype(F32)
        bx = jnp.where(part == 2, bx - bx_hi, bx_hi)
        bx_ref[...] = jnp.where(col < 240, bx, 0.0).astype(BF16)
        t = (iota((NZ, NZ), 0) - iota((NZ, NZ), 1) + 6) & 127
        hi, lo = split2(tap_sum(t, ft_ref, 2))
        zf_ref[0:NZ, 0:NZ] = hi
        zf_ref[NZ : 2 * NZ, 0:NZ] = hi
        zf_ref[0:NZ, NZ : 2 * NZ] = lo
        zf_ref[NZ : 2 * NZ, NZ : 2 * NZ] = jnp.zeros((NZ, NZ), BF16)
        r, c = iota((NZ, 2 * NZ), 0), iota((NZ, 2 * NZ), 1)
        t = ((r & 63) - lax.shift_right_logical(c & 127, 1) + 6) & 63
        zc = tap_sum(t, ct_ref, 2)
        same = lax.shift_right_logical(r, 6) == lax.shift_right_logical(c, 7)
        hi, lo = split2(jnp.where(same, zc, 0.0))
        zc_ref[0:NZ, :] = hi
        zc_ref[NZ : 2 * NZ, :] = hi
        zc_ref[2 * NZ : 3 * NZ, :] = lo

    for k in range(1, nx):
        hop2(k).wait()

    for n in range(3):
        rt_ref[n] = r2_ref[:, n].reshape(nx * ny, 128).T

    boxes = (
        (1, 0, acc_ref, a_ref, wz_ref, (wx_ref, wy_ref)),
        (0, 20, accl_ref, al_ref, wl_ref, None),
        (2, 0, accr_ref, ar_ref, wr_ref, None),
    )
    for n in range(len(boxes) + 1):
        if n < len(boxes):
            side, x0, _, a, wz, own = boxes[n]
            field = [rt_ref[side, f * 8 : f * 8 + 8, :] for f in range(5)]
            ready = prepare(field[0], field[1:4], field[4], x0)
        if n > 0:
            spread_chunk(RES, ARR, *boxes[n - 1][2:5])
        if n < len(boxes):
            for s in range(8):
                build_group(ready, s, RES + s * 128, a, wz, own)

    up_y = lax.rem(gy + 1, ny)
    down_y = lax.rem(gy + ny - 1, ny)
    def x_pass(y0, y1):
        for y in range(y0, y1):
            lanes = slice(y * NZ, (y + 1) * NZ)
            rows = []
            for ref, count in ((acc_ref, XP), (accl_ref, 16), (accr_ref, 16)):
                rows.append(ref[y * count : (y + 1) * count])
                if count == XP:
                    rows.append(jnp.zeros((8, NZ), F32))
            hi, lo = split2(jnp.concatenate(rows, axis=0))
            xh_ref[0:80, lanes] = hi
            xh_ref[80:160, lanes] = lo
            xh_ref[160:240, lanes] = hi
            xh_ref[240:256, lanes] = jnp.zeros((16, NZ), BF16)
        lanes = slice(y0 * NZ, y1 * NZ)
        conv = dot_nn(bx_ref[...], xh_ref[:, lanes])
        f_ref[:, lanes] = conv[0:XP]
        co_ref[:, lanes] = conv[XP : XP + CP]

    def y_copy(n, src, dst, to):
        return pltpu.make_async_remote_copy(
            src_ref=src,
            dst_ref=dst,
            send_sem=sy_sem.at[n],
            recv_sem=ry_sem.at[n],
            device_id=(gx, to),
            device_id_type=MESH,
        )

    def fine_copy(n, y0, first, count, dst, to):
        return y_copy(
            n,
            f_ref.at[pl.ds(0, 32), pl.ds((y0 + first) * NZ, count * NZ)],
            dst.at[:, pl.ds(first * NZ, count * NZ)],
            to,
        )

    fine_copies = [
        fine_copy(4, 10, 0, 5, fl_ref, up_y),
        fine_copy(5, 0, 0, 5, fr_ref, down_y),
        fine_copy(6, 10, 5, 4, fl_ref, up_y),
        fine_copy(7, 0, 5, 4, fr_ref, down_y),
    ]
    x_pass(10, 15)
    fine_copies[0].start()
    x_pass(0, 5)
    fine_copies[1].start()
    x_pass(15, 19)
    x_pass(5, 10)

    r, c = iota((2 * NZ, NZ), 0), iota((2 * NZ, NZ), 1)
    pair = jnp.where(lax.shift_right_logical(r, 1) == c, 1.0, 0.0).astype(BF16)
    coarse = co_ref[...]
    tiles = []
    for m in range(5):
        both = []
        for j in (2 * m, 2 * m + 1):
            row = coarse[:, 2 * j * NZ : (2 * j + 1) * NZ]
            if 2 * j + 1 < YR:
                row = row + coarse[:, (2 * j + 1) * NZ : (2 * j + 2) * NZ]
            both.append(row)
        tiles.append(jnp.concatenate(both, axis=1))
    packed = jnp.concatenate(tiles, axis=0)
    hi, lo = split2(packed)
    packed = dot_nn(hi, pair) + dot_nn(lo, pair)
    for m in range(5):
        c3_ref[m] = packed[m * CP : (m + 1) * CP]

    for n, (y0, m0) in enumerate(((10, 1), (0, 0))):
        for y in range(FH):
            edge_ref[n, 3 * y : 3 * y + 3, :] = f_ref[32:35, (y0 + y) * NZ : (y0 + y + 1) * NZ]
        edge_ref[n, 27:32, :] = jnp.zeros((5, NZ), F32)
        for m in range(CH):
            edge_ref[n, 32 + 2 * m : 34 + 2 * m, :] = c3_ref[m0 + m, 16:18, :]
    half = pl.ds(0, 16)
    y_copies = [
        y_copy(0, edge_ref.at[0], el_ref, up_y),
        y_copy(1, edge_ref.at[1], er_ref, down_y),
        y_copy(2, c3_ref.at[pl.ds(1, CH), half], cl_ref, up_y),
        y_copy(3, c3_ref.at[pl.ds(0, CH), half], cr_ref, down_y),
    ]
    for copy in y_copies + fine_copies[2:4]:
        copy.start()

    def fine_z(block):
        hi, lo = split2(block)
        both = dot_nn(jnp.concatenate([hi, lo], axis=1), zf_ref[...])
        return both[:, 0:NZ] + both[:, NZ : 2 * NZ]

    def coarse_z(block):
        hi, lo = split2(block)
        return dot_nn(jnp.concatenate([hi, lo], axis=1), zc_ref[0 : 2 * NZ, :]) + dot_nn(
            hi, zc_ref[2 * NZ : 3 * NZ, :]
        )

    def stacked(ref, count):
        return jnp.concatenate([ref[:, y * NZ : (y + 1) * NZ] for y in range(count)], axis=0)

    own = fine_z(stacked(f_ref, YR))
    for y in range(YR):
        fin_ref[:, (y + 6) * NZ : (y + 7) * NZ] = own[y * XP : (y + 1) * XP]
    zero = jnp.zeros((XP, 6 * NZ), F32)
    fin_ref[:, 0 : 6 * NZ] = zero
    fin_ref[:, 25 * NZ : 31 * NZ] = zero
    own = coarse_z(jnp.concatenate([c3_ref[m] for m in range(5)], axis=0))
    zero = jnp.zeros((CP, 6 * NZ), F32)
    cin_ref[:, 0 : 6 * NZ] = zero
    cin_ref[:, 16 * NZ : 22 * NZ] = zero
    for m in range(5):
        cin_ref[:, (2 * m + 6) * NZ : (2 * m + 8) * NZ] = own[m * CP : (m + 1) * CP]

    for copy in y_copies:
        copy.wait()
    for ref, edge, at in ((cl_ref, el_ref, 0), (cr_ref, er_ref, 14)):
        halo = coarse_z(jnp.concatenate([ref[m] for m in range(CH)] + [edge[32:40, :]], axis=0))
        for m in range(CH):
            lanes = slice((2 * m + at) * NZ, (2 * m + at + 2) * NZ)
            cin_ref[0:16, lanes] += halo[m * 16 : (m + 1) * 16]
            cin_ref[16:18, lanes] += halo[64 + 2 * m : 66 + 2 * m]

    def coarse_y(i, carry):
        rows = pl.ds(pl.multiple_of(i * 8, 8), 8)
        out = jnp.zeros((8, 10 * NZ), F32)
        for k in range(TAPS):
            out = out + ct_ref[1, k] * cin_ref[rows, k * NZ : (k + 10) * NZ]
        for j in range(10):
            one = out[:, j * NZ : (j + 1) * NZ]
            up_ref[j, pl.ds(i * 16, 8, stride=2), :] = one
            up_ref[j, pl.ds(i * 16 + 1, 8, stride=2), :] = one
        return carry

    lax.fori_loop(0, CP // 8, coarse_y, 0)

    for copy in fine_copies:
        copy.wait()
    for ref, edge, at in ((fl_ref, el_ref, 0), (fr_ref, er_ref, 22)):
        halo = fine_z(jnp.concatenate([stacked(ref, FH), edge[0:32, :]], axis=0))
        for y in range(FH):
            lanes = slice((y + at) * NZ, (y + at + 1) * NZ)
            fin_ref[0:32, lanes] += halo[y * 32 : (y + 1) * 32]
            fin_ref[32:35, lanes] += halo[288 + 3 * y : 291 + 3 * y]

    def fine_y(i, carry):
        rows = pl.ds(pl.multiple_of(i * 8, 8), 8)
        out = jnp.zeros((8, YR * NZ), F32)
        for k in range(TAPS):
            out = out + ft_ref[1, k] * fin_ref[rows, k * NZ : (k + YR) * NZ]
        for y in range(YR):
            fo_ref[rows, y * NZ : (y + 1) * NZ] = (
                out[:, y * NZ : (y + 1) * NZ] + up_ref[y // 2, rows, :]
            )
        fo_ref[rows, YR * NZ : YP * NZ] = jnp.zeros((8, NZ), F32)
        return carry

    lax.fori_loop(0, XP // 8, fine_y, 0)

    for p in range(YP // 2):
        half = jnp.concatenate(
            [fo_ref[:, y * NZ : (y + 1) * NZ] for y in (2 * p, 2 * p + 1)], axis=0
        ).astype(BF16)
        hb_ref[p * 2 * XP : (p + 1) * 2 * XP, 0:NZ] = half
        hb_ref[p * 2 * XP : (p + 1) * 2 * XP, NZ : 2 * NZ] = half

    outputs = [
        pltpu.make_async_copy(grid_ref, grid_hbm, out_sem.at[0]),
        pltpu.make_async_copy(res_ref, res_hbm, out_sem.at[1]),
        pltpu.make_async_copy(arr_ref, arr_hbm, out_sem.at[2]),
    ]

    def values_of(c):
        return dot_nn(hb_ref[...], wz_ref[:, c * 256 : (c + 1) * 256])

    def reduced(c, values):
        lanes = slice(c * 256, (c + 1) * 256)
        wy = wy_ref[:, lanes]
        part = jnp.zeros((XP, 256), F32)
        for y in range(YR):
            part = part + wy[y : y + 1] * values[y * XP : (y + 1) * XP]
        value = jnp.sum(part * wx_ref[:, lanes], axis=0, keepdims=True)
        if c < RES // 256:
            live = iota((1, 256), 1) + c * 256 < count_ref[0]
            value = jnp.where(live, value, 0.0)
            at, ref = 2 * c, res_ref
        else:
            at, ref = 2 * (c - RES // 256), ao_ref
        ref[at : at + 1, :] = value[:, 0:128]
        ref[at + 1 : at + 2, :] = value[:, 128:256]

    for c in range(RES // 256, ATOMS // 256):
        reduced(c, values_of(c))
    for y in range(CY):
        for i in range(CX // 8):
            grid_ref[pl.ds(y + i * 8 * CY, 8, stride=CY), :] = fo_ref[
                i * 8 : i * 8 + 8, y * NZ : (y + 1) * NZ
            ]
    outputs[0].start()

    occupied = rt_ref[1, 32:40, :]
    value = jnp.where(occupied > 0.5, ao_ref[...], 0.0)
    hi, mid, lo = split3(value)
    wide = (NZ, ARR)
    spread_to = jnp.where(lax.shift_right_logical(iota(wide, 1), 3) == iota(wide, 0), 1.0, 0.0)
    spread_to = spread_to.astype(BF16)
    flat = dot_nn(hi, spread_to) + dot_nn(mid, spread_to) + dot_nn(lo, spread_to)
    keep = (iota((8, ARR), 1) & 7) == iota((8, ARR), 0)
    arr_ref[...] = jnp.sum(jnp.where(keep, flat, 0.0), axis=0, keepdims=True)
    outputs[2].start()

    for c in range(RES // 256):
        reduced(c, values_of(c))
    outputs[1].start()
    for copy in outputs:
        copy.wait()


def far_first(count):
    turn = count // 2
    return sorted(range(1, count), key=lambda k: (-min(k % turn, turn - k % turn), -k))


def hand_out(*refs):
    given, out, held, sems = refs[0:3], refs[3:6], refs[6:9], refs[9]
    reads = [pltpu.make_async_copy(given[n], held[n], sems.at[n]) for n in range(3)]
    writes = [pltpu.make_async_copy(held[n], out[n], sems.at[n + 3]) for n in range(3)]
    for copy in reads:
        copy.start()
    for read, write in zip(reads, writes):
        read.wait()
        write.start()
    for copy in writes:
        copy.wait()


def on_device(rq, rf, rc, count, mq, mf, mc, md, ft, ct):
    nx = lax.axis_size("gx")
    ny = lax.axis_size("gy")
    hbm = pl.BlockSpec(memory_space=pltpu.HBM)
    lanes = YR * NZ
    near = YP * 16
    dma = pltpu.SemaphoreType.DMA
    res, arr, grid = pl.pallas_call(
        functools.partial(kernel, nx, ny),
        out_shape=(
            jax.ShapeDtypeStruct((16, 128), F32),
            jax.ShapeDtypeStruct((1, ARR), F32),
            jax.ShapeDtypeStruct((CX * CY, NZ), F32),
        ),
        in_specs=[hbm] * 10,
        out_specs=(hbm, hbm, hbm),
        scratch_shapes=[
            pltpu.VMEM((16, 128), F32),
            pltpu.VMEM((1, ARR), F32),
            pltpu.VMEM((CX * CY, NZ), F32),
            pltpu.VMEM((16, 128), F32),
            pltpu.VMEM((3, RES), F32),
            pltpu.VMEM((16, 128), jnp.int32),
            pltpu.SMEM((1,), jnp.int32),
            pltpu.VMEM((1, MOV), F32),
            pltpu.VMEM((3, MOV), F32),
            pltpu.VMEM((1, MOV), jnp.int32),
            pltpu.VMEM((1, MOV), jnp.int32),
            pltpu.SMEM((3, TAPS), F32),
            pltpu.SMEM((3, TAPS), F32),
            pltpu.VMEM((8, MOV), F32),
            pltpu.VMEM((128, 128), F32),
            pltpu.VMEM((128, 128), F32),
            pltpu.VMEM((nx + 2, ny, 128), F32),
            pltpu.VMEM((nx, 3, ny, 128), F32),
            pltpu.VMEM((3, 128, 128), F32),
            pltpu.VMEM((5, 16, 128), F32),
            pltpu.VMEM((5, 16, 128), F32),
            pltpu.VMEM((5, 16, 128), F32),
            pltpu.VMEM((ROWS, ATOMS), BF16),
            pltpu.VMEM((near, ATOMS), BF16),
            pltpu.VMEM((near, ATOMS), BF16),
            pltpu.VMEM((XP, ATOMS), F32),
            pltpu.VMEM((CP, ATOMS), F32),
            pltpu.VMEM((2 * NZ, ATOMS), BF16),
            pltpu.VMEM((NZ, ATOMS), BF16),
            pltpu.VMEM((NZ, ATOMS), BF16),
            pltpu.VMEM((ROWS, NZ), F32),
            pltpu.VMEM((near, NZ), F32),
            pltpu.VMEM((near, NZ), F32),
            pltpu.VMEM((256, lanes), BF16),
            pltpu.VMEM((64, 256), BF16),
            pltpu.VMEM((2 * NZ, 2 * NZ), BF16),
            pltpu.VMEM((3 * NZ, 2 * NZ), BF16),
            pltpu.VMEM((XP, lanes), F32),
            pltpu.VMEM((CP, lanes), F32),
            pltpu.VMEM((5, CP, NZ), F32),
            pltpu.VMEM((32, FH * NZ), F32),
            pltpu.VMEM((32, FH * NZ), F32),
            pltpu.VMEM((CH, 16, NZ), F32),
            pltpu.VMEM((CH, 16, NZ), F32),
            pltpu.VMEM((2, 40, NZ), F32),
            pltpu.VMEM((40, NZ), F32),
            pltpu.VMEM((40, NZ), F32),
            pltpu.VMEM((XP, 31 * NZ), F32),
            pltpu.VMEM((CP, 22 * NZ), F32),
            pltpu.VMEM((XP, YP * NZ), F32),
            pltpu.VMEM((10, 2 * CP, NZ), F32),
            pltpu.VMEM((ROWS, 2 * NZ), BF16),
            pltpu.VMEM((8, 128), F32),
            dma((10,)),
            dma((3,)),
            dma((ny,)),
            dma((ny,)),
            dma((nx,)),
            dma((nx,)),
            dma((2,)),
            dma((2,)),
            dma((8,)),
            dma((8,)),
        ],
        compiler_params=pltpu.CompilerParams(
            collective_id=0, has_side_effects=True, vmem_limit_bytes=64 << 20
        ),
        name="multilevel",
    )(
        rq.reshape(16, 128),
        rf,
        rc.reshape(16, 128),
        count,
        mq.reshape(1, MOV),
        mf,
        mc.reshape(1, MOV),
        md.reshape(1, MOV),
        ft,
        ct,
    )
    res, arr, grid = pl.pallas_call(
        hand_out,
        out_shape=(
            jax.ShapeDtypeStruct((16, 128), F32),
            jax.ShapeDtypeStruct((1, ARR), F32),
            jax.ShapeDtypeStruct((CX * CY, NZ), F32),
        ),
        in_specs=[hbm] * 3,
        out_specs=(hbm, hbm, hbm),
        scratch_shapes=[
            pltpu.VMEM((16, 128), F32),
            pltpu.VMEM((1, ARR), F32),
            pltpu.VMEM((CX * CY, NZ), F32),
            dma((6,)),
        ],
        name="hand_out",
    )(res, arr, grid)
    return res.reshape(RES), arr, grid.reshape(CX, CY, NZ)


def solution(mesh):
    both = ("gx", "gy")
    return jax.shard_map(
        on_device,
        mesh=mesh,
        in_specs=(
            P(both),
            P(None, both),
            P(both),
            P(both),
            P(both),
            P(None, both),
            P(both),
            P(both, None),
            P(),
            P(),
        ),
        out_specs=(P(both), P(both, None), P("gx", "gy", None)),
        check_vma=False,
    )
```
